512 devices in a mesh: blocks: 128 (over x, y, z_hi, core), phi: 4 (over z_lo).
Axes of the slice: x: 4, y: 8, z: 8 (z_hi: 2, z_lo: 4; z = z_hi * 4 + z_lo), core: 2. Of those that a mesh axis runs over, the one named last changes fastest.
Arguments:
- field: float32 [3, 2048, 64, 512], P(None, 'blocks', 'phi'), may hold values from -6 to 6
- velocity: float32 [3, 2048, 64, 512], P(None, 'blocks', 'phi'), may hold values from -6 to 6
- strip_shift: int32 [2048], P('blocks'), may hold values from 0 to 6, as said below
- strip_frac: float32 [2048], P('blocks'), may hold values from 0 to 1
- edge_shift: int32 [2], replicated, may hold values from 0 to 6, as said below
- edge_frac: float32 [2], replicated, may hold values from 0 to 1
Outputs:
- advected: float32 [3, 2048, 64, 512], P(None, 'blocks', 'phi')
The draws below stay inside these ranges and needn't reach their ends.
Inputs may be any that keep to these rules, and one draw needn't show every extreme that they name: `strip_shift`: some strip has a shift of exactly 6 and some strip a shift of 0. `edge_shift`: exactly one of the two boundary offsets equals 6; the other is smaller.
All inputs are finite; a program needn't handle non-finite values.
Results may differ from the reference program's by a relative error of at most 0.00002.
Values sent between devices are 32-bit elements; how exact they have to be, the bound alone decides.
No kernel may reach another device: no remote copies, remote signals or barrier semaphores. Data moves between devices by JAX's collectives and lax.ppermute only.
A program may use at most 128 MiB of HBM per device.

```python
import jax
import jax.numpy as jnp

NZ = 512
KMAX = 6
NX = 2048
NY = 64


def draw_strip_shift(key, part):
    source_key, spot_key = jax.random.split(jax.random.fold_in(key, 11))
    values = jax.random.randint(source_key, (NX,), 0, KMAX + 1, dtype=jnp.int32)
    spot = jax.random.randint(spot_key, (), 0, NX, dtype=jnp.int32)
    other = (spot + 1) % NX
    places = jnp.arange(NX, dtype=jnp.int32)
    values = jnp.where(places == other, 0, values)
    return jnp.where(places == spot, KMAX, values).astype(jnp.int32)


def draw_edge_shift(key, part):
    source_key, spot_key = jax.random.split(jax.random.fold_in(key, 23))
    values = jax.random.randint(source_key, (2,), 0, KMAX, dtype=jnp.int32)
    spot = jax.random.randint(spot_key, (), 0, 2, dtype=jnp.int32)
    return jnp.where(jnp.arange(2, dtype=jnp.int32) == spot, KMAX, values).astype(jnp.int32)


def block_scale(own_key, shape, pieces, smallest, top_value):
    def one(position, blocks):
        heights = jax.random.uniform(jax.random.fold_in(jax.random.fold_in(own_key, 6), position), (blocks,), jnp.float32, smallest / len(pieces), top_value / len(pieces))
        return jnp.repeat(jnp.exp(heights), shape[position] // blocks).reshape((-1,) + (1,) * (len(shape) - position - 1))

    factor_of = one(*pieces[0])
    for cut in pieces[1:]:
        factor_of = factor_of * one(*cut)
    return factor_of


def centred(stream_key, shape, width, bound, shards=(), kind=jnp.bfloat16):
    factor_of = block_scale(stream_key, shape, shards, -0.22, 0.18) if shards else 1.0
    drawn = jax.random.normal(stream_key, shape, jnp.float32) * width * factor_of
    return jnp.minimum(jnp.maximum(drawn, -bound), bound).astype(kind)


def setup_inputs(seed: int = 0) -> dict:
    streams_of = jax.random.split(jax.random.key(seed), 7)
    return {
        "field": centred(streams_of[0], (3, NX, NY, NZ), 1.0, 6.0, ((1, 128), (2, 4)), jnp.float32),
        "velocity": centred(streams_of[1], (3, NX, NY, NZ), 1.0, 6.0, ((1, 128), (2, 4)), jnp.float32),
        "strip_shift": draw_strip_shift(jax.random.fold_in(streams_of[6], 71), 0),
        "strip_frac": jnp.clip(1.0 * jax.random.uniform(streams_of[3], (NX,), jnp.float32) ** block_scale(streams_of[3], (NX,), ((0, 128),), -0.2, 0.2), 0.0, 1.0),
        "edge_shift": draw_edge_shift(jax.random.fold_in(streams_of[6], 71), 0),
        "edge_frac": jnp.clip(jax.random.uniform(streams_of[5], (2,), jnp.float32, 0.0, 1.0), 0.0, 1.0),
    }


COURANT = 0.4


def below(values):
    return jnp.roll(values, 1, axis=-1)


def above(values):
    return jnp.roll(values, -1, axis=-1)


def ct_update(padded):
    field_x, field_y, field_z = padded[0], padded[1], padded[2]
    flow_x, flow_y, flow_z = padded[3], padded[4], padded[5]
    zedge_fx = 0.5 * (field_x[1:, 1:] + field_x[1:, :-1])
    zedge_fy = 0.5 * (field_y[1:, 1:] + field_y[:-1, 1:])
    zedge_vx = 0.25 * (flow_x[1:, 1:] + flow_x[:-1, 1:] + flow_x[1:, :-1] + flow_x[:-1, :-1])
    zedge_vy = 0.25 * (flow_y[1:, 1:] + flow_y[:-1, 1:] + flow_y[1:, :-1] + flow_y[:-1, :-1])
    emf_z = zedge_vy * zedge_fx - zedge_vx * zedge_fy
    middle_fx = field_x[:, 1:-1]
    middle_fz = field_z[:, 1:-1]
    middle_vx = flow_x[:, 1:-1]
    middle_vz = flow_z[:, 1:-1]
    yedge_fx = 0.5 * (middle_fx[1:] + below(middle_fx[1:]))
    yedge_fz = 0.5 * (middle_fz[1:] + middle_fz[:-1])
    paired_vx = middle_vx[1:] + middle_vx[:-1]
    paired_vz = middle_vz[1:] + middle_vz[:-1]
    yedge_vx = 0.25 * (paired_vx + below(paired_vx))
    yedge_vz = 0.25 * (paired_vz + below(paired_vz))
    emf_y = yedge_vx * yedge_fz - yedge_vz * yedge_fx
    radial_fy = field_y[1:-1]
    radial_fz = field_z[1:-1]
    radial_vy = flow_y[1:-1]
    radial_vz = flow_z[1:-1]
    xedge_fy = 0.5 * (radial_fy[:, 1:] + below(radial_fy[:, 1:]))
    xedge_fz = 0.5 * (radial_fz[:, 1:] + radial_fz[:, :-1])
    couple_vy = radial_vy[:, 1:] + radial_vy[:, :-1]
    couple_vz = radial_vz[:, 1:] + radial_vz[:, :-1]
    xedge_vy = 0.25 * (couple_vy + below(couple_vy))
    xedge_vz = 0.25 * (couple_vz + below(couple_vz))
    emf_x = xedge_vz * xedge_fy - xedge_vy * xedge_fz
    radial_count = emf_x.shape[0]
    azimuth_count = emf_y.shape[1]
    new_x = field_x[1:-1, 1:-1] - COURANT * ((emf_z[:radial_count, 1:] - emf_z[:radial_count, :azimuth_count]) - (above(emf_y[:radial_count]) - emf_y[:radial_count]))
    new_y = field_y[1:-1, 1:-1] - COURANT * ((above(emf_x[:, :azimuth_count]) - emf_x[:, :azimuth_count]) - (emf_z[1:, :azimuth_count] - emf_z[:radial_count, :azimuth_count]))
    new_z = field_z[1:-1, 1:-1] - COURANT * ((emf_y[1:] - emf_y[:radial_count]) - (emf_x[:, 1:] - emf_x[:, :azimuth_count]))
    return jnp.stack([new_x, new_y, new_z])


def lower_remap(rows, shift, weight):
    return (1.0 - weight) * jnp.roll(rows, shift, axis=1) + weight * jnp.roll(rows, shift + 1, axis=1)


def upper_remap(rows, shift, weight):
    return (1.0 - weight) * jnp.roll(rows, -shift, axis=1) + weight * jnp.roll(rows, -shift - 1, axis=1)


def reference(field, velocity, strip_shift, strip_frac, edge_shift, edge_frac):
    stacked = jnp.concatenate([field, velocity], axis=0)
    inner_ghost = lower_remap(stacked[:, -1], edge_shift[0], edge_frac[0])
    outer_ghost = upper_remap(stacked[:, 0], edge_shift[1], edge_frac[1])
    widened = jnp.concatenate([inner_ghost[:, None], stacked, outer_ghost[:, None]], axis=1)
    padded = jnp.concatenate([widened[:, :, -1:], widened, widened[:, :, :1]], axis=2)
    updated = ct_update(padded)

    def one_strip(rows, shift, weight):
        return lower_remap(rows, shift, weight)

    return jax.vmap(one_strip, in_axes=(1, 0, 0), out_axes=1)(updated, strip_shift, strip_frac)
```

```python
import jax
import jax.numpy as jnp
from jax import lax
from jax.experimental import pallas as pl
from jax.experimental.pallas import tpu as pltpu
from jax.sharding import PartitionSpec as P

KMAX = 6
COURANT = 0.4
WIDE = KMAX + 2


def shifted(x, db, dp):
    nb, nq = lax.axis_size("blocks"), lax.axis_size("phi")
    if dp == 0:
        return lax.ppermute(x, "blocks", [(b, (b + db) % nb) for b in range(nb)])
    if db == 0:
        return lax.ppermute(x, "phi", [(q, (q + dp) % nq) for q in range(nq)])
    pairs = [
        (b * nq + q, ((b + db) % nb) * nq + (q + dp) % nq)
        for b in range(nb)
        for q in range(nq)
    ]
    return lax.ppermute(x, ("blocks", "phi"), pairs)


def below(v):
    return pltpu.roll(v, 1, 1)


def above(v):
    return pltpu.roll(v, v.shape[1] - 1, 1)


def ct_kernel(p_ref, u_ref, ez_s, ey_s, ex_s):
    rows = u_ref.shape[1]
    ny = u_ref.shape[2]

    def emf_row(a, carry):
        fx_a = p_ref[0, a, pl.ds(1, ny + 1), :]
        fx_ab = p_ref[0, a, pl.ds(0, ny + 1), :]
        fy_a = p_ref[1, a, pl.ds(1, ny + 1), :]
        fy_m = p_ref[1, a - 1, pl.ds(1, ny + 1), :]
        vx = (
            p_ref[3, a, pl.ds(1, ny + 1), :]
            + p_ref[3, a - 1, pl.ds(1, ny + 1), :]
            + p_ref[3, a, pl.ds(0, ny + 1), :]
            + p_ref[3, a - 1, pl.ds(0, ny + 1), :]
        )
        vy = (
            p_ref[4, a, pl.ds(1, ny + 1), :]
            + p_ref[4, a - 1, pl.ds(1, ny + 1), :]
            + p_ref[4, a, pl.ds(0, ny + 1), :]
            + p_ref[4, a - 1, pl.ds(0, ny + 1), :]
        )
        ez = (0.25 * vy) * (0.5 * (fx_a + fx_ab)) - (0.25 * vx) * (0.5 * (fy_a + fy_m))
        ez_s[a - 1, pl.ds(0, ny + 1), :] = ez

        mfx = p_ref[0, a, pl.ds(1, ny), :]
        mfz = p_ref[2, a, pl.ds(1, ny), :]
        mfz_m = p_ref[2, a - 1, pl.ds(1, ny), :]
        pvx = p_ref[3, a, pl.ds(1, ny), :] + p_ref[3, a - 1, pl.ds(1, ny), :]
        pvz = p_ref[5, a, pl.ds(1, ny), :] + p_ref[5, a - 1, pl.ds(1, ny), :]
        yfx = 0.5 * (mfx + below(mfx))
        yfz = 0.5 * (mfz + mfz_m)
        yvx = 0.25 * (pvx + below(pvx))
        yvz = 0.25 * (pvz + below(pvz))
        ey_s[a - 1] = yvx * yfz - yvz * yfx

        rfy = p_ref[1, a, pl.ds(1, ny + 1), :]
        rfz = p_ref[2, a, pl.ds(1, ny + 1), :]
        rfz_b = p_ref[2, a, pl.ds(0, ny + 1), :]
        cvy = p_ref[4, a, pl.ds(1, ny + 1), :] + p_ref[4, a, pl.ds(0, ny + 1), :]
        cvz = p_ref[5, a, pl.ds(1, ny + 1), :] + p_ref[5, a, pl.ds(0, ny + 1), :]
        xfy = 0.5 * (rfy + below(rfy))
        xfz = 0.5 * (rfz + rfz_b)
        xvy = 0.25 * (cvy + below(cvy))
        xvz = 0.25 * (cvz + below(cvz))
        ex_s[a - 1, pl.ds(0, ny + 1), :] = xvz * xfy - xvy * xfz
        return carry

    lax.fori_loop(1, rows + 2, emf_row, 0)

    def update_row(r, carry):
        a = r + 1
        ez_r = ez_s[r, pl.ds(0, ny), :]
        ez_r1 = ez_s[r, pl.ds(1, ny), :]
        ez_n = ez_s[r + 1, pl.ds(0, ny), :]
        ey_r = ey_s[r]
        ey_n = ey_s[r + 1]
        ex_r = ex_s[r, pl.ds(0, ny), :]
        ex_r1 = ex_s[r, pl.ds(1, ny), :]
        fx = p_ref[0, a, pl.ds(1, ny), :]
        fy = p_ref[1, a, pl.ds(1, ny), :]
        fz = p_ref[2, a, pl.ds(1, ny), :]
        u_ref[0, r] = fx - COURANT * ((ez_r1 - ez_r) - (above(ey_r) - ey_r))
        u_ref[1, r] = fy - COURANT * ((above(ex_r) - ex_r) - (ez_n - ez_r))
        u_ref[2, r] = fz - COURANT * ((ey_n - ey_r) - (ex_r1 - ex_r))
        return carry

    lax.fori_loop(0, rows, update_row, 0)


def ct_update(padded):
    _, px, py, nz = padded.shape
    rows, ny = px - 2, py - 2
    vmem = pl.BlockSpec(memory_space=pltpu.VMEM)
    return pl.pallas_call(
        ct_kernel,
        out_shape=jax.ShapeDtypeStruct((3, rows, ny, nz), padded.dtype),
        in_specs=[vmem],
        out_specs=vmem,
        scratch_shapes=[
            pltpu.VMEM((rows + 1, ny + 8, nz), jnp.float32),
            pltpu.VMEM((rows + 1, ny, nz), jnp.float32),
            pltpu.VMEM((rows + 1, ny + 8, nz), jnp.float32),
        ],
        cost_estimate=pl.CostEstimate(
            flops=120 * rows * ny * nz, transcendentals=0,
            bytes_accessed=4 * (6 * px * py + 3 * rows * ny) * nz,
        ),
    )(padded)


def advect_kernel(shift_ref, frac_ref, u_ref, rec_ref, o_ref, ext):
    rows, ny = u_ref.shape[1], u_ref.shape[2]
    lead = 8
    ext[:, :, pl.ds(lead - KMAX - 1, KMAX + 1), :] = rec_ref[...]
    ext[:, :, pl.ds(lead, ny), :] = u_ref[...]

    def strip(x, carry):
        s = shift_ref[x]
        w = frac_ref[x]
        for k in range(KMAX + 1):
            @pl.when(s == k)
            def _():
                near = ext[:, x, pl.ds(lead - k, ny), :]
                far = ext[:, x, pl.ds(lead - k - 1, ny), :]
                o_ref[:, x] = (1.0 - w) * near + w * far
        return carry

    lax.fori_loop(0, rows, strip, 0)


def advect(updated, received, strip_shift, strip_frac):
    _, rows, ny, nz = updated.shape
    vmem = pl.BlockSpec(memory_space=pltpu.VMEM)
    smem = pl.BlockSpec(memory_space=pltpu.SMEM)
    return pl.pallas_call(
        advect_kernel,
        out_shape=jax.ShapeDtypeStruct(updated.shape, updated.dtype),
        in_specs=[smem, smem, vmem, vmem],
        out_specs=vmem,
        scratch_shapes=[pltpu.VMEM((3, rows, ny + 8, nz), jnp.float32)],
        cost_estimate=pl.CostEstimate(
            flops=3 * 3 * rows * ny * nz, transcendentals=0,
            bytes_accessed=4 * 3 * rows * (2 * ny + KMAX + 1) * nz,
        ),
    )(strip_shift, strip_frac, updated, received)


def body(field, velocity, strip_shift, strip_frac, edge_shift, edge_frac):
    stacked = jnp.concatenate([field, velocity], axis=0)
    _, nx, ny, nz = stacked.shape
    nb = lax.axis_size("blocks")
    b = lax.axis_index("blocks")

    xm = shifted(stacked[:, nx - 1], 1, 0)
    xp = shifted(stacked[:, 0], -1, 0)
    ym = shifted(stacked[:, :, ny - 1], 0, 1)
    yp = shifted(stacked[:, :, 0], 0, -1)
    mm = shifted(stacked[:, nx - 1, ny - WIDE :], 1, 1)
    pm = shifted(stacked[:, 0, ny - 1 : ny], -1, 1)
    mp = shifted(stacked[:, nx - 1, 0:1], 1, -1)
    pp = shifted(stacked[:, 0, :WIDE], -1, -1)

    span = ny + 2
    low_line = jnp.concatenate([mm, xm, mp], axis=1)
    inner = edge_shift[0]
    low_ghost = (1.0 - edge_frac[0]) * lax.dynamic_slice_in_dim(
        low_line, WIDE - 1 - inner, span, axis=1
    ) + edge_frac[0] * lax.dynamic_slice_in_dim(low_line, WIDE - 2 - inner, span, axis=1)
    low_row = jnp.where(b == 0, low_ghost, low_line[:, WIDE - 1 : WIDE - 1 + span])

    high_line = jnp.concatenate([pm, xp, pp], axis=1)
    outer = edge_shift[1]
    high_ghost = (1.0 - edge_frac[1]) * lax.dynamic_slice_in_dim(
        high_line, outer, span, axis=1
    ) + edge_frac[1] * lax.dynamic_slice_in_dim(high_line, outer + 1, span, axis=1)
    high_row = jnp.where(b == nb - 1, high_ghost, high_line[:, :span])

    middle = jnp.concatenate([ym[:, :, None], stacked, yp[:, :, None]], axis=2)
    padded = jnp.concatenate([low_row[:, None], middle, high_row[:, None]], axis=1)

    updated = ct_update(padded)
    received = shifted(updated[:, :, ny - KMAX - 1 :], 0, 1)
    return advect(updated, received, strip_shift, strip_frac)


def solution(mesh):
    placed = (
        P(None, "blocks", "phi", None),
        P(None, "blocks", "phi", None),
        P("blocks"),
        P("blocks"),
        P(),
        P(),
    )
    return jax.shard_map(
        body, mesh=mesh, in_specs=placed, out_specs=P(None, "blocks", "phi", None), check_vma=False
    )
```

```python
import jax
import jax.numpy as jnp
from jax import lax
from jax.experimental import pallas as pl
from jax.experimental.pallas import tpu as pltpu
from jax.sharding import PartitionSpec as P

KMAX = 6
COURANT = 0.4
WIDE = KMAX + 2


def shifted(x, db, dp):
    nb, nq = lax.axis_size("blocks"), lax.axis_size("phi")
    if dp == 0:
        return lax.ppermute(x, "blocks", [(b, (b + db) % nb) for b in range(nb)])
    if db == 0:
        return lax.ppermute(x, "phi", [(q, (q + dp) % nq) for q in range(nq)])
    pairs = [
        (b * nq + q, ((b + db) % nb) * nq + (q + dp) % nq)
        for b in range(nb)
        for q in range(nq)
    ]
    return lax.ppermute(x, ("blocks", "phi"), pairs)


def below(v):
    return pltpu.roll(v, 1, 1)


def above(v):
    return pltpu.roll(v, v.shape[1] - 1, 1)


def ct_kernel(p_ref, u_ref, ez_s, ey_s, ex_s):
    rows = u_ref.shape[1]
    ny = u_ref.shape[2]

    def emf_row(a, carry):
        fx_a = p_ref[0, a, pl.ds(1, ny + 1), :]
        fx_ab = p_ref[0, a, pl.ds(0, ny + 1), :]
        fy_a = p_ref[1, a, pl.ds(1, ny + 1), :]
        fy_m = p_ref[1, a - 1, pl.ds(1, ny + 1), :]
        vx = (
            p_ref[3, a, pl.ds(1, ny + 1), :]
            + p_ref[3, a - 1, pl.ds(1, ny + 1), :]
            + p_ref[3, a, pl.ds(0, ny + 1), :]
            + p_ref[3, a - 1, pl.ds(0, ny + 1), :]
        )
        vy = (
            p_ref[4, a, pl.ds(1, ny + 1), :]
            + p_ref[4, a - 1, pl.ds(1, ny + 1), :]
            + p_ref[4, a, pl.ds(0, ny + 1), :]
            + p_ref[4, a - 1, pl.ds(0, ny + 1), :]
        )
        ez = (0.25 * vy) * (0.5 * (fx_a + fx_ab)) - (0.25 * vx) * (0.5 * (fy_a + fy_m))
        ez_s[a - 1, pl.ds(0, ny + 1), :] = ez

        mfx = p_ref[0, a, pl.ds(1, ny), :]
        mfz = p_ref[2, a, pl.ds(1, ny), :]
        mfz_m = p_ref[2, a - 1, pl.ds(1, ny), :]
        pvx = p_ref[3, a, pl.ds(1, ny), :] + p_ref[3, a - 1, pl.ds(1, ny), :]
        pvz = p_ref[5, a, pl.ds(1, ny), :] + p_ref[5, a - 1, pl.ds(1, ny), :]
        yfx = 0.5 * (mfx + below(mfx))
        yfz = 0.5 * (mfz + mfz_m)
        yvx = 0.25 * (pvx + below(pvx))
        yvz = 0.25 * (pvz + below(pvz))
        ey_s[a - 1] = yvx * yfz - yvz * yfx

        rfy = p_ref[1, a, pl.ds(1, ny + 1), :]
        rfz = p_ref[2, a, pl.ds(1, ny + 1), :]
        rfz_b = p_ref[2, a, pl.ds(0, ny + 1), :]
        cvy = p_ref[4, a, pl.ds(1, ny + 1), :] + p_ref[4, a, pl.ds(0, ny + 1), :]
        cvz = p_ref[5, a, pl.ds(1, ny + 1), :] + p_ref[5, a, pl.ds(0, ny + 1), :]
        xfy = 0.5 * (rfy + below(rfy))
        xfz = 0.5 * (rfz + rfz_b)
        xvy = 0.25 * (cvy + below(cvy))
        xvz = 0.25 * (cvz + below(cvz))
        ex_s[a - 1, pl.ds(0, ny + 1), :] = xvz * xfy - xvy * xfz
        return carry

    lax.fori_loop(1, rows + 2, emf_row, 0)

    def update_row(r, carry):
        a = r + 1
        ez_r = ez_s[r, pl.ds(0, ny), :]
        ez_r1 = ez_s[r, pl.ds(1, ny), :]
        ez_n = ez_s[r + 1, pl.ds(0, ny), :]
        ey_r = ey_s[r]
        ey_n = ey_s[r + 1]
        ex_r = ex_s[r, pl.ds(0, ny), :]
        ex_r1 = ex_s[r, pl.ds(1, ny), :]
        fx = p_ref[0, a, pl.ds(1, ny), :]
        fy = p_ref[1, a, pl.ds(1, ny), :]
        fz = p_ref[2, a, pl.ds(1, ny), :]
        u_ref[0, r] = fx - COURANT * ((ez_r1 - ez_r) - (above(ey_r) - ey_r))
        u_ref[1, r] = fy - COURANT * ((above(ex_r) - ex_r) - (ez_n - ez_r))
        u_ref[2, r] = fz - COURANT * ((ey_n - ey_r) - (ex_r1 - ex_r))
        return carry

    lax.fori_loop(0, rows, update_row, 0)


def ct_update(padded):
    _, px, py, nz = padded.shape
    rows, ny = px - 2, py - 2
    vmem = pl.BlockSpec(memory_space=pltpu.VMEM)
    return pl.pallas_call(
        ct_kernel,
        out_shape=jax.ShapeDtypeStruct((3, rows, ny, nz), padded.dtype),
        in_specs=[vmem],
        out_specs=vmem,
        scratch_shapes=[
            pltpu.VMEM((rows + 1, ny + 8, nz), jnp.float32),
            pltpu.VMEM((rows + 1, ny, nz), jnp.float32),
            pltpu.VMEM((rows + 1, ny + 8, nz), jnp.float32),
        ],
        cost_estimate=pl.CostEstimate(
            flops=120 * rows * ny * nz, transcendentals=0,
            bytes_accessed=4 * (6 * px * py + 3 * rows * ny) * nz,
        ),
    )(padded)


def advect_kernel(shift_ref, frac_ref, u_ref, rec_ref, o_ref, ext):
    rows, ny = u_ref.shape[1], u_ref.shape[2]
    lead = 8
    ext[:, :, pl.ds(lead - KMAX - 1, KMAX + 1), :] = rec_ref[...]
    ext[:, :, pl.ds(lead, ny), :] = u_ref[...]

    def strip(x, carry):
        s = shift_ref[x]
        w = frac_ref[x]
        for k in range(KMAX + 1):
            @pl.when(s == k)
            def _():
                near = ext[:, x, pl.ds(lead - k, ny), :]
                far = ext[:, x, pl.ds(lead - k - 1, ny), :]
                o_ref[:, x] = (1.0 - w) * near + w * far
        return carry

    lax.fori_loop(0, rows, strip, 0)


def advect(updated, received, strip_shift, strip_frac):
    _, rows, ny, nz = updated.shape
    vmem = pl.BlockSpec(memory_space=pltpu.VMEM)
    smem = pl.BlockSpec(memory_space=pltpu.SMEM)
    return pl.pallas_call(
        advect_kernel,
        out_shape=jax.ShapeDtypeStruct(updated.shape, updated.dtype),
        in_specs=[smem, smem, vmem, vmem],
        out_specs=vmem,
        scratch_shapes=[pltpu.VMEM((3, rows, ny + 8, nz), jnp.float32)],
        cost_estimate=pl.CostEstimate(
            flops=3 * 3 * rows * ny * nz, transcendentals=0,
            bytes_accessed=4 * 3 * rows * (2 * ny + KMAX + 1) * nz,
        ),
    )(strip_shift, strip_frac, updated, received)


def body(field, velocity, strip_shift, strip_frac, edge_shift, edge_frac):
    stacked = jnp.concatenate([field, velocity], axis=0)
    _, nx, ny, nz = stacked.shape
    nb = lax.axis_size("blocks")
    b = lax.axis_index("blocks")

    xm = shifted(stacked[:, nx - 1], 1, 0)
    xp = shifted(stacked[:, 0], -1, 0)
    low_col = jnp.concatenate(
        [xm[:, ny - WIDE :], xm[:, ny - 1 : ny], stacked[:, :, ny - 1], xp[:, ny - 1 : ny]], axis=1
    )
    high_col = jnp.concatenate(
        [xp[:, :WIDE], xm[:, 0:1], stacked[:, :, 0], xp[:, 0:1]], axis=1
    )
    from_low = shifted(low_col, 0, 1)
    from_high = shifted(high_col, 0, -1)
    ym = from_low[:, WIDE:]
    yp = from_high[:, WIDE:]

    span = ny + 2
    low_line = jnp.concatenate([from_low[:, :WIDE], xm, yp[:, 0:1]], axis=1)
    inner = edge_shift[0]
    low_ghost = (1.0 - edge_frac[0]) * lax.dynamic_slice_in_dim(
        low_line, WIDE - 1 - inner, span, axis=1
    ) + edge_frac[0] * lax.dynamic_slice_in_dim(low_line, WIDE - 2 - inner, span, axis=1)
    low_plain = jnp.concatenate([ym[:, 0:1], xm, yp[:, 0:1]], axis=1)
    low_row = jnp.where(b == 0, low_ghost, low_plain)

    high_line = jnp.concatenate([ym[:, nx + 1 :], xp, from_high[:, :WIDE]], axis=1)
    outer = edge_shift[1]
    high_ghost = (1.0 - edge_frac[1]) * lax.dynamic_slice_in_dim(
        high_line, outer, span, axis=1
    ) + edge_frac[1] * lax.dynamic_slice_in_dim(high_line, outer + 1, span, axis=1)
    high_plain = jnp.concatenate([ym[:, nx + 1 :], xp, yp[:, nx + 1 :]], axis=1)
    high_row = jnp.where(b == nb - 1, high_ghost, high_plain)

    ym = ym[:, 1 : nx + 1]
    yp = yp[:, 1 : nx + 1]
    middle = jnp.concatenate([ym[:, :, None], stacked, yp[:, :, None]], axis=2)
    padded = jnp.concatenate([low_row[:, None], middle, high_row[:, None]], axis=1)

    updated = ct_update(padded)
    received = shifted(updated[:, :, ny - KMAX - 1 :], 0, 1)
    return advect(updated, received, strip_shift, strip_frac)


def solution(mesh):
    placed = (
        P(None, "blocks", "phi", None),
        P(None, "blocks", "phi", None),
        P("blocks"),
        P("blocks"),
        P(),
        P(),
    )
    return jax.shard_map(
        body, mesh=mesh, in_specs=placed, out_specs=P(None, "blocks", "phi", None), check_vma=False
    )
```

```python
import jax
import jax.numpy as jnp
from jax import lax
from jax.experimental import pallas as pl
from jax.experimental.pallas import tpu as pltpu
from jax.sharding import PartitionSpec as P

KMAX = 6
COURANT = 0.4
WIDE = KMAX + 2


def shifted(x, db, dp):
    nb, nq = lax.axis_size("blocks"), lax.axis_size("phi")
    if dp == 0:
        return lax.ppermute(x, "blocks", [(b, (b + db) % nb) for b in range(nb)])
    if db == 0:
        return lax.ppermute(x, "phi", [(q, (q + dp) % nq) for q in range(nq)])
    pairs = [
        (b * nq + q, ((b + db) % nb) * nq + (q + dp) % nq)
        for b in range(nb)
        for q in range(nq)
    ]
    return lax.ppermute(x, ("blocks", "phi"), pairs)


def below(v):
    return pltpu.roll(v, 1, 1)


def above(v):
    return pltpu.roll(v, v.shape[1] - 1, 1)


OFF = 7


def ct_kernel(f_hbm, v_hbm, low_ref, high_ref, lcol_ref, hcol_ref, u_ref, top_ref,
              p_ref, ez_s, ey_s, ex_s, sem):
    rows = u_ref.shape[1]
    ny = u_ref.shape[2]
    copies = [
        pltpu.make_async_copy(f_hbm, p_ref.at[0:3, 1 : rows + 1, pl.ds(OFF + 1, ny)], sem.at[0]),
        pltpu.make_async_copy(v_hbm, p_ref.at[3:6, 1 : rows + 1, pl.ds(OFF + 1, ny)], sem.at[1]),
    ]
    for c in copies:
        c.start()
    p_ref[:, 0, pl.ds(OFF, ny + 2), :] = low_ref[...]
    p_ref[:, rows + 1, pl.ds(OFF, ny + 2), :] = high_ref[...]
    for a in range(rows):
        p_ref[:, a + 1, OFF, :] = lcol_ref[:, WIDE + 1 + a, :]
        p_ref[:, a + 1, OFF + ny + 1, :] = hcol_ref[:, WIDE + 1 + a, :]
    for c in copies:
        c.wait()

    def emf_row(a, carry):
        fx_a = p_ref[0, a, pl.ds(OFF + 1, ny + 1), :]
        fx_ab = p_ref[0, a, pl.ds(OFF, ny + 1), :]
        fy_a = p_ref[1, a, pl.ds(OFF + 1, ny + 1), :]
        fy_m = p_ref[1, a - 1, pl.ds(OFF + 1, ny + 1), :]
        vx = (
            p_ref[3, a, pl.ds(OFF + 1, ny + 1), :]
            + p_ref[3, a - 1, pl.ds(OFF + 1, ny + 1), :]
            + p_ref[3, a, pl.ds(OFF, ny + 1), :]
            + p_ref[3, a - 1, pl.ds(OFF, ny + 1), :]
        )
        vy = (
            p_ref[4, a, pl.ds(OFF + 1, ny + 1), :]
            + p_ref[4, a - 1, pl.ds(OFF + 1, ny + 1), :]
            + p_ref[4, a, pl.ds(OFF, ny + 1), :]
            + p_ref[4, a - 1, pl.ds(OFF, ny + 1), :]
        )
        ez = (0.25 * vy) * (0.5 * (fx_a + fx_ab)) - (0.25 * vx) * (0.5 * (fy_a + fy_m))
        ez_s[a - 1, pl.ds(0, ny + 1), :] = ez

        mfx = p_ref[0, a, pl.ds(OFF + 1, ny), :]
        mfz = p_ref[2, a, pl.ds(OFF + 1, ny), :]
        mfz_m = p_ref[2, a - 1, pl.ds(OFF + 1, ny), :]
        pvx = p_ref[3, a, pl.ds(OFF + 1, ny), :] + p_ref[3, a - 1, pl.ds(OFF + 1, ny), :]
        pvz = p_ref[5, a, pl.ds(OFF + 1, ny), :] + p_ref[5, a - 1, pl.ds(OFF + 1, ny), :]
        yfx = 0.5 * (mfx + below(mfx))
        yfz = 0.5 * (mfz + mfz_m)
        yvx = 0.25 * (pvx + below(pvx))
        yvz = 0.25 * (pvz + below(pvz))
        ey_s[a - 1] = yvx * yfz - yvz * yfx

        rfy = p_ref[1, a, pl.ds(OFF + 1, ny + 1), :]
        rfz = p_ref[2, a, pl.ds(OFF + 1, ny + 1), :]
        rfz_b = p_ref[2, a, pl.ds(OFF, ny + 1), :]
        cvy = p_ref[4, a, pl.ds(OFF + 1, ny + 1), :] + p_ref[4, a, pl.ds(OFF, ny + 1), :]
        cvz = p_ref[5, a, pl.ds(OFF + 1, ny + 1), :] + p_ref[5, a, pl.ds(OFF, ny + 1), :]
        xfy = 0.5 * (rfy + below(rfy))
        xfz = 0.5 * (rfz + rfz_b)
        xvy = 0.25 * (cvy + below(cvy))
        xvz = 0.25 * (cvz + below(cvz))
        ex_s[a - 1, pl.ds(0, ny + 1), :] = xvz * xfy - xvy * xfz
        return carry

    lax.fori_loop(1, rows + 2, emf_row, 0)

    keep = KMAX + 1

    def update_row(r, carry):
        a = r + 1
        ez_r = ez_s[r, pl.ds(0, ny), :]
        ez_r1 = ez_s[r, pl.ds(1, ny), :]
        ez_n = ez_s[r + 1, pl.ds(0, ny), :]
        ey_r = ey_s[r]
        ey_n = ey_s[r + 1]
        ex_r = ex_s[r, pl.ds(0, ny), :]
        ex_r1 = ex_s[r, pl.ds(1, ny), :]
        fx = p_ref[0, a, pl.ds(OFF + 1, ny), :]
        fy = p_ref[1, a, pl.ds(OFF + 1, ny), :]
        fz = p_ref[2, a, pl.ds(OFF + 1, ny), :]
        new = (
            fx - COURANT * ((ez_r1 - ez_r) - (above(ey_r) - ey_r)),
            fy - COURANT * ((above(ex_r) - ex_r) - (ez_n - ez_r)),
            fz - COURANT * ((ey_n - ey_r) - (ex_r1 - ex_r)),
        )
        for c in range(3):
            u_ref[c, r] = new[c]
        return carry

    lax.fori_loop(0, rows, update_row, 0)
    for c in range(3):
        for r in range(rows):
            top_ref[pl.ds((c * rows + r) * keep, keep), :] = u_ref[c, r, pl.ds(ny - keep, keep), :]


def ct_update(field, velocity, low_row, high_row, low_col, high_col):
    _, rows, ny, nz = field.shape
    keep = KMAX + 1
    vmem = pl.BlockSpec(memory_space=pltpu.VMEM)
    hbm = pl.BlockSpec(memory_space=pl.ANY)
    return pl.pallas_call(
        ct_kernel,
        out_shape=(
            jax.ShapeDtypeStruct((3, rows, ny, nz), field.dtype),
            jax.ShapeDtypeStruct((3 * rows * keep, nz), field.dtype),
        ),
        in_specs=[hbm, hbm, vmem, vmem, vmem, vmem],
        out_specs=(vmem, vmem),
        scratch_shapes=[
            pltpu.VMEM((6, rows + 2, OFF + ny + 2, nz), jnp.float32),
            pltpu.VMEM((rows + 1, ny + 8, nz), jnp.float32),
            pltpu.VMEM((rows + 1, ny, nz), jnp.float32),
            pltpu.VMEM((rows + 1, ny + 8, nz), jnp.float32),
            pltpu.SemaphoreType.DMA((2,)),
        ],
        cost_estimate=pl.CostEstimate(
            flops=120 * rows * ny * nz, transcendentals=0,
            bytes_accessed=4 * (6 * rows * ny + 3 * rows * ny) * nz,
        ),
    )(field, velocity, low_row, high_row, low_col, high_col)


def advect_kernel(shift_ref, frac_ref, u_ref, rec_ref, o_ref, ext):
    rows, ny = u_ref.shape[1], u_ref.shape[2]
    lead = 8
    keep = KMAX + 1
    for c in range(3):
        for x in range(rows):
            ext[c, x, pl.ds(lead - keep, keep), :] = rec_ref[pl.ds((c * rows + x) * keep, keep), :]
    ext[:, :, pl.ds(lead, ny), :] = u_ref[...]

    def strip(x, carry):
        s = shift_ref[x]
        w = frac_ref[x]
        for k in range(KMAX + 1):
            @pl.when(s == k)
            def _():
                near = ext[:, x, pl.ds(lead - k, ny), :]
                far = ext[:, x, pl.ds(lead - k - 1, ny), :]
                o_ref[:, x] = (1.0 - w) * near + w * far
        return carry

    lax.fori_loop(0, rows, strip, 0)


def advect(updated, received, strip_shift, strip_frac):
    _, rows, ny, nz = updated.shape
    vmem = pl.BlockSpec(memory_space=pltpu.VMEM)
    smem = pl.BlockSpec(memory_space=pltpu.SMEM)
    return pl.pallas_call(
        advect_kernel,
        out_shape=jax.ShapeDtypeStruct(updated.shape, updated.dtype),
        in_specs=[smem, smem, vmem, vmem],
        out_specs=vmem,
        scratch_shapes=[pltpu.VMEM((3, rows, ny + 8, nz), jnp.float32)],
        cost_estimate=pl.CostEstimate(
            flops=3 * 3 * rows * ny * nz, transcendentals=0,
            bytes_accessed=4 * 3 * rows * (2 * ny + KMAX + 1) * nz,
        ),
    )(strip_shift, strip_frac, updated, received)


def body(field, velocity, strip_shift, strip_frac, edge_shift, edge_frac):
    _, nx, ny, nz = field.shape
    nb = lax.axis_size("blocks")
    b = lax.axis_index("blocks")

    xm = shifted(jnp.concatenate([field[:, nx - 1], velocity[:, nx - 1]], axis=0), 1, 0)
    xp = shifted(jnp.concatenate([field[:, 0], velocity[:, 0]], axis=0), -1, 0)
    low_col = jnp.concatenate(
        [
            xm[:, ny - WIDE :],
            xm[:, ny - 1 : ny],
            jnp.concatenate([field[:, :, ny - 1], velocity[:, :, ny - 1]], axis=0),
            xp[:, ny - 1 : ny],
        ],
        axis=1,
    )
    high_col = jnp.concatenate(
        [
            xp[:, :WIDE],
            xm[:, 0:1],
            jnp.concatenate([field[:, :, 0], velocity[:, :, 0]], axis=0),
            xp[:, 0:1],
        ],
        axis=1,
    )
    from_low = shifted(low_col, 0, 1)
    from_high = shifted(high_col, 0, -1)
    ym = from_low[:, WIDE:]
    yp = from_high[:, WIDE:]

    span = ny + 2
    low_line = jnp.concatenate([from_low[:, :WIDE], xm, yp[:, 0:1]], axis=1)
    inner = edge_shift[0]
    low_ghost = (1.0 - edge_frac[0]) * lax.dynamic_slice_in_dim(
        low_line, WIDE - 1 - inner, span, axis=1
    ) + edge_frac[0] * lax.dynamic_slice_in_dim(low_line, WIDE - 2 - inner, span, axis=1)
    low_plain = jnp.concatenate([ym[:, 0:1], xm, yp[:, 0:1]], axis=1)
    low_row = jnp.where(b == 0, low_ghost, low_plain)

    high_line = jnp.concatenate([ym[:, nx + 1 :], xp, from_high[:, :WIDE]], axis=1)
    outer = edge_shift[1]
    high_ghost = (1.0 - edge_frac[1]) * lax.dynamic_slice_in_dim(
        high_line, outer, span, axis=1
    ) + edge_frac[1] * lax.dynamic_slice_in_dim(high_line, outer + 1, span, axis=1)
    high_plain = jnp.concatenate([ym[:, nx + 1 :], xp, yp[:, nx + 1 :]], axis=1)
    high_row = jnp.where(b == nb - 1, high_ghost, high_plain)

    updated, top = ct_update(field, velocity, low_row, high_row, from_low, from_high)
    received = shifted(top, 0, 1)
    return advect(updated, received, strip_shift, strip_frac)


def solution(mesh):
    placed = (
        P(None, "blocks", "phi", None),
        P(None, "blocks", "phi", None),
        P("blocks"),
        P("blocks"),
        P(),
        P(),
    )
    return jax.shard_map(
        body, mesh=mesh, in_specs=placed, out_specs=P(None, "blocks", "phi", None), check_vma=False
    )
```

```python
import jax
import jax.numpy as jnp
from jax import lax
from jax.experimental import pallas as pl
from jax.experimental.pallas import tpu as pltpu
from jax.sharding import PartitionSpec as P

KMAX = 6
COURANT = 0.4
WIDE = KMAX + 2


def shifted(x, db, dp):
    nb, nq = lax.axis_size("blocks"), lax.axis_size("phi")
    if dp == 0:
        return lax.ppermute(x, "blocks", [(b, (b + db) % nb) for b in range(nb)])
    if db == 0:
        return lax.ppermute(x, "phi", [(q, (q + dp) % nq) for q in range(nq)])
    pairs = [
        (b * nq + q, ((b + db) % nb) * nq + (q + dp) % nq)
        for b in range(nb)
        for q in range(nq)
    ]
    return lax.ppermute(x, ("blocks", "phi"), pairs)


def below(v):
    return pltpu.roll(v, 1, 1)


def above(v):
    return pltpu.roll(v, v.shape[1] - 1, 1)


OFF = 7
LEAD = 8


def assemble(f_hbm, v_hbm, low_ref, high_ref, lcol_ref, hcol_ref, p_ref, sem, y0):
    rows = p_ref.shape[1] - 2
    ny = p_ref.shape[2] - OFF - 2
    cells = ny - y0
    copies = [
        pltpu.make_async_copy(
            f_hbm.at[:, :, pl.ds(y0, cells)], p_ref.at[0:3, 1 : rows + 1, pl.ds(OFF + 1 + y0, cells)], sem.at[0]
        ),
        pltpu.make_async_copy(
            v_hbm.at[:, :, pl.ds(y0, cells)], p_ref.at[3:6, 1 : rows + 1, pl.ds(OFF + 1 + y0, cells)], sem.at[1]
        ),
    ]
    for c in copies:
        c.start()
    p_ref[:, 0, pl.ds(OFF, ny + 2), :] = low_ref[...]
    p_ref[:, rows + 1, pl.ds(OFF, ny + 2), :] = high_ref[...]
    for a in range(rows):
        if lcol_ref is not None:
            p_ref[:, a + 1, OFF, :] = lcol_ref[:, WIDE + 1 + a, :]
        if hcol_ref is not None:
            p_ref[:, a + 1, OFF + ny + 1, :] = hcol_ref[:, WIDE + 1 + a, :]
    for c in copies:
        c.wait()


def ct_window(p_ref, ez_s, ey_s, ex_s, ylo, n, emit):
    rows = p_ref.shape[1] - 2
    hi = OFF + ylo + 1
    lo = OFF + ylo

    def emf_row(a, carry):
        fx_a = p_ref[0, a, pl.ds(hi, n + 1), :]
        fx_ab = p_ref[0, a, pl.ds(lo, n + 1), :]
        fy_a = p_ref[1, a, pl.ds(hi, n + 1), :]
        fy_m = p_ref[1, a - 1, pl.ds(hi, n + 1), :]
        vx = (
            p_ref[3, a, pl.ds(hi, n + 1), :]
            + p_ref[3, a - 1, pl.ds(hi, n + 1), :]
            + p_ref[3, a, pl.ds(lo, n + 1), :]
            + p_ref[3, a - 1, pl.ds(lo, n + 1), :]
        )
        vy = (
            p_ref[4, a, pl.ds(hi, n + 1), :]
            + p_ref[4, a - 1, pl.ds(hi, n + 1), :]
            + p_ref[4, a, pl.ds(lo, n + 1), :]
            + p_ref[4, a - 1, pl.ds(lo, n + 1), :]
        )
        ez = (0.25 * vy) * (0.5 * (fx_a + fx_ab)) - (0.25 * vx) * (0.5 * (fy_a + fy_m))
        ez_s[a - 1, pl.ds(0, n + 1), :] = ez

        mfx = p_ref[0, a, pl.ds(hi, n), :]
        mfz = p_ref[2, a, pl.ds(hi, n), :]
        mfz_m = p_ref[2, a - 1, pl.ds(hi, n), :]
        pvx = p_ref[3, a, pl.ds(hi, n), :] + p_ref[3, a - 1, pl.ds(hi, n), :]
        pvz = p_ref[5, a, pl.ds(hi, n), :] + p_ref[5, a - 1, pl.ds(hi, n), :]
        yfx = 0.5 * (mfx + below(mfx))
        yfz = 0.5 * (mfz + mfz_m)
        yvx = 0.25 * (pvx + below(pvx))
        yvz = 0.25 * (pvz + below(pvz))
        ey_s[a - 1, pl.ds(0, n), :] = yvx * yfz - yvz * yfx

        rfy = p_ref[1, a, pl.ds(hi, n + 1), :]
        rfz = p_ref[2, a, pl.ds(hi, n + 1), :]
        rfz_b = p_ref[2, a, pl.ds(lo, n + 1), :]
        cvy = p_ref[4, a, pl.ds(hi, n + 1), :] + p_ref[4, a, pl.ds(lo, n + 1), :]
        cvz = p_ref[5, a, pl.ds(hi, n + 1), :] + p_ref[5, a, pl.ds(lo, n + 1), :]
        xfy = 0.5 * (rfy + below(rfy))
        xfz = 0.5 * (rfz + rfz_b)
        xvy = 0.25 * (cvy + below(cvy))
        xvz = 0.25 * (cvz + below(cvz))
        ex_s[a - 1, pl.ds(0, n + 1), :] = xvz * xfy - xvy * xfz
        return carry

    lax.fori_loop(1, rows + 2, emf_row, 0)

    def update_row(r, carry):
        a = r + 1
        ez_r = ez_s[r, pl.ds(0, n), :]
        ez_r1 = ez_s[r, pl.ds(1, n), :]
        ez_n = ez_s[r + 1, pl.ds(0, n), :]
        ey_r = ey_s[r, pl.ds(0, n), :]
        ey_n = ey_s[r + 1, pl.ds(0, n), :]
        ex_r = ex_s[r, pl.ds(0, n), :]
        ex_r1 = ex_s[r, pl.ds(1, n), :]
        fx = p_ref[0, a, pl.ds(hi, n), :]
        fy = p_ref[1, a, pl.ds(hi, n), :]
        fz = p_ref[2, a, pl.ds(hi, n), :]
        emit(0, r, fx - COURANT * ((ez_r1 - ez_r) - (above(ey_r) - ey_r)))
        emit(1, r, fy - COURANT * ((above(ex_r) - ex_r) - (ez_n - ez_r)))
        emit(2, r, fz - COURANT * ((ey_n - ey_r) - (ex_r1 - ex_r)))
        return carry

    lax.fori_loop(0, rows, update_row, 0)


def scratch_for(rows, ny, nz):
    return [
        pltpu.VMEM((6, rows + 2, OFF + ny + 2, nz), jnp.float32),
        pltpu.VMEM((rows + 1, ny + 8, nz), jnp.float32),
        pltpu.VMEM((rows + 1, ny + 8, nz), jnp.float32),
        pltpu.VMEM((rows + 1, ny + 8, nz), jnp.float32),
        pltpu.SemaphoreType.DMA((2,)),
    ]


def top_kernel(f_hbm, v_hbm, low_ref, high_ref, hcol_ref, top_ref, p_ref, ez_s, ey_s, ex_s, sem):
    rows, ny = p_ref.shape[1] - 2, p_ref.shape[2] - OFF - 2
    keep = KMAX + 1
    assemble(f_hbm, v_hbm, low_ref, high_ref, None, hcol_ref, p_ref, sem, ny - keep - 1)

    def emit(c, r, value):
        top_ref[c, r] = value

    ct_window(p_ref, ez_s, ey_s, ex_s, ny - keep, keep, emit)


def ct_top(field, velocity, low_row, high_row, high_col):
    _, rows, ny, nz = field.shape
    keep = KMAX + 1
    vmem = pl.BlockSpec(memory_space=pltpu.VMEM)
    hbm = pl.BlockSpec(memory_space=pl.ANY)
    return pl.pallas_call(
        top_kernel,
        out_shape=jax.ShapeDtypeStruct((3, rows, keep, nz), field.dtype),
        in_specs=[hbm, hbm, vmem, vmem, vmem],
        out_specs=vmem,
        scratch_shapes=scratch_for(rows, ny, nz),
        cost_estimate=pl.CostEstimate(
            flops=120 * rows * keep * nz, transcendentals=0,
            bytes_accessed=4 * 9 * rows * keep * nz,
        ),
    )(field, velocity, low_row, high_row, high_col)


def blend(ext, o_ref, x, s, w, start, count):
    for k in range(KMAX + 1):
        @pl.when(s == k)
        def _():
            near = ext[:, x, pl.ds(LEAD + start - k, count), :]
            far = ext[:, x, pl.ds(LEAD + start - k - 1, count), :]
            o_ref[:, x, pl.ds(start, count), :] = (1.0 - w) * near + w * far


def bottom_kernel(shift_ref, frac_ref, f_hbm, v_hbm, low_ref, high_ref, lcol_ref, top_ref,
                  o_ref, low_u_ref, p_ref, ez_s, ey_s, ex_s, sem, ext):
    rows, ny = p_ref.shape[1] - 2, p_ref.shape[2] - OFF - 2
    keep = KMAX + 1
    n = ny - keep
    assemble(f_hbm, v_hbm, low_ref, high_ref, lcol_ref, None, p_ref, sem, 0)

    def emit(c, r, value):
        ext[c, r, pl.ds(LEAD, n), :] = value

    ct_window(p_ref, ez_s, ey_s, ex_s, 0, n, emit)
    ext[:, :, pl.ds(LEAD + n, keep), :] = top_ref[...]
    low_u_ref[...] = ext[:, :, pl.ds(LEAD, LEAD), :]

    def strip(x, carry):
        blend(ext, o_ref, x, shift_ref[x], frac_ref[x], keep, ny - keep)
        return carry

    lax.fori_loop(0, rows, strip, 0)


def ct_bottom(strip_shift, strip_frac, field, velocity, low_row, high_row, low_col, top):
    _, rows, ny, nz = field.shape
    vmem = pl.BlockSpec(memory_space=pltpu.VMEM)
    smem = pl.BlockSpec(memory_space=pltpu.SMEM)
    hbm = pl.BlockSpec(memory_space=pl.ANY)
    keep = KMAX + 1
    return pl.pallas_call(
        bottom_kernel,
        out_shape=(
            jax.ShapeDtypeStruct(field.shape, field.dtype),
            jax.ShapeDtypeStruct((3, rows, LEAD, nz), field.dtype),
        ),
        in_specs=[smem, smem, hbm, hbm, vmem, vmem, vmem, vmem],
        out_specs=(vmem, vmem),
        scratch_shapes=scratch_for(rows, ny, nz) + [pltpu.VMEM((3, rows, LEAD + ny, nz), jnp.float32)],
        cost_estimate=pl.CostEstimate(
            flops=130 * rows * (ny - keep) * nz, transcendentals=0,
            bytes_accessed=4 * 12 * rows * ny * nz,
        ),
    )(strip_shift, strip_frac, field, velocity, low_row, high_row, low_col, top)


def edge_kernel(shift_ref, frac_ref, rec_ref, low_u_ref, part_ref, o_ref, ext):
    rows = low_u_ref.shape[1]
    keep = KMAX + 1
    ext[:, :, pl.ds(LEAD - keep, keep), :] = rec_ref[...]
    ext[:, :, pl.ds(LEAD, LEAD), :] = low_u_ref[...]
    ny = part_ref.shape[2]
    o_ref[:, :, pl.ds(keep, ny - keep), :] = part_ref[:, :, pl.ds(keep, ny - keep), :]

    def strip(x, carry):
        blend(ext, o_ref, x, shift_ref[x], frac_ref[x], 0, keep)
        return carry

    lax.fori_loop(0, rows, strip, 0)


def advect_edge(strip_shift, strip_frac, received, low_u, partial):
    _, rows, ny, nz = partial.shape
    vmem = pl.BlockSpec(memory_space=pltpu.VMEM)
    smem = pl.BlockSpec(memory_space=pltpu.SMEM)
    keep = KMAX + 1
    return pl.pallas_call(
        edge_kernel,
        out_shape=jax.ShapeDtypeStruct(partial.shape, partial.dtype),
        in_specs=[smem, smem, vmem, vmem, vmem],
        out_specs=vmem,
        scratch_shapes=[pltpu.VMEM((3, rows, 2 * LEAD, nz), jnp.float32)],
        cost_estimate=pl.CostEstimate(
            flops=9 * rows * keep * nz, transcendentals=0,
            bytes_accessed=4 * 3 * rows * 3 * keep * nz,
        ),
    )(strip_shift, strip_frac, received, low_u, partial)


def body(field, velocity, strip_shift, strip_frac, edge_shift, edge_frac):
    _, nx, ny, nz = field.shape
    nb = lax.axis_size("blocks")
    b = lax.axis_index("blocks")

    xm = shifted(jnp.concatenate([field[:, nx - 1], velocity[:, nx - 1]], axis=0), 1, 0)
    xp = shifted(jnp.concatenate([field[:, 0], velocity[:, 0]], axis=0), -1, 0)
    low_col = jnp.concatenate(
        [
            xm[:, ny - WIDE :],
            xm[:, ny - 1 : ny],
            jnp.concatenate([field[:, :, ny - 1], velocity[:, :, ny - 1]], axis=0),
            xp[:, ny - 1 : ny],
        ],
        axis=1,
    )
    high_col = jnp.concatenate(
        [
            xp[:, :WIDE],
            xm[:, 0:1],
            jnp.concatenate([field[:, :, 0], velocity[:, :, 0]], axis=0),
            xp[:, 0:1],
        ],
        axis=1,
    )
    from_low = shifted(low_col, 0, 1)
    from_high = shifted(high_col, 0, -1)
    ym = from_low[:, WIDE:]
    yp = from_high[:, WIDE:]

    span = ny + 2
    low_line = jnp.concatenate([from_low[:, :WIDE], xm, yp[:, 0:1]], axis=1)
    inner = edge_shift[0]
    low_ghost = (1.0 - edge_frac[0]) * lax.dynamic_slice_in_dim(
        low_line, WIDE - 1 - inner, span, axis=1
    ) + edge_frac[0] * lax.dynamic_slice_in_dim(low_line, WIDE - 2 - inner, span, axis=1)
    low_plain = jnp.concatenate([ym[:, 0:1], xm, yp[:, 0:1]], axis=1)
    low_row = jnp.where(b == 0, low_ghost, low_plain)

    high_line = jnp.concatenate([ym[:, nx + 1 :], xp, from_high[:, :WIDE]], axis=1)
    outer = edge_shift[1]
    high_ghost = (1.0 - edge_frac[1]) * lax.dynamic_slice_in_dim(
        high_line, outer, span, axis=1
    ) + edge_frac[1] * lax.dynamic_slice_in_dim(high_line, outer + 1, span, axis=1)
    high_plain = jnp.concatenate([ym[:, nx + 1 :], xp, yp[:, nx + 1 :]], axis=1)
    high_row = jnp.where(b == nb - 1, high_ghost, high_plain)

    top = ct_top(field, velocity, low_row, high_row, from_high)
    received = shifted(top, 0, 1)
    partial, low_u = ct_bottom(strip_shift, strip_frac, field, velocity, low_row, high_row, from_low, top)
    return advect_edge(strip_shift, strip_frac, received, low_u, partial)


def solution(mesh):
    placed = (
        P(None, "blocks", "phi", None),
        P(None, "blocks", "phi", None),
        P("blocks"),
        P("blocks"),
        P(),
        P(),
    )
    return jax.shard_map(
        body, mesh=mesh, in_specs=placed, out_specs=P(None, "blocks", "phi", None), check_vma=False
    )
```

```python
import jax
import jax.numpy as jnp
from jax import lax
from jax.experimental import pallas as pl
from jax.experimental.pallas import tpu as pltpu
from jax.sharding import PartitionSpec as P

KMAX = 6
COURANT = 0.4
WIDE = KMAX + 2


def shifted(x, db, dp):
    nb, nq = lax.axis_size("blocks"), lax.axis_size("phi")
    if dp == 0:
        return lax.ppermute(x, "blocks", [(b, (b + db) % nb) for b in range(nb)])
    if db == 0:
        return lax.ppermute(x, "phi", [(q, (q + dp) % nq) for q in range(nq)])
    pairs = [
        (b * nq + q, ((b + db) % nb) * nq + (q + dp) % nq)
        for b in range(nb)
        for q in range(nq)
    ]
    return lax.ppermute(x, ("blocks", "phi"), pairs)


def below(v):
    return pltpu.roll(v, 1, 1)


def above(v):
    return pltpu.roll(v, v.shape[1] - 1, 1)


OFF = 7


def edge_row(dst, line, plain, ghost_on, shift, weight, base, sign):
    span = dst.shape[1]

    @pl.when(ghost_on == 0)
    def _():
        dst[...] = plain

    for k in range(KMAX + 1):
        @pl.when(jnp.logical_and(ghost_on != 0, shift == k))
        def _():
            lead = base + sign * k
            dst[...] = (1.0 - weight) * line[:, pl.ds(lead, span), :] + weight * line[:, pl.ds(lead + sign, span), :]


def ct_kernel(eshift_ref, efrac_ref, flag_ref, f_hbm, v_hbm, xm_ref, xp_ref, lcol_ref, hcol_ref,
              u_ref, top_ref, p_ref, ez_s, ey_s, ex_s, line, sem):
    rows = u_ref.shape[1]
    ny = u_ref.shape[2]
    copies = [
        pltpu.make_async_copy(f_hbm, p_ref.at[0:3, 1 : rows + 1, pl.ds(OFF + 1, ny)], sem.at[0]),
        pltpu.make_async_copy(v_hbm, p_ref.at[3:6, 1 : rows + 1, pl.ds(OFF + 1, ny)], sem.at[1]),
    ]
    for c in copies:
        c.start()
    for a in range(rows):
        p_ref[:, a + 1, OFF, :] = lcol_ref[:, WIDE + 1 + a, :]
        p_ref[:, a + 1, OFF + ny + 1, :] = hcol_ref[:, WIDE + 1 + a, :]

    line[:, pl.ds(0, WIDE), :] = lcol_ref[:, pl.ds(0, WIDE), :]
    line[:, pl.ds(WIDE, ny), :] = xm_ref[...]
    line[:, WIDE + ny, :] = hcol_ref[:, WIDE, :]
    low_plain = line[:, pl.ds(WIDE - 1, ny + 2), :]
    edge_row(p_ref.at[:, 0, pl.ds(OFF, ny + 2)], line, low_plain, flag_ref[0],
             eshift_ref[0], efrac_ref[0], WIDE - 1, -1)

    line[:, 0, :] = lcol_ref[:, WIDE + rows + 1, :]
    line[:, pl.ds(1, ny), :] = xp_ref[...]
    line[:, pl.ds(ny + 1, WIDE), :] = hcol_ref[:, pl.ds(0, WIDE), :]
    high_plain = line[:, pl.ds(0, ny + 2), :]
    edge_row(p_ref.at[:, rows + 1, pl.ds(OFF, ny + 2)], line, high_plain, flag_ref[1],
             eshift_ref[1], efrac_ref[1], 0, 1)
    for c in copies:
        c.wait()

    def emf_row(a, carry):
        fx_a = p_ref[0, a, pl.ds(OFF + 1, ny + 1), :]
        fx_ab = p_ref[0, a, pl.ds(OFF, ny + 1), :]
        fy_a = p_ref[1, a, pl.ds(OFF + 1, ny + 1), :]
        fy_m = p_ref[1, a - 1, pl.ds(OFF + 1, ny + 1), :]
        vx = (
            p_ref[3, a, pl.ds(OFF + 1, ny + 1), :]
            + p_ref[3, a - 1, pl.ds(OFF + 1, ny + 1), :]
            + p_ref[3, a, pl.ds(OFF, ny + 1), :]
            + p_ref[3, a - 1, pl.ds(OFF, ny + 1), :]
        )
        vy = (
            p_ref[4, a, pl.ds(OFF + 1, ny + 1), :]
            + p_ref[4, a - 1, pl.ds(OFF + 1, ny + 1), :]
            + p_ref[4, a, pl.ds(OFF, ny + 1), :]
            + p_ref[4, a - 1, pl.ds(OFF, ny + 1), :]
        )
        ez = (0.25 * vy) * (0.5 * (fx_a + fx_ab)) - (0.25 * vx) * (0.5 * (fy_a + fy_m))
        ez_s[a - 1, pl.ds(0, ny + 1), :] = ez

        mfx = p_ref[0, a, pl.ds(OFF + 1, ny), :]
        mfz = p_ref[2, a, pl.ds(OFF + 1, ny), :]
        mfz_m = p_ref[2, a - 1, pl.ds(OFF + 1, ny), :]
        pvx = p_ref[3, a, pl.ds(OFF + 1, ny), :] + p_ref[3, a - 1, pl.ds(OFF + 1, ny), :]
        pvz = p_ref[5, a, pl.ds(OFF + 1, ny), :] + p_ref[5, a - 1, pl.ds(OFF + 1, ny), :]
        yfx = 0.5 * (mfx + below(mfx))
        yfz = 0.5 * (mfz + mfz_m)
        yvx = 0.25 * (pvx + below(pvx))
        yvz = 0.25 * (pvz + below(pvz))
        ey_s[a - 1] = yvx * yfz - yvz * yfx

        rfy = p_ref[1, a, pl.ds(OFF + 1, ny + 1), :]
        rfz = p_ref[2, a, pl.ds(OFF + 1, ny + 1), :]
        rfz_b = p_ref[2, a, pl.ds(OFF, ny + 1), :]
        cvy = p_ref[4, a, pl.ds(OFF + 1, ny + 1), :] + p_ref[4, a, pl.ds(OFF, ny + 1), :]
        cvz = p_ref[5, a, pl.ds(OFF + 1, ny + 1), :] + p_ref[5, a, pl.ds(OFF, ny + 1), :]
        xfy = 0.5 * (rfy + below(rfy))
        xfz = 0.5 * (rfz + rfz_b)
        xvy = 0.25 * (cvy + below(cvy))
        xvz = 0.25 * (cvz + below(cvz))
        ex_s[a - 1, pl.ds(0, ny + 1), :] = xvz * xfy - xvy * xfz
        return carry

    lax.fori_loop(1, rows + 2, emf_row, 0)

    keep = KMAX + 1

    def update_row(r, carry):
        a = r + 1
        ez_r = ez_s[r, pl.ds(0, ny), :]
        ez_r1 = ez_s[r, pl.ds(1, ny), :]
        ez_n = ez_s[r + 1, pl.ds(0, ny), :]
        ey_r = ey_s[r]
        ey_n = ey_s[r + 1]
        ex_r = ex_s[r, pl.ds(0, ny), :]
        ex_r1 = ex_s[r, pl.ds(1, ny), :]
        fx = p_ref[0, a, pl.ds(OFF + 1, ny), :]
        fy = p_ref[1, a, pl.ds(OFF + 1, ny), :]
        fz = p_ref[2, a, pl.ds(OFF + 1, ny), :]
        new = (
            fx - COURANT * ((ez_r1 - ez_r) - (above(ey_r) - ey_r)),
            fy - COURANT * ((above(ex_r) - ex_r) - (ez_n - ez_r)),
            fz - COURANT * ((ey_n - ey_r) - (ex_r1 - ex_r)),
        )
        for c in range(3):
            u_ref[c, r] = new[c]
        return carry

    lax.fori_loop(0, rows, update_row, 0)
    for c in range(3):
        for r in range(rows):
            top_ref[pl.ds((c * rows + r) * keep, keep), :] = u_ref[c, r, pl.ds(ny - keep, keep), :]


def ct_update(eshift, efrac, flags, field, velocity, xm, xp, low_col, high_col):
    _, rows, ny, nz = field.shape
    keep = KMAX + 1
    vmem = pl.BlockSpec(memory_space=pltpu.VMEM)
    smem = pl.BlockSpec(memory_space=pltpu.SMEM)
    hbm = pl.BlockSpec(memory_space=pl.ANY)
    return pl.pallas_call(
        ct_kernel,
        out_shape=(
            jax.ShapeDtypeStruct((3, rows, ny, nz), field.dtype),
            jax.ShapeDtypeStruct((3 * rows * keep, nz), field.dtype),
        ),
        in_specs=[smem, smem, smem, hbm, hbm, vmem, vmem, vmem, vmem],
        out_specs=(vmem, vmem),
        scratch_shapes=[
            pltpu.VMEM((6, rows + 2, OFF + ny + 2, nz), jnp.float32),
            pltpu.VMEM((rows + 1, ny + 8, nz), jnp.float32),
            pltpu.VMEM((rows + 1, ny, nz), jnp.float32),
            pltpu.VMEM((rows + 1, ny + 8, nz), jnp.float32),
            pltpu.VMEM((6, ny + WIDE + 8, nz), jnp.float32),
            pltpu.SemaphoreType.DMA((2,)),
        ],
        cost_estimate=pl.CostEstimate(
            flops=120 * rows * ny * nz, transcendentals=0,
            bytes_accessed=4 * (6 * rows * ny + 3 * rows * ny) * nz,
        ),
    )(eshift, efrac, flags, field, velocity, xm, xp, low_col, high_col)


def advect_kernel(shift_ref, frac_ref, u_ref, rec_ref, o_ref, ext):
    rows, ny = u_ref.shape[1], u_ref.shape[2]
    lead = 8
    keep = KMAX + 1
    for c in range(3):
        for x in range(rows):
            ext[c, x, pl.ds(lead - keep, keep), :] = rec_ref[pl.ds((c * rows + x) * keep, keep), :]
    ext[:, :, pl.ds(lead, ny), :] = u_ref[...]

    def strip(x, carry):
        s = shift_ref[x]
        w = frac_ref[x]
        for k in range(KMAX + 1):
            @pl.when(s == k)
            def _():
                near = ext[:, x, pl.ds(lead - k, ny), :]
                far = ext[:, x, pl.ds(lead - k - 1, ny), :]
                o_ref[:, x] = (1.0 - w) * near + w * far
        return carry

    lax.fori_loop(0, rows, strip, 0)


def advect(updated, received, strip_shift, strip_frac):
    _, rows, ny, nz = updated.shape
    vmem = pl.BlockSpec(memory_space=pltpu.VMEM)
    smem = pl.BlockSpec(memory_space=pltpu.SMEM)
    return pl.pallas_call(
        advect_kernel,
        out_shape=jax.ShapeDtypeStruct(updated.shape, updated.dtype),
        in_specs=[smem, smem, vmem, vmem],
        out_specs=vmem,
        scratch_shapes=[pltpu.VMEM((3, rows, ny + 8, nz), jnp.float32)],
        cost_estimate=pl.CostEstimate(
            flops=3 * 3 * rows * ny * nz, transcendentals=0,
            bytes_accessed=4 * 3 * rows * (2 * ny + KMAX + 1) * nz,
        ),
    )(strip_shift, strip_frac, updated, received)


def body(field, velocity, strip_shift, strip_frac, edge_shift, edge_frac):
    _, nx, ny, nz = field.shape
    nb = lax.axis_size("blocks")
    b = lax.axis_index("blocks")

    xm = shifted(jnp.concatenate([field[:, nx - 1], velocity[:, nx - 1]], axis=0), 1, 0)
    xp = shifted(jnp.concatenate([field[:, 0], velocity[:, 0]], axis=0), -1, 0)
    low_col = jnp.concatenate(
        [
            xm[:, ny - WIDE :],
            xm[:, ny - 1 : ny],
            jnp.concatenate([field[:, :, ny - 1], velocity[:, :, ny - 1]], axis=0),
            xp[:, ny - 1 : ny],
        ],
        axis=1,
    )
    high_col = jnp.concatenate(
        [
            xp[:, :WIDE],
            xm[:, 0:1],
            jnp.concatenate([field[:, :, 0], velocity[:, :, 0]], axis=0),
            xp[:, 0:1],
        ],
        axis=1,
    )
    from_low = shifted(low_col, 0, 1)
    from_high = shifted(high_col, 0, -1)
    flags = jnp.stack([b == 0, b == nb - 1]).astype(jnp.int32)
    updated, top = ct_update(edge_shift, edge_frac, flags, field, velocity, xm, xp, from_low, from_high)
    received = shifted(top, 0, 1)
    return advect(updated, received, strip_shift, strip_frac)


def solution(mesh):
    placed = (
        P(None, "blocks", "phi", None),
        P(None, "blocks", "phi", None),
        P("blocks"),
        P("blocks"),
        P(),
        P(),
    )
    return jax.shard_map(
        body, mesh=mesh, in_specs=placed, out_specs=P(None, "blocks", "phi", None), check_vma=False
    )
```

```python
import jax
import jax.numpy as jnp
from jax import lax
from jax.experimental import pallas as pl
from jax.experimental.pallas import tpu as pltpu
from jax.sharding import PartitionSpec as P

KMAX = 6
COURANT = 0.4
WIDE = KMAX + 2


def shifted(x, db, dp):
    nb, nq = lax.axis_size("blocks"), lax.axis_size("phi")
    if dp == 0:
        return lax.ppermute(x, "blocks", [(b, (b + db) % nb) for b in range(nb)])
    if db == 0:
        return lax.ppermute(x, "phi", [(q, (q + dp) % nq) for q in range(nq)])
    pairs = [
        (b * nq + q, ((b + db) % nb) * nq + (q + dp) % nq)
        for b in range(nb)
        for q in range(nq)
    ]
    return lax.ppermute(x, ("blocks", "phi"), pairs)


def below(v):
    return pltpu.roll(v, 1, 1)


def above(v):
    return pltpu.roll(v, v.shape[1] - 1, 1)


OFF = 7


def edge_row(dst, line, plain, ghost_on, shift, weight, base, sign):
    span = dst.shape[1]

    @pl.when(ghost_on == 0)
    def _():
        dst[...] = plain

    for k in range(KMAX + 1):
        @pl.when(jnp.logical_and(ghost_on != 0, shift == k))
        def _():
            lead = base + sign * k
            dst[...] = (1.0 - weight) * line[:, pl.ds(lead, span), :] + weight * line[:, pl.ds(lead + sign, span), :]


def ct_kernel(eshift_ref, efrac_ref, flag_ref, f_hbm, v_hbm, xm_ref, xp_ref, lend_ref, lown_ref, hend_ref, hown_ref,
              u_ref, top_ref, p_ref, ez_s, ey_s, ex_s, line, sem):
    rows = u_ref.shape[1]
    ny = u_ref.shape[2]
    copies = [
        pltpu.make_async_copy(f_hbm, p_ref.at[0:3, 1 : rows + 1, pl.ds(OFF + 1, ny)], sem.at[0]),
        pltpu.make_async_copy(v_hbm, p_ref.at[3:6, 1 : rows + 1, pl.ds(OFF + 1, ny)], sem.at[1]),
    ]
    for c in copies:
        c.start()
    for a in range(rows):
        p_ref[:, a + 1, OFF, :] = lown_ref[:, a, :]
        p_ref[:, a + 1, OFF + ny + 1, :] = hown_ref[:, a, :]

    line[:, pl.ds(0, WIDE), :] = lend_ref[:, pl.ds(0, WIDE), :]
    line[:, pl.ds(WIDE, ny), :] = xm_ref[...]
    line[:, WIDE + ny, :] = hend_ref[:, WIDE, :]
    low_plain = line[:, pl.ds(WIDE - 1, ny + 2), :]
    edge_row(p_ref.at[:, 0, pl.ds(OFF, ny + 2)], line, low_plain, flag_ref[0],
             eshift_ref[0], efrac_ref[0], WIDE - 1, -1)

    line[:, 0, :] = lend_ref[:, WIDE, :]
    line[:, pl.ds(1, ny), :] = xp_ref[...]
    line[:, pl.ds(ny + 1, WIDE), :] = hend_ref[:, pl.ds(0, WIDE), :]
    high_plain = line[:, pl.ds(0, ny + 2), :]
    edge_row(p_ref.at[:, rows + 1, pl.ds(OFF, ny + 2)], line, high_plain, flag_ref[1],
             eshift_ref[1], efrac_ref[1], 0, 1)
    for c in copies:
        c.wait()

    def emf_row(a, carry):
        fx_a = p_ref[0, a, pl.ds(OFF + 1, ny + 1), :]
        fx_ab = p_ref[0, a, pl.ds(OFF, ny + 1), :]
        fy_a = p_ref[1, a, pl.ds(OFF + 1, ny + 1), :]
        fy_m = p_ref[1, a - 1, pl.ds(OFF + 1, ny + 1), :]
        vx = (
            p_ref[3, a, pl.ds(OFF + 1, ny + 1), :]
            + p_ref[3, a - 1, pl.ds(OFF + 1, ny + 1), :]
            + p_ref[3, a, pl.ds(OFF, ny + 1), :]
            + p_ref[3, a - 1, pl.ds(OFF, ny + 1), :]
        )
        vy = (
            p_ref[4, a, pl.ds(OFF + 1, ny + 1), :]
            + p_ref[4, a - 1, pl.ds(OFF + 1, ny + 1), :]
            + p_ref[4, a, pl.ds(OFF, ny + 1), :]
            + p_ref[4, a - 1, pl.ds(OFF, ny + 1), :]
        )
        ez = (0.25 * vy) * (0.5 * (fx_a + fx_ab)) - (0.25 * vx) * (0.5 * (fy_a + fy_m))
        ez_s[a - 1, pl.ds(0, ny + 1), :] = ez

        mfx = p_ref[0, a, pl.ds(OFF + 1, ny), :]
        mfz = p_ref[2, a, pl.ds(OFF + 1, ny), :]
        mfz_m = p_ref[2, a - 1, pl.ds(OFF + 1, ny), :]
        pvx = p_ref[3, a, pl.ds(OFF + 1, ny), :] + p_ref[3, a - 1, pl.ds(OFF + 1, ny), :]
        pvz = p_ref[5, a, pl.ds(OFF + 1, ny), :] + p_ref[5, a - 1, pl.ds(OFF + 1, ny), :]
        yfx = 0.5 * (mfx + below(mfx))
        yfz = 0.5 * (mfz + mfz_m)
        yvx = 0.25 * (pvx + below(pvx))
        yvz = 0.25 * (pvz + below(pvz))
        ey_s[a - 1] = yvx * yfz - yvz * yfx

        rfy = p_ref[1, a, pl.ds(OFF + 1, ny + 1), :]
        rfz = p_ref[2, a, pl.ds(OFF + 1, ny + 1), :]
        rfz_b = p_ref[2, a, pl.ds(OFF, ny + 1), :]
        cvy = p_ref[4, a, pl.ds(OFF + 1, ny + 1), :] + p_ref[4, a, pl.ds(OFF, ny + 1), :]
        cvz = p_ref[5, a, pl.ds(OFF + 1, ny + 1), :] + p_ref[5, a, pl.ds(OFF, ny + 1), :]
        xfy = 0.5 * (rfy + below(rfy))
        xfz = 0.5 * (rfz + rfz_b)
        xvy = 0.25 * (cvy + below(cvy))
        xvz = 0.25 * (cvz + below(cvz))
        ex_s[a - 1, pl.ds(0, ny + 1), :] = xvz * xfy - xvy * xfz
        return carry

    lax.fori_loop(1, rows + 2, emf_row, 0)

    keep = KMAX + 1

    def update_row(r, carry):
        a = r + 1
        ez_r = ez_s[r, pl.ds(0, ny), :]
        ez_r1 = ez_s[r, pl.ds(1, ny), :]
        ez_n = ez_s[r + 1, pl.ds(0, ny), :]
        ey_r = ey_s[r]
        ey_n = ey_s[r + 1]
        ex_r = ex_s[r, pl.ds(0, ny), :]
        ex_r1 = ex_s[r, pl.ds(1, ny), :]
        fx = p_ref[0, a, pl.ds(OFF + 1, ny), :]
        fy = p_ref[1, a, pl.ds(OFF + 1, ny), :]
        fz = p_ref[2, a, pl.ds(OFF + 1, ny), :]
        new = (
            fx - COURANT * ((ez_r1 - ez_r) - (above(ey_r) - ey_r)),
            fy - COURANT * ((above(ex_r) - ex_r) - (ez_n - ez_r)),
            fz - COURANT * ((ey_n - ey_r) - (ex_r1 - ex_r)),
        )
        for c in range(3):
            u_ref[c, r] = new[c]
        return carry

    lax.fori_loop(0, rows, update_row, 0)
    for c in range(3):
        for r in range(rows):
            top_ref[pl.ds((c * rows + r) * keep, keep), :] = u_ref[c, r, pl.ds(ny - keep, keep), :]


def ct_update(eshift, efrac, flags, field, velocity, xm, xp, low_in, high_in):
    _, rows, ny, nz = field.shape
    keep = KMAX + 1
    vmem = pl.BlockSpec(memory_space=pltpu.VMEM)
    smem = pl.BlockSpec(memory_space=pltpu.SMEM)
    hbm = pl.BlockSpec(memory_space=pl.ANY)
    return pl.pallas_call(
        ct_kernel,
        out_shape=(
            jax.ShapeDtypeStruct((3, rows, ny, nz), field.dtype),
            jax.ShapeDtypeStruct((3 * rows * keep, nz), field.dtype),
        ),
        in_specs=[smem, smem, smem, hbm, hbm, vmem, vmem, vmem, vmem, vmem, vmem],
        out_specs=(vmem, vmem),
        scratch_shapes=[
            pltpu.VMEM((6, rows + 2, OFF + ny + 2, nz), jnp.float32),
            pltpu.VMEM((rows + 1, ny + 8, nz), jnp.float32),
            pltpu.VMEM((rows + 1, ny, nz), jnp.float32),
            pltpu.VMEM((rows + 1, ny + 8, nz), jnp.float32),
            pltpu.VMEM((6, ny + WIDE + 8, nz), jnp.float32),
            pltpu.SemaphoreType.DMA((2,)),
        ],
        cost_estimate=pl.CostEstimate(
            flops=120 * rows * ny * nz, transcendentals=0,
            bytes_accessed=4 * (6 * rows * ny + 3 * rows * ny) * nz,
        ),
    )(eshift, efrac, flags, field, velocity, xm, xp, *low_in, *high_in)


def advect_kernel(shift_ref, frac_ref, u_ref, rec_ref, o_ref, ext):
    rows, ny = u_ref.shape[1], u_ref.shape[2]
    lead = 8
    keep = KMAX + 1
    for c in range(3):
        for x in range(rows):
            ext[c, x, pl.ds(lead - keep, keep), :] = rec_ref[pl.ds((c * rows + x) * keep, keep), :]
    ext[:, :, pl.ds(lead, ny), :] = u_ref[...]

    def strip(x, carry):
        s = shift_ref[x]
        w = frac_ref[x]
        for k in range(KMAX + 1):
            @pl.when(s == k)
            def _():
                near = ext[:, x, pl.ds(lead - k, ny), :]
                far = ext[:, x, pl.ds(lead - k - 1, ny), :]
                o_ref[:, x] = (1.0 - w) * near + w * far
        return carry

    lax.fori_loop(0, rows, strip, 0)


def advect(updated, received, strip_shift, strip_frac):
    _, rows, ny, nz = updated.shape
    vmem = pl.BlockSpec(memory_space=pltpu.VMEM)
    smem = pl.BlockSpec(memory_space=pltpu.SMEM)
    return pl.pallas_call(
        advect_kernel,
        out_shape=jax.ShapeDtypeStruct(updated.shape, updated.dtype),
        in_specs=[smem, smem, vmem, vmem],
        out_specs=vmem,
        scratch_shapes=[pltpu.VMEM((3, rows, ny + 8, nz), jnp.float32)],
        cost_estimate=pl.CostEstimate(
            flops=3 * 3 * rows * ny * nz, transcendentals=0,
            bytes_accessed=4 * 3 * rows * (2 * ny + KMAX + 1) * nz,
        ),
    )(strip_shift, strip_frac, updated, received)


def body(field, velocity, strip_shift, strip_frac, edge_shift, edge_frac):
    _, nx, ny, nz = field.shape
    nb = lax.axis_size("blocks")
    b = lax.axis_index("blocks")

    xm = shifted(jnp.concatenate([field[:, nx - 1], velocity[:, nx - 1]], axis=0), 1, 0)
    xp = shifted(jnp.concatenate([field[:, 0], velocity[:, 0]], axis=0), -1, 0)
    own_low = jnp.concatenate([field[:, :, ny - 1], velocity[:, :, ny - 1]], axis=0)
    own_high = jnp.concatenate([field[:, :, 0], velocity[:, :, 0]], axis=0)
    low_ends = jnp.concatenate([xm[:, ny - WIDE :], xp[:, ny - 1 : ny]], axis=1)
    high_ends = jnp.concatenate([xp[:, :WIDE], xm[:, 0:1]], axis=1)
    from_low = shifted((low_ends, own_low), 0, 1)
    from_high = shifted((high_ends, own_high), 0, -1)
    flags = jnp.stack([b == 0, b == nb - 1]).astype(jnp.int32)
    updated, top = ct_update(edge_shift, edge_frac, flags, field, velocity, xm, xp, from_low, from_high)
    received = shifted(top, 0, 1)
    return advect(updated, received, strip_shift, strip_frac)


def solution(mesh):
    placed = (
        P(None, "blocks", "phi", None),
        P(None, "blocks", "phi", None),
        P("blocks"),
        P("blocks"),
        P(),
        P(),
    )
    return jax.shard_map(
        body, mesh=mesh, in_specs=placed, out_specs=P(None, "blocks", "phi", None), check_vma=False
    )
```

```python
import jax
import jax.numpy as jnp
from jax import lax
from jax.experimental import pallas as pl
from jax.experimental.pallas import tpu as pltpu
from jax.sharding import PartitionSpec as P

KMAX = 6
COURANT = 0.4
WIDE = KMAX + 2


def shifted(x, db, dp):
    nb, nq = lax.axis_size("blocks"), lax.axis_size("phi")
    if dp == 0:
        return lax.ppermute(x, "blocks", [(b, (b + db) % nb) for b in range(nb)])
    if db == 0:
        return lax.ppermute(x, "phi", [(q, (q + dp) % nq) for q in range(nq)])
    pairs = [
        (b * nq + q, ((b + db) % nb) * nq + (q + dp) % nq)
        for b in range(nb)
        for q in range(nq)
    ]
    return lax.ppermute(x, ("blocks", "phi"), pairs)


def below(v):
    return pltpu.roll(v, 1, 1)


def above(v):
    return pltpu.roll(v, v.shape[1] - 1, 1)


OFF = 7


def edge_row(dst, line, plain, ghost_on, shift, weight, base, sign):
    span = dst.shape[1]

    @pl.when(ghost_on == 0)
    def _():
        dst[...] = plain

    for k in range(KMAX + 1):
        @pl.when(jnp.logical_and(ghost_on != 0, shift == k))
        def _():
            lead = base + sign * k
            dst[...] = (1.0 - weight) * line[:, pl.ds(lead, span), :] + weight * line[:, pl.ds(lead + sign, span), :]


def ct_kernel(eshift_ref, efrac_ref, flag_ref, f_hbm, v_hbm, xm_ref, xp_ref, lend_ref, lown_ref, hend_ref, hown_ref,
              u_ref, top_ref, p_ref, ez_s, ey_s, ex_s, line, sem):
    rows = u_ref.shape[1]
    ny = u_ref.shape[2]
    copies = [
        pltpu.make_async_copy(f_hbm, p_ref.at[0:3, 1 : rows + 1, pl.ds(OFF + 1, ny)], sem.at[0]),
        pltpu.make_async_copy(v_hbm, p_ref.at[3:6, 1 : rows + 1, pl.ds(OFF + 1, ny)], sem.at[1]),
    ]
    for c in copies:
        c.start()
    for a in range(rows):
        p_ref[:, a + 1, OFF, :] = lown_ref[:, a, :]
        p_ref[:, a + 1, OFF + ny + 1, :] = hown_ref[:, a, :]

    line[:, pl.ds(0, WIDE), :] = lend_ref[:, pl.ds(0, WIDE), :]
    line[:, pl.ds(WIDE, ny), :] = xm_ref[...]
    line[:, WIDE + ny, :] = hend_ref[:, WIDE, :]
    low_plain = line[:, pl.ds(WIDE - 1, ny + 2), :]
    edge_row(p_ref.at[:, 0, pl.ds(OFF, ny + 2)], line, low_plain, flag_ref[0],
             eshift_ref[0], efrac_ref[0], WIDE - 1, -1)

    line[:, 0, :] = lend_ref[:, WIDE, :]
    line[:, pl.ds(1, ny), :] = xp_ref[...]
    line[:, pl.ds(ny + 1, WIDE), :] = hend_ref[:, pl.ds(0, WIDE), :]
    high_plain = line[:, pl.ds(0, ny + 2), :]
    edge_row(p_ref.at[:, rows + 1, pl.ds(OFF, ny + 2)], line, high_plain, flag_ref[1],
             eshift_ref[1], efrac_ref[1], 0, 1)
    for c in copies:
        c.wait()

    def emf_row(a, carry):
        hi, lo, m = pl.ds(OFF + 1, ny + 1), pl.ds(OFF, ny + 1), a - 1
        fx_hi, fx_lo = p_ref[0, a, hi, :], p_ref[0, a, lo, :]
        fy_hi, fy_m = p_ref[1, a, hi, :], p_ref[1, m, hi, :]
        fz_hi, fz_lo, fz_m = p_ref[2, a, hi, :], p_ref[2, a, lo, :], p_ref[2, m, hi, :]
        vx_hi, vx_lo = p_ref[3, a, hi, :], p_ref[3, a, lo, :]
        vxm_hi, vxm_lo = p_ref[3, m, hi, :], p_ref[3, m, lo, :]
        vy_hi, vy_lo = p_ref[4, a, hi, :], p_ref[4, a, lo, :]
        vym_hi, vym_lo = p_ref[4, m, hi, :], p_ref[4, m, lo, :]
        vz_hi, vz_lo, vzm_hi = p_ref[5, a, hi, :], p_ref[5, a, lo, :], p_ref[5, m, hi, :]

        pair_x = vx_hi + vxm_hi
        pair_y = vy_hi + vym_hi
        vx = pair_x + (vx_lo + vxm_lo)
        vy = pair_y + (vy_lo + vym_lo)
        ez = (0.25 * vy) * (0.5 * (fx_hi + fx_lo)) - (0.25 * vx) * (0.5 * (fy_hi + fy_m))
        ez_s[a - 1, pl.ds(0, ny + 1), :] = ez

        mfx = fx_hi[:ny]
        pvx = pair_x[:ny]
        pvz = (vz_hi + vzm_hi)[:ny]
        yfx = 0.5 * (mfx + below(mfx))
        yfz = 0.5 * (fz_hi[:ny] + fz_m[:ny])
        yvx = 0.25 * (pvx + below(pvx))
        yvz = 0.25 * (pvz + below(pvz))
        ey_s[a - 1] = yvx * yfz - yvz * yfx

        @pl.when(a <= rows)
        def _():
            cvy = vy_hi + vy_lo
            cvz = vz_hi + vz_lo
            xfy = 0.5 * (fy_hi + below(fy_hi))
            xfz = 0.5 * (fz_hi + fz_lo)
            xvy = 0.25 * (cvy + below(cvy))
            xvz = 0.25 * (cvz + below(cvz))
            ex_s[a - 1, pl.ds(0, ny + 1), :] = xvz * xfy - xvy * xfz

        return carry

    lax.fori_loop(1, rows + 2, emf_row, 0)

    keep = KMAX + 1

    def update_row(r, carry):
        a = r + 1
        ez_r = ez_s[r, pl.ds(0, ny), :]
        ez_r1 = ez_s[r, pl.ds(1, ny), :]
        ez_n = ez_s[r + 1, pl.ds(0, ny), :]
        ey_r = ey_s[r]
        ey_n = ey_s[r + 1]
        ex_r = ex_s[r, pl.ds(0, ny), :]
        ex_r1 = ex_s[r, pl.ds(1, ny), :]
        fx = p_ref[0, a, pl.ds(OFF + 1, ny), :]
        fy = p_ref[1, a, pl.ds(OFF + 1, ny), :]
        fz = p_ref[2, a, pl.ds(OFF + 1, ny), :]
        new = (
            fx - COURANT * ((ez_r1 - ez_r) - (above(ey_r) - ey_r)),
            fy - COURANT * ((above(ex_r) - ex_r) - (ez_n - ez_r)),
            fz - COURANT * ((ey_n - ey_r) - (ex_r1 - ex_r)),
        )
        for c in range(3):
            u_ref[c, r] = new[c]
        return carry

    lax.fori_loop(0, rows, update_row, 0)
    for c in range(3):
        for r in range(rows):
            top_ref[pl.ds((c * rows + r) * keep, keep), :] = u_ref[c, r, pl.ds(ny - keep, keep), :]


def ct_update(eshift, efrac, flags, field, velocity, xm, xp, low_in, high_in):
    _, rows, ny, nz = field.shape
    keep = KMAX + 1
    vmem = pl.BlockSpec(memory_space=pltpu.VMEM)
    smem = pl.BlockSpec(memory_space=pltpu.SMEM)
    hbm = pl.BlockSpec(memory_space=pl.ANY)
    return pl.pallas_call(
        ct_kernel,
        out_shape=(
            jax.ShapeDtypeStruct((3, rows, ny, nz), field.dtype),
            jax.ShapeDtypeStruct((3 * rows * keep, nz), field.dtype),
        ),
        in_specs=[smem, smem, smem, hbm, hbm, vmem, vmem, vmem, vmem, vmem, vmem],
        out_specs=(vmem, vmem),
        scratch_shapes=[
            pltpu.VMEM((6, rows + 2, OFF + ny + 2, nz), jnp.float32),
            pltpu.VMEM((rows + 1, ny + 8, nz), jnp.float32),
            pltpu.VMEM((rows + 1, ny, nz), jnp.float32),
            pltpu.VMEM((rows + 1, ny + 8, nz), jnp.float32),
            pltpu.VMEM((6, ny + WIDE + 8, nz), jnp.float32),
            pltpu.SemaphoreType.DMA((2,)),
        ],
        cost_estimate=pl.CostEstimate(
            flops=120 * rows * ny * nz, transcendentals=0,
            bytes_accessed=4 * (6 * rows * ny + 3 * rows * ny) * nz,
        ),
    )(eshift, efrac, flags, field, velocity, xm, xp, *low_in, *high_in)


def advect_kernel(shift_ref, frac_ref, u_ref, rec_ref, o_ref, ext):
    rows, ny = u_ref.shape[1], u_ref.shape[2]
    lead = 8
    keep = KMAX + 1
    for c in range(3):
        for x in range(rows):
            ext[c, x, pl.ds(lead - keep, keep), :] = rec_ref[pl.ds((c * rows + x) * keep, keep), :]
    ext[:, :, pl.ds(lead, ny), :] = u_ref[...]

    def strip(x, carry):
        s = shift_ref[x]
        w = frac_ref[x]
        for k in range(KMAX + 1):
            @pl.when(s == k)
            def _():
                near = ext[:, x, pl.ds(lead - k, ny), :]
                far = ext[:, x, pl.ds(lead - k - 1, ny), :]
                o_ref[:, x] = (1.0 - w) * near + w * far
        return carry

    lax.fori_loop(0, rows, strip, 0)


def advect(updated, received, strip_shift, strip_frac):
    _, rows, ny, nz = updated.shape
    vmem = pl.BlockSpec(memory_space=pltpu.VMEM)
    smem = pl.BlockSpec(memory_space=pltpu.SMEM)
    return pl.pallas_call(
        advect_kernel,
        out_shape=jax.ShapeDtypeStruct(updated.shape, updated.dtype),
        in_specs=[smem, smem, vmem, vmem],
        out_specs=vmem,
        scratch_shapes=[pltpu.VMEM((3, rows, ny + 8, nz), jnp.float32)],
        cost_estimate=pl.CostEstimate(
            flops=3 * 3 * rows * ny * nz, transcendentals=0,
            bytes_accessed=4 * 3 * rows * (2 * ny + KMAX + 1) * nz,
        ),
    )(strip_shift, strip_frac, updated, received)


def body(field, velocity, strip_shift, strip_frac, edge_shift, edge_frac):
    _, nx, ny, nz = field.shape
    nb = lax.axis_size("blocks")
    b = lax.axis_index("blocks")

    xm = shifted(jnp.concatenate([field[:, nx - 1], velocity[:, nx - 1]], axis=0), 1, 0)
    xp = shifted(jnp.concatenate([field[:, 0], velocity[:, 0]], axis=0), -1, 0)
    own_low = jnp.concatenate([field[:, :, ny - 1], velocity[:, :, ny - 1]], axis=0)
    own_high = jnp.concatenate([field[:, :, 0], velocity[:, :, 0]], axis=0)
    low_ends = jnp.concatenate([xm[:, ny - WIDE :], xp[:, ny - 1 : ny]], axis=1)
    high_ends = jnp.concatenate([xp[:, :WIDE], xm[:, 0:1]], axis=1)
    from_low = shifted((low_ends, own_low), 0, 1)
    from_high = shifted((high_ends, own_high), 0, -1)
    flags = jnp.stack([b == 0, b == nb - 1]).astype(jnp.int32)
    updated, top = ct_update(edge_shift, edge_frac, flags, field, velocity, xm, xp, from_low, from_high)
    received = shifted(top, 0, 1)
    return advect(updated, received, strip_shift, strip_frac)


def solution(mesh):
    placed = (
        P(None, "blocks", "phi", None),
        P(None, "blocks", "phi", None),
        P("blocks"),
        P("blocks"),
        P(),
        P(),
    )
    return jax.shard_map(
        body, mesh=mesh, in_specs=placed, out_specs=P(None, "blocks", "phi", None), check_vma=False
    )
```

```python
import jax
import jax.numpy as jnp
from jax import lax
from jax.experimental import pallas as pl
from jax.experimental.pallas import tpu as pltpu
from jax.sharding import PartitionSpec as P

KMAX = 6
COURANT = 0.4
WIDE = KMAX + 2


def shifted(x, db, dp):
    nb, nq = lax.axis_size("blocks"), lax.axis_size("phi")
    if dp == 0:
        return lax.ppermute(x, "blocks", [(b, (b + db) % nb) for b in range(nb)])
    if db == 0:
        return lax.ppermute(x, "phi", [(q, (q + dp) % nq) for q in range(nq)])
    pairs = [
        (b * nq + q, ((b + db) % nb) * nq + (q + dp) % nq)
        for b in range(nb)
        for q in range(nq)
    ]
    return lax.ppermute(x, ("blocks", "phi"), pairs)


def below(v):
    return pltpu.roll(v, 1, 1)


def above(v):
    return pltpu.roll(v, v.shape[1] - 1, 1)


OFF = 7


def edge_row(dst, line, plain, ghost_on, shift, weight, base, sign):
    span = dst.shape[1]

    @pl.when(ghost_on == 0)
    def _():
        dst[...] = plain

    for k in range(KMAX + 1):
        @pl.when(jnp.logical_and(ghost_on != 0, shift == k))
        def _():
            lead = base + sign * k
            dst[...] = (1.0 - weight) * line[:, pl.ds(lead, span), :] + weight * line[:, pl.ds(lead + sign, span), :]


def ct_kernel(eshift_ref, efrac_ref, flag_ref, f_hbm, v_hbm, xm_ref, xp_ref, lend_ref, lown_ref, hend_ref, hown_ref,
              u_ref, top_ref, p_ref, ez_s, ey_s, ex_s, line, sem):
    rows = u_ref.shape[1]
    ny = u_ref.shape[2]
    copies = [
        pltpu.make_async_copy(f_hbm, p_ref.at[0:3, 1 : rows + 1, pl.ds(OFF + 1, ny)], sem.at[0]),
        pltpu.make_async_copy(v_hbm, p_ref.at[3:6, 1 : rows + 1, pl.ds(OFF + 1, ny)], sem.at[1]),
    ]
    for c in copies:
        c.start()
    for a in range(rows):
        p_ref[:, a + 1, OFF, :] = lown_ref[:, a, :]
        p_ref[:, a + 1, OFF + ny + 1, :] = hown_ref[:, a, :]

    line[:, pl.ds(0, WIDE), :] = lend_ref[:, pl.ds(0, WIDE), :]
    line[:, pl.ds(WIDE, ny), :] = xm_ref[...]
    line[:, WIDE + ny, :] = hend_ref[:, WIDE, :]
    low_plain = line[:, pl.ds(WIDE - 1, ny + 2), :]
    edge_row(p_ref.at[:, 0, pl.ds(OFF, ny + 2)], line, low_plain, flag_ref[0],
             eshift_ref[0], efrac_ref[0], WIDE - 1, -1)

    line[:, 0, :] = lend_ref[:, WIDE, :]
    line[:, pl.ds(1, ny), :] = xp_ref[...]
    line[:, pl.ds(ny + 1, WIDE), :] = hend_ref[:, pl.ds(0, WIDE), :]
    high_plain = line[:, pl.ds(0, ny + 2), :]
    edge_row(p_ref.at[:, rows + 1, pl.ds(OFF, ny + 2)], line, high_plain, flag_ref[1],
             eshift_ref[1], efrac_ref[1], 0, 1)
    for c in copies:
        c.wait()

    def emf_row(a, carry):
        fx_a = p_ref[0, a, pl.ds(OFF + 1, ny + 1), :]
        fx_ab = p_ref[0, a, pl.ds(OFF, ny + 1), :]
        fy_a = p_ref[1, a, pl.ds(OFF + 1, ny + 1), :]
        fy_m = p_ref[1, a - 1, pl.ds(OFF + 1, ny + 1), :]
        vx = (
            p_ref[3, a, pl.ds(OFF + 1, ny + 1), :]
            + p_ref[3, a - 1, pl.ds(OFF + 1, ny + 1), :]
            + p_ref[3, a, pl.ds(OFF, ny + 1), :]
            + p_ref[3, a - 1, pl.ds(OFF, ny + 1), :]
        )
        vy = (
            p_ref[4, a, pl.ds(OFF + 1, ny + 1), :]
            + p_ref[4, a - 1, pl.ds(OFF + 1, ny + 1), :]
            + p_ref[4, a, pl.ds(OFF, ny + 1), :]
            + p_ref[4, a - 1, pl.ds(OFF, ny + 1), :]
        )
        ez = (0.25 * vy) * (0.5 * (fx_a + fx_ab)) - (0.25 * vx) * (0.5 * (fy_a + fy_m))
        ez_s[a - 1, pl.ds(0, ny + 1), :] = ez

        mfx = p_ref[0, a, pl.ds(OFF + 1, ny), :]
        mfz = p_ref[2, a, pl.ds(OFF + 1, ny), :]
        mfz_m = p_ref[2, a - 1, pl.ds(OFF + 1, ny), :]
        pvx = p_ref[3, a, pl.ds(OFF + 1, ny), :] + p_ref[3, a - 1, pl.ds(OFF + 1, ny), :]
        pvz = p_ref[5, a, pl.ds(OFF + 1, ny), :] + p_ref[5, a - 1, pl.ds(OFF + 1, ny), :]
        yfx = 0.5 * (mfx + below(mfx))
        yfz = 0.5 * (mfz + mfz_m)
        yvx = 0.25 * (pvx + below(pvx))
        yvz = 0.25 * (pvz + below(pvz))
        ey_s[a - 1] = yvx * yfz - yvz * yfx

        rfy = p_ref[1, a, pl.ds(OFF + 1, ny + 1), :]
        rfz = p_ref[2, a, pl.ds(OFF + 1, ny + 1), :]
        rfz_b = p_ref[2, a, pl.ds(OFF, ny + 1), :]
        cvy = p_ref[4, a, pl.ds(OFF + 1, ny + 1), :] + p_ref[4, a, pl.ds(OFF, ny + 1), :]
        cvz = p_ref[5, a, pl.ds(OFF + 1, ny + 1), :] + p_ref[5, a, pl.ds(OFF, ny + 1), :]
        xfy = 0.5 * (rfy + below(rfy))
        xfz = 0.5 * (rfz + rfz_b)
        xvy = 0.25 * (cvy + below(cvy))
        xvz = 0.25 * (cvz + below(cvz))
        ex_s[a - 1, pl.ds(0, ny + 1), :] = xvz * xfy - xvy * xfz
        return carry

    lax.fori_loop(1, rows + 2, emf_row, 0)

    keep = KMAX + 1

    def update_row(r, carry):
        a = r + 1
        ez_r = ez_s[r, pl.ds(0, ny), :]
        ez_r1 = ez_s[r, pl.ds(1, ny), :]
        ez_n = ez_s[r + 1, pl.ds(0, ny), :]
        ey_r = ey_s[r]
        ey_n = ey_s[r + 1]
        ex_r = ex_s[r, pl.ds(0, ny), :]
        ex_r1 = ex_s[r, pl.ds(1, ny), :]
        fx = p_ref[0, a, pl.ds(OFF + 1, ny), :]
        fy = p_ref[1, a, pl.ds(OFF + 1, ny), :]
        fz = p_ref[2, a, pl.ds(OFF + 1, ny), :]
        new = (
            fx - COURANT * ((ez_r1 - ez_r) - (above(ey_r) - ey_r)),
            fy - COURANT * ((above(ex_r) - ex_r) - (ez_n - ez_r)),
            fz - COURANT * ((ey_n - ey_r) - (ex_r1 - ex_r)),
        )
        for c in range(3):
            u_ref[c, r] = new[c]
        return carry

    lax.fori_loop(0, rows, update_row, 0)
    for c in range(3):
        for r in range(rows):
            top_ref[pl.ds((c * rows + r) * keep, keep), :] = u_ref[c, r, pl.ds(ny - keep, keep), :]


def ct_update(eshift, efrac, flags, field, velocity, xm, xp, low_in, high_in):
    _, rows, ny, nz = field.shape
    keep = KMAX + 1
    vmem = pl.BlockSpec(memory_space=pltpu.VMEM)
    smem = pl.BlockSpec(memory_space=pltpu.SMEM)
    hbm = pl.BlockSpec(memory_space=pl.ANY)
    return pl.pallas_call(
        ct_kernel,
        out_shape=(
            jax.ShapeDtypeStruct((3, rows, ny, nz), field.dtype),
            jax.ShapeDtypeStruct((3 * rows * keep, nz), field.dtype),
        ),
        in_specs=[smem, smem, smem, hbm, hbm, vmem, vmem, vmem, vmem, vmem, vmem],
        out_specs=(vmem, vmem),
        scratch_shapes=[
            pltpu.VMEM((6, rows + 2, OFF + ny + 2, nz), jnp.float32),
            pltpu.VMEM((rows + 1, ny + 8, nz), jnp.float32),
            pltpu.VMEM((rows + 1, ny, nz), jnp.float32),
            pltpu.VMEM((rows + 1, ny + 8, nz), jnp.float32),
            pltpu.VMEM((6, ny + WIDE + 8, nz), jnp.float32),
            pltpu.SemaphoreType.DMA((2,)),
        ],
        cost_estimate=pl.CostEstimate(
            flops=120 * rows * ny * nz, transcendentals=0,
            bytes_accessed=4 * (6 * rows * ny + 3 * rows * ny) * nz,
        ),
    )(eshift, efrac, flags, field, velocity, xm, xp, *low_in, *high_in)


def advect_kernel(shift_ref, frac_ref, u_ref, rec_hbm, o_ref, flat, ext, sem):
    rows, ny = u_ref.shape[1], u_ref.shape[2]
    lead = 8
    keep = KMAX + 1
    fetch = pltpu.make_async_copy(rec_hbm, flat, sem.at[0])
    fetch.start()

    def inner(x, carry):
        s = shift_ref[x]
        w = frac_ref[x]
        for k in range(KMAX + 1):
            @pl.when(s == k)
            def _():
                near = u_ref[:, x, pl.ds(keep - k, ny - keep), :]
                far = u_ref[:, x, pl.ds(keep - k - 1, ny - keep), :]
                o_ref[:, x, pl.ds(keep, ny - keep), :] = (1.0 - w) * near + w * far
        return carry

    lax.fori_loop(0, rows, inner, 0)
    ext[:, :, pl.ds(lead, lead), :] = u_ref[:, :, pl.ds(0, lead), :]
    fetch.wait()
    for c in range(3):
        for x in range(rows):
            ext[c, x, pl.ds(lead - keep, keep), :] = flat[pl.ds((c * rows + x) * keep, keep), :]

    def edge(x, carry):
        s = shift_ref[x]
        w = frac_ref[x]
        for k in range(KMAX + 1):
            @pl.when(s == k)
            def _():
                near = ext[:, x, pl.ds(lead - k, keep), :]
                far = ext[:, x, pl.ds(lead - k - 1, keep), :]
                o_ref[:, x, pl.ds(0, keep), :] = (1.0 - w) * near + w * far
        return carry

    lax.fori_loop(0, rows, edge, 0)


def advect(updated, received, strip_shift, strip_frac):
    _, rows, ny, nz = updated.shape
    vmem = pl.BlockSpec(memory_space=pltpu.VMEM)
    smem = pl.BlockSpec(memory_space=pltpu.SMEM)
    hbm = pl.BlockSpec(memory_space=pl.ANY)
    return pl.pallas_call(
        advect_kernel,
        out_shape=jax.ShapeDtypeStruct(updated.shape, updated.dtype),
        in_specs=[smem, smem, vmem, hbm],
        out_specs=vmem,
        scratch_shapes=[
            pltpu.VMEM(received.shape, jnp.float32),
            pltpu.VMEM((3, rows, 2 * 8, nz), jnp.float32),
            pltpu.SemaphoreType.DMA((1,)),
        ],
        cost_estimate=pl.CostEstimate(
            flops=3 * 3 * rows * ny * nz, transcendentals=0,
            bytes_accessed=4 * 3 * rows * (2 * ny + KMAX + 1) * nz,
        ),
    )(strip_shift, strip_frac, updated, received)


def body(field, velocity, strip_shift, strip_frac, edge_shift, edge_frac):
    _, nx, ny, nz = field.shape
    nb = lax.axis_size("blocks")
    b = lax.axis_index("blocks")

    xm = shifted(jnp.concatenate([field[:, nx - 1], velocity[:, nx - 1]], axis=0), 1, 0)
    xp = shifted(jnp.concatenate([field[:, 0], velocity[:, 0]], axis=0), -1, 0)
    own_low = jnp.concatenate([field[:, :, ny - 1], velocity[:, :, ny - 1]], axis=0)
    own_high = jnp.concatenate([field[:, :, 0], velocity[:, :, 0]], axis=0)
    low_ends = jnp.concatenate([xm[:, ny - WIDE :], xp[:, ny - 1 : ny]], axis=1)
    high_ends = jnp.concatenate([xp[:, :WIDE], xm[:, 0:1]], axis=1)
    from_low = shifted((low_ends, own_low), 0, 1)
    from_high = shifted((high_ends, own_high), 0, -1)
    flags = jnp.stack([b == 0, b == nb - 1]).astype(jnp.int32)
    updated, top = ct_update(edge_shift, edge_frac, flags, field, velocity, xm, xp, from_low, from_high)
    received = shifted(top, 0, 1)
    return advect(updated, received, strip_shift, strip_frac)


def solution(mesh):
    placed = (
        P(None, "blocks", "phi", None),
        P(None, "blocks", "phi", None),
        P("blocks"),
        P("blocks"),
        P(),
        P(),
    )
    return jax.shard_map(
        body, mesh=mesh, in_specs=placed, out_specs=P(None, "blocks", "phi", None), check_vma=False
    )
```

```python
import jax
import jax.numpy as jnp
from jax import lax
from jax.experimental import pallas as pl
from jax.experimental.pallas import tpu as pltpu
from jax.sharding import PartitionSpec as P

KMAX = 6
COURANT = 0.4
WIDE = KMAX + 2


def shifted(x, db, dp):
    nb, nq = lax.axis_size("blocks"), lax.axis_size("phi")
    if dp == 0:
        return lax.ppermute(x, "blocks", [(b, (b + db) % nb) for b in range(nb)])
    if db == 0:
        return lax.ppermute(x, "phi", [(q, (q + dp) % nq) for q in range(nq)])
    pairs = [
        (b * nq + q, ((b + db) % nb) * nq + (q + dp) % nq)
        for b in range(nb)
        for q in range(nq)
    ]
    return lax.ppermute(x, ("blocks", "phi"), pairs)


def below(v):
    return pltpu.roll(v, 1, 1)


def above(v):
    return pltpu.roll(v, v.shape[1] - 1, 1)


OFF = 7


def edge_row(dst, line, plain, ghost_on, shift, weight, base, sign):
    span = dst.shape[1]

    @pl.when(ghost_on == 0)
    def _():
        dst[...] = plain

    for k in range(KMAX + 1):
        @pl.when(jnp.logical_and(ghost_on != 0, shift == k))
        def _():
            lead = base + sign * k
            dst[...] = (1.0 - weight) * line[:, pl.ds(lead, span), :] + weight * line[:, pl.ds(lead + sign, span), :]


def ct_kernel(eshift_ref, efrac_ref, flag_ref, f_hbm, v_hbm, xm_ref, xp_ref, lend_ref, lown_ref, hend_ref, hown_ref,
              u_ref, top_ref, p_ref, ez_s, ey_s, ex_s, line, sem):
    rows = u_ref.shape[1]
    ny = u_ref.shape[2]
    copies = [
        pltpu.make_async_copy(f_hbm, p_ref.at[0:3, 1 : rows + 1, pl.ds(OFF + 1, ny)], sem.at[0]),
        pltpu.make_async_copy(v_hbm, p_ref.at[3:6, 1 : rows + 1, pl.ds(OFF + 1, ny)], sem.at[1]),
    ]
    for c in copies:
        c.start()
    for a in range(rows):
        p_ref[:, a + 1, OFF, :] = lown_ref[:, a, :]
        p_ref[:, a + 1, OFF + ny + 1, :] = hown_ref[:, a, :]

    line[:, pl.ds(0, WIDE), :] = lend_ref[:, pl.ds(0, WIDE), :]
    line[:, pl.ds(WIDE, ny), :] = xm_ref[...]
    line[:, WIDE + ny, :] = hend_ref[:, WIDE, :]
    low_plain = line[:, pl.ds(WIDE - 1, ny + 2), :]
    edge_row(p_ref.at[:, 0, pl.ds(OFF, ny + 2)], line, low_plain, flag_ref[0],
             eshift_ref[0], efrac_ref[0], WIDE - 1, -1)

    line[:, 0, :] = lend_ref[:, WIDE, :]
    line[:, pl.ds(1, ny), :] = xp_ref[...]
    line[:, pl.ds(ny + 1, WIDE), :] = hend_ref[:, pl.ds(0, WIDE), :]
    high_plain = line[:, pl.ds(0, ny + 2), :]
    edge_row(p_ref.at[:, rows + 1, pl.ds(OFF, ny + 2)], line, high_plain, flag_ref[1],
             eshift_ref[1], efrac_ref[1], 0, 1)
    for c in copies:
        c.wait()

    def emf_row(a, carry):
        fx_a = p_ref[0, a, pl.ds(OFF + 1, ny + 1), :]
        fx_ab = p_ref[0, a, pl.ds(OFF, ny + 1), :]
        fy_a = p_ref[1, a, pl.ds(OFF + 1, ny + 1), :]
        fy_m = p_ref[1, a - 1, pl.ds(OFF + 1, ny + 1), :]
        vx = (
            p_ref[3, a, pl.ds(OFF + 1, ny + 1), :]
            + p_ref[3, a - 1, pl.ds(OFF + 1, ny + 1), :]
            + p_ref[3, a, pl.ds(OFF, ny + 1), :]
            + p_ref[3, a - 1, pl.ds(OFF, ny + 1), :]
        )
        vy = (
            p_ref[4, a, pl.ds(OFF + 1, ny + 1), :]
            + p_ref[4, a - 1, pl.ds(OFF + 1, ny + 1), :]
            + p_ref[4, a, pl.ds(OFF, ny + 1), :]
            + p_ref[4, a - 1, pl.ds(OFF, ny + 1), :]
        )
        ez = (0.25 * vy) * (0.5 * (fx_a + fx_ab)) - (0.25 * vx) * (0.5 * (fy_a + fy_m))
        ez_s[a - 1, pl.ds(0, ny + 1), :] = ez

        mfx = p_ref[0, a, pl.ds(OFF + 1, ny), :]
        mfz = p_ref[2, a, pl.ds(OFF + 1, ny), :]
        mfz_m = p_ref[2, a - 1, pl.ds(OFF + 1, ny), :]
        pvx = p_ref[3, a, pl.ds(OFF + 1, ny), :] + p_ref[3, a - 1, pl.ds(OFF + 1, ny), :]
        pvz = p_ref[5, a, pl.ds(OFF + 1, ny), :] + p_ref[5, a - 1, pl.ds(OFF + 1, ny), :]
        yfx = 0.5 * (mfx + below(mfx))
        yfz = 0.5 * (mfz + mfz_m)
        yvx = 0.25 * (pvx + below(pvx))
        yvz = 0.25 * (pvz + below(pvz))
        ey_s[a - 1] = yvx * yfz - yvz * yfx

        rfy = p_ref[1, a, pl.ds(OFF + 1, ny + 1), :]
        rfz = p_ref[2, a, pl.ds(OFF + 1, ny + 1), :]
        rfz_b = p_ref[2, a, pl.ds(OFF, ny + 1), :]
        cvy = p_ref[4, a, pl.ds(OFF + 1, ny + 1), :] + p_ref[4, a, pl.ds(OFF, ny + 1), :]
        cvz = p_ref[5, a, pl.ds(OFF + 1, ny + 1), :] + p_ref[5, a, pl.ds(OFF, ny + 1), :]
        xfy = 0.5 * (rfy + below(rfy))
        xfz = 0.5 * (rfz + rfz_b)
        xvy = 0.25 * (cvy + below(cvy))
        xvz = 0.25 * (cvz + below(cvz))
        ex_s[a - 1, pl.ds(0, ny + 1), :] = xvz * xfy - xvy * xfz
        return carry

    lax.fori_loop(1, rows + 2, emf_row, 0)

    keep = KMAX + 1

    def update_row(r, carry):
        a = r + 1
        ez_r = ez_s[r, pl.ds(0, ny), :]
        ez_r1 = ez_s[r, pl.ds(1, ny), :]
        ez_n = ez_s[r + 1, pl.ds(0, ny), :]
        ey_r = ey_s[r]
        ey_n = ey_s[r + 1]
        ex_r = ex_s[r, pl.ds(0, ny), :]
        ex_r1 = ex_s[r, pl.ds(1, ny), :]
        fx = p_ref[0, a, pl.ds(OFF + 1, ny), :]
        fy = p_ref[1, a, pl.ds(OFF + 1, ny), :]
        fz = p_ref[2, a, pl.ds(OFF + 1, ny), :]
        new = (
            fx - COURANT * ((ez_r1 - ez_r) - (above(ey_r) - ey_r)),
            fy - COURANT * ((above(ex_r) - ex_r) - (ez_n - ez_r)),
            fz - COURANT * ((ey_n - ey_r) - (ex_r1 - ex_r)),
        )
        for c in range(3):
            u_ref[c, r] = new[c]
        return carry

    lax.fori_loop(0, rows, update_row, 0)
    for c in range(3):
        for r in range(rows):
            top_ref[pl.ds((c * rows + r) * keep, keep), :] = u_ref[c, r, pl.ds(ny - keep, keep), :]


def ct_update(eshift, efrac, flags, field, velocity, xm, xp, low_in, high_in):
    _, rows, ny, nz = field.shape
    keep = KMAX + 1
    vmem = pl.BlockSpec(memory_space=pltpu.VMEM)
    smem = pl.BlockSpec(memory_space=pltpu.SMEM)
    hbm = pl.BlockSpec(memory_space=pl.ANY)
    return pl.pallas_call(
        ct_kernel,
        out_shape=(
            jax.ShapeDtypeStruct((3, rows, ny, nz), field.dtype),
            jax.ShapeDtypeStruct((3 * rows * keep, nz), field.dtype),
        ),
        in_specs=[smem, smem, smem, hbm, hbm, vmem, vmem, vmem, vmem, vmem, vmem],
        out_specs=(vmem, vmem),
        scratch_shapes=[
            pltpu.VMEM((6, rows + 2, OFF + ny + 2, nz), jnp.float32),
            pltpu.VMEM((rows + 1, ny + 8, nz), jnp.float32),
            pltpu.VMEM((rows + 1, ny, nz), jnp.float32),
            pltpu.VMEM((rows + 1, ny + 8, nz), jnp.float32),
            pltpu.VMEM((6, ny + WIDE + 8, nz), jnp.float32),
            pltpu.SemaphoreType.DMA((2,)),
        ],
        cost_estimate=pl.CostEstimate(
            flops=120 * rows * ny * nz, transcendentals=0,
            bytes_accessed=4 * (6 * rows * ny + 3 * rows * ny) * nz,
        ),
    )(eshift, efrac, flags, field, velocity, xm, xp, *low_in, *high_in)


def blend(src, o_ref, x, s, w, src_start, dst_start, count):
    for k in range(KMAX + 1):
        @pl.when(s == k)
        def _():
            near = src[:, x, pl.ds(src_start - k, count), :]
            far = src[:, x, pl.ds(src_start - k - 1, count), :]
            o_ref[:, x, pl.ds(dst_start, count), :] = (1.0 - w) * near + w * far


def local_kernel(shift_ref, frac_ref, u_ref, o_hbm, out, sem):
    rows, ny = u_ref.shape[1], u_ref.shape[2]
    keep = KMAX + 1

    def strip(x, carry):
        blend(u_ref, out, x, shift_ref[x], frac_ref[x], keep, keep, ny - keep)
        return carry

    lax.fori_loop(0, rows, strip, 0)
    put = pltpu.make_async_copy(out, o_hbm, sem.at[0])
    put.start()
    put.wait()


def advect_local(updated, strip_shift, strip_frac):
    _, rows, ny, nz = updated.shape
    vmem = pl.BlockSpec(memory_space=pltpu.VMEM)
    smem = pl.BlockSpec(memory_space=pltpu.SMEM)
    hbm = pl.BlockSpec(memory_space=pl.ANY)
    return pl.pallas_call(
        local_kernel,
        out_shape=jax.ShapeDtypeStruct(updated.shape, updated.dtype),
        in_specs=[smem, smem, vmem],
        out_specs=hbm,
        scratch_shapes=[pltpu.VMEM(updated.shape, jnp.float32), pltpu.SemaphoreType.DMA((1,))],
        cost_estimate=pl.CostEstimate(
            flops=3 * 3 * rows * ny * nz, transcendentals=0,
            bytes_accessed=4 * 3 * rows * 2 * ny * nz,
        ),
    )(strip_shift, strip_frac, updated)


def edge_kernel(shift_ref, frac_ref, u_ref, rec_hbm, part_hbm, o_hbm, flat, ext, tile, sem):
    rows = u_ref.shape[1]
    lead = 8
    keep = KMAX + 1
    fetch = pltpu.make_async_copy(rec_hbm, flat, sem.at[0])
    fetch.start()
    head = pltpu.make_async_copy(part_hbm.at[:, :, pl.ds(0, lead), :], tile, sem.at[1])
    head.start()
    ext[:, :, pl.ds(lead, lead), :] = u_ref[:, :, pl.ds(0, lead), :]
    fetch.wait()
    for c in range(3):
        for x in range(rows):
            ext[c, x, pl.ds(lead - keep, keep), :] = flat[pl.ds((c * rows + x) * keep, keep), :]
    head.wait()

    def strip(x, carry):
        blend(ext, tile, x, shift_ref[x], frac_ref[x], lead, 0, keep)
        return carry

    lax.fori_loop(0, rows, strip, 0)
    put = pltpu.make_async_copy(tile, o_hbm.at[:, :, pl.ds(0, lead), :], sem.at[2])
    put.start()
    put.wait()


def advect_edge(updated, received, partial, strip_shift, strip_frac):
    _, rows, ny, nz = updated.shape
    vmem = pl.BlockSpec(memory_space=pltpu.VMEM)
    smem = pl.BlockSpec(memory_space=pltpu.SMEM)
    hbm = pl.BlockSpec(memory_space=pl.ANY)
    return pl.pallas_call(
        edge_kernel,
        out_shape=jax.ShapeDtypeStruct(updated.shape, updated.dtype),
        in_specs=[smem, smem, vmem, hbm, hbm],
        out_specs=hbm,
        input_output_aliases={4: 0},
        scratch_shapes=[
            pltpu.VMEM(received.shape, jnp.float32),
            pltpu.VMEM((3, rows, 16, nz), jnp.float32),
            pltpu.VMEM((3, rows, 8, nz), jnp.float32),
            pltpu.SemaphoreType.DMA((3,)),
        ],
        cost_estimate=pl.CostEstimate(
            flops=9 * rows * (KMAX + 1) * nz, transcendentals=0,
            bytes_accessed=4 * 3 * rows * 3 * 8 * nz,
        ),
    )(strip_shift, strip_frac, updated, received, partial)


def body(field, velocity, strip_shift, strip_frac, edge_shift, edge_frac):
    _, nx, ny, nz = field.shape
    nb = lax.axis_size("blocks")
    b = lax.axis_index("blocks")

    xm = shifted(jnp.concatenate([field[:, nx - 1], velocity[:, nx - 1]], axis=0), 1, 0)
    xp = shifted(jnp.concatenate([field[:, 0], velocity[:, 0]], axis=0), -1, 0)
    own_low = jnp.concatenate([field[:, :, ny - 1], velocity[:, :, ny - 1]], axis=0)
    own_high = jnp.concatenate([field[:, :, 0], velocity[:, :, 0]], axis=0)
    low_ends = jnp.concatenate([xm[:, ny - WIDE :], xp[:, ny - 1 : ny]], axis=1)
    high_ends = jnp.concatenate([xp[:, :WIDE], xm[:, 0:1]], axis=1)
    from_low = shifted((low_ends, own_low), 0, 1)
    from_high = shifted((high_ends, own_high), 0, -1)
    flags = jnp.stack([b == 0, b == nb - 1]).astype(jnp.int32)
    updated, top = ct_update(edge_shift, edge_frac, flags, field, velocity, xm, xp, from_low, from_high)
    received = shifted(top, 0, 1)
    partial = advect_local(updated, strip_shift, strip_frac)
    return advect_edge(updated, received, partial, strip_shift, strip_frac)


def solution(mesh):
    placed = (
        P(None, "blocks", "phi", None),
        P(None, "blocks", "phi", None),
        P("blocks"),
        P("blocks"),
        P(),
        P(),
    )
    return jax.shard_map(
        body, mesh=mesh, in_specs=placed, out_specs=P(None, "blocks", "phi", None), check_vma=False
    )
```

```python
import jax
import jax.numpy as jnp
from jax import lax
from jax.experimental import pallas as pl
from jax.experimental.pallas import tpu as pltpu
from jax.sharding import PartitionSpec as P

KMAX = 6
COURANT = 0.4
WIDE = KMAX + 2


def shifted(x, db, dp):
    nb, nq = lax.axis_size("blocks"), lax.axis_size("phi")
    if dp == 0:
        return lax.ppermute(x, "blocks", [(b, (b + db) % nb) for b in range(nb)])
    if db == 0:
        return lax.ppermute(x, "phi", [(q, (q + dp) % nq) for q in range(nq)])
    pairs = [
        (b * nq + q, ((b + db) % nb) * nq + (q + dp) % nq)
        for b in range(nb)
        for q in range(nq)
    ]
    return lax.ppermute(x, ("blocks", "phi"), pairs)


def below(v):
    return pltpu.roll(v, 1, 1)


def above(v):
    return pltpu.roll(v, v.shape[1] - 1, 1)


OFF = 7


def edge_row(dst, line, plain, ghost_on, shift, weight, base, sign):
    span = dst.shape[1]

    @pl.when(ghost_on == 0)
    def _():
        dst[...] = plain

    for k in range(KMAX + 1):
        @pl.when(jnp.logical_and(ghost_on != 0, shift == k))
        def _():
            lead = base + sign * k
            dst[...] = (1.0 - weight) * line[:, pl.ds(lead, span), :] + weight * line[:, pl.ds(lead + sign, span), :]


def ct_kernel(eshift_ref, efrac_ref, flag_ref, f_hbm, v_hbm, xm_ref, xp_ref, lend_ref, lown_ref, hend_ref, hown_ref,
              u_ref, top_ref, p_ref, ez_s, ey_s, ex_s, line, sem):
    rows = u_ref.shape[1]
    ny = u_ref.shape[2]
    copies = [
        pltpu.make_async_copy(f_hbm, p_ref.at[0:3, 1 : rows + 1, pl.ds(OFF + 1, ny)], sem.at[0]),
        pltpu.make_async_copy(v_hbm, p_ref.at[3:6, 1 : rows + 1, pl.ds(OFF + 1, ny)], sem.at[1]),
    ]
    for c in copies:
        c.start()
    for a in range(rows):
        p_ref[:, a + 1, OFF, :] = lown_ref[:, a, :]
        p_ref[:, a + 1, OFF + ny + 1, :] = hown_ref[:, a, :]

    line[:, pl.ds(0, WIDE), :] = lend_ref[:, pl.ds(0, WIDE), :]
    line[:, pl.ds(WIDE, ny), :] = xm_ref[...]
    line[:, WIDE + ny, :] = hend_ref[:, WIDE, :]
    low_plain = line[:, pl.ds(WIDE - 1, ny + 2), :]
    edge_row(p_ref.at[:, 0, pl.ds(OFF, ny + 2)], line, low_plain, flag_ref[0],
             eshift_ref[0], efrac_ref[0], WIDE - 1, -1)

    line[:, 0, :] = lend_ref[:, WIDE, :]
    line[:, pl.ds(1, ny), :] = xp_ref[...]
    line[:, pl.ds(ny + 1, WIDE), :] = hend_ref[:, pl.ds(0, WIDE), :]
    high_plain = line[:, pl.ds(0, ny + 2), :]
    edge_row(p_ref.at[:, rows + 1, pl.ds(OFF, ny + 2)], line, high_plain, flag_ref[1],
             eshift_ref[1], efrac_ref[1], 0, 1)
    for c in copies:
        c.wait()

    def emf_row(a, carry):
        fx_a = p_ref[0, a, pl.ds(OFF + 1, ny + 1), :]
        fx_ab = p_ref[0, a, pl.ds(OFF, ny + 1), :]
        fy_a = p_ref[1, a, pl.ds(OFF + 1, ny + 1), :]
        fy_m = p_ref[1, a - 1, pl.ds(OFF + 1, ny + 1), :]
        vx = (
            p_ref[3, a, pl.ds(OFF + 1, ny + 1), :]
            + p_ref[3, a - 1, pl.ds(OFF + 1, ny + 1), :]
            + p_ref[3, a, pl.ds(OFF, ny + 1), :]
            + p_ref[3, a - 1, pl.ds(OFF, ny + 1), :]
        )
        vy = (
            p_ref[4, a, pl.ds(OFF + 1, ny + 1), :]
            + p_ref[4, a - 1, pl.ds(OFF + 1, ny + 1), :]
            + p_ref[4, a, pl.ds(OFF, ny + 1), :]
            + p_ref[4, a - 1, pl.ds(OFF, ny + 1), :]
        )
        ez = (0.25 * vy) * (0.5 * (fx_a + fx_ab)) - (0.25 * vx) * (0.5 * (fy_a + fy_m))
        ez_s[a - 1, pl.ds(0, ny + 1), :] = ez

        mfx = p_ref[0, a, pl.ds(OFF + 1, ny), :]
        mfz = p_ref[2, a, pl.ds(OFF + 1, ny), :]
        mfz_m = p_ref[2, a - 1, pl.ds(OFF + 1, ny), :]
        pvx = p_ref[3, a, pl.ds(OFF + 1, ny), :] + p_ref[3, a - 1, pl.ds(OFF + 1, ny), :]
        pvz = p_ref[5, a, pl.ds(OFF + 1, ny), :] + p_ref[5, a - 1, pl.ds(OFF + 1, ny), :]
        yfx = 0.5 * (mfx + below(mfx))
        yfz = 0.5 * (mfz + mfz_m)
        yvx = 0.25 * (pvx + below(pvx))
        yvz = 0.25 * (pvz + below(pvz))
        ey_s[a - 1] = yvx * yfz - yvz * yfx

        rfy = p_ref[1, a, pl.ds(OFF + 1, ny + 1), :]
        rfz = p_ref[2, a, pl.ds(OFF + 1, ny + 1), :]
        rfz_b = p_ref[2, a, pl.ds(OFF, ny + 1), :]
        cvy = p_ref[4, a, pl.ds(OFF + 1, ny + 1), :] + p_ref[4, a, pl.ds(OFF, ny + 1), :]
        cvz = p_ref[5, a, pl.ds(OFF + 1, ny + 1), :] + p_ref[5, a, pl.ds(OFF, ny + 1), :]
        xfy = 0.5 * (rfy + below(rfy))
        xfz = 0.5 * (rfz + rfz_b)
        xvy = 0.25 * (cvy + below(cvy))
        xvz = 0.25 * (cvz + below(cvz))
        ex_s[a - 1, pl.ds(0, ny + 1), :] = xvz * xfy - xvy * xfz
        return carry

    lax.fori_loop(1, rows + 2, emf_row, 0)

    keep = KMAX + 1

    def update_row(r, carry):
        a = r + 1
        ez_r = ez_s[r, pl.ds(0, ny), :]
        ez_r1 = ez_s[r, pl.ds(1, ny), :]
        ez_n = ez_s[r + 1, pl.ds(0, ny), :]
        ey_r = ey_s[r]
        ey_n = ey_s[r + 1]
        ex_r = ex_s[r, pl.ds(0, ny), :]
        ex_r1 = ex_s[r, pl.ds(1, ny), :]
        fx = p_ref[0, a, pl.ds(OFF + 1, ny), :]
        fy = p_ref[1, a, pl.ds(OFF + 1, ny), :]
        fz = p_ref[2, a, pl.ds(OFF + 1, ny), :]
        new = (
            fx - COURANT * ((ez_r1 - ez_r) - (above(ey_r) - ey_r)),
            fy - COURANT * ((above(ex_r) - ex_r) - (ez_n - ez_r)),
            fz - COURANT * ((ey_n - ey_r) - (ex_r1 - ex_r)),
        )
        for c in range(3):
            u_ref[c, r] = new[c]
        return carry

    lax.fori_loop(0, rows, update_row, 0)
    for c in range(3):
        for r in range(rows):
            top_ref[pl.ds((c * rows + r) * keep, keep), :] = u_ref[c, r, pl.ds(ny - keep, keep), :]


def ct_update(eshift, efrac, flags, field, velocity, xm, xp, low_in, high_in):
    _, rows, ny, nz = field.shape
    keep = KMAX + 1
    vmem = pl.BlockSpec(memory_space=pltpu.VMEM)
    smem = pl.BlockSpec(memory_space=pltpu.SMEM)
    hbm = pl.BlockSpec(memory_space=pl.ANY)
    return pl.pallas_call(
        ct_kernel,
        out_shape=(
            jax.ShapeDtypeStruct((3, rows, ny, nz), field.dtype),
            jax.ShapeDtypeStruct((3 * rows * keep, nz), field.dtype),
        ),
        in_specs=[smem, smem, smem, hbm, hbm, vmem, vmem, vmem, vmem, vmem, vmem],
        out_specs=(vmem, vmem),
        scratch_shapes=[
            pltpu.VMEM((6, rows + 2, OFF + ny + 2, nz), jnp.float32),
            pltpu.VMEM((rows + 1, ny + 8, nz), jnp.float32),
            pltpu.VMEM((rows + 1, ny, nz), jnp.float32),
            pltpu.VMEM((rows + 1, ny + 8, nz), jnp.float32),
            pltpu.VMEM((6, ny + WIDE + 8, nz), jnp.float32),
            pltpu.SemaphoreType.DMA((2,)),
        ],
        cost_estimate=pl.CostEstimate(
            flops=120 * rows * ny * nz, transcendentals=0,
            bytes_accessed=4 * (6 * rows * ny + 3 * rows * ny) * nz,
        ),
    )(eshift, efrac, flags, field, velocity, xm, xp, *low_in, *high_in)


def blend(src, o_ref, x, s, w, src_start, dst_start, count):
    for k in range(KMAX + 1):
        @pl.when(s == k)
        def _():
            near = src[:, x, pl.ds(src_start - k, count), :]
            far = src[:, x, pl.ds(src_start - k - 1, count), :]
            o_ref[:, x, pl.ds(dst_start, count), :] = (1.0 - w) * near + w * far


def local_kernel(shift_ref, frac_ref, u_ref, o_hbm, out, sem):
    rows, ny = u_ref.shape[1], u_ref.shape[2]
    keep = KMAX + 1

    def strip(x, carry):
        blend(u_ref, out, x, shift_ref[x], frac_ref[x], keep, keep, ny - keep)
        return carry

    lax.fori_loop(0, rows, strip, 0)
    put = pltpu.make_async_copy(out, o_hbm, sem.at[0])
    put.start()
    put.wait()


def advect_local(updated, strip_shift, strip_frac):
    _, rows, ny, nz = updated.shape
    vmem = pl.BlockSpec(memory_space=pltpu.VMEM)
    smem = pl.BlockSpec(memory_space=pltpu.SMEM)
    hbm = pl.BlockSpec(memory_space=pl.ANY)
    return pl.pallas_call(
        local_kernel,
        out_shape=jax.ShapeDtypeStruct(updated.shape, updated.dtype),
        in_specs=[smem, smem, vmem],
        out_specs=hbm,
        scratch_shapes=[pltpu.VMEM(updated.shape, jnp.float32), pltpu.SemaphoreType.DMA((1,))],
        cost_estimate=pl.CostEstimate(
            flops=3 * 3 * rows * ny * nz, transcendentals=0,
            bytes_accessed=4 * 3 * rows * 2 * ny * nz,
        ),
    )(strip_shift, strip_frac, updated)


def edge_kernel(shift_ref, frac_ref, u_hbm, rec_hbm, part_hbm, o_hbm, flat, ext, tile, sem):
    rows = u_hbm.shape[1]
    lead = 8
    keep = KMAX + 1
    fetch = pltpu.make_async_copy(rec_hbm, flat, sem.at[0])
    fetch.start()
    head = pltpu.make_async_copy(part_hbm.at[:, :, pl.ds(0, lead), :], tile, sem.at[1])
    head.start()
    low = pltpu.make_async_copy(u_hbm.at[:, :, pl.ds(0, lead), :], ext.at[:, :, pl.ds(lead, lead), :], sem.at[3])
    low.start()
    fetch.wait()
    for c in range(3):
        for x in range(rows):
            ext[c, x, pl.ds(lead - keep, keep), :] = flat[pl.ds((c * rows + x) * keep, keep), :]
    head.wait()
    low.wait()

    def strip(x, carry):
        blend(ext, tile, x, shift_ref[x], frac_ref[x], lead, 0, keep)
        return carry

    lax.fori_loop(0, rows, strip, 0)
    put = pltpu.make_async_copy(tile, o_hbm.at[:, :, pl.ds(0, lead), :], sem.at[2])
    put.start()
    put.wait()


def advect_edge(updated, received, partial, strip_shift, strip_frac):
    _, rows, ny, nz = updated.shape
    vmem = pl.BlockSpec(memory_space=pltpu.VMEM)
    smem = pl.BlockSpec(memory_space=pltpu.SMEM)
    hbm = pl.BlockSpec(memory_space=pl.ANY)
    return pl.pallas_call(
        edge_kernel,
        out_shape=jax.ShapeDtypeStruct(updated.shape, updated.dtype),
        in_specs=[smem, smem, hbm, hbm, hbm],
        out_specs=hbm,
        input_output_aliases={4: 0},
        scratch_shapes=[
            pltpu.VMEM(received.shape, jnp.float32),
            pltpu.VMEM((3, rows, 16, nz), jnp.float32),
            pltpu.VMEM((3, rows, 8, nz), jnp.float32),
            pltpu.SemaphoreType.DMA((4,)),
        ],
        cost_estimate=pl.CostEstimate(
            flops=9 * rows * (KMAX + 1) * nz, transcendentals=0,
            bytes_accessed=4 * 3 * rows * 3 * 8 * nz,
        ),
    )(strip_shift, strip_frac, updated, received, partial)


def body(field, velocity, strip_shift, strip_frac, edge_shift, edge_frac):
    _, nx, ny, nz = field.shape
    nb = lax.axis_size("blocks")
    b = lax.axis_index("blocks")

    xm = shifted(jnp.concatenate([field[:, nx - 1], velocity[:, nx - 1]], axis=0), 1, 0)
    xp = shifted(jnp.concatenate([field[:, 0], velocity[:, 0]], axis=0), -1, 0)
    own_low = jnp.concatenate([field[:, :, ny - 1], velocity[:, :, ny - 1]], axis=0)
    own_high = jnp.concatenate([field[:, :, 0], velocity[:, :, 0]], axis=0)
    low_ends = jnp.concatenate([xm[:, ny - WIDE :], xp[:, ny - 1 : ny]], axis=1)
    high_ends = jnp.concatenate([xp[:, :WIDE], xm[:, 0:1]], axis=1)
    from_low = shifted((low_ends, own_low), 0, 1)
    from_high = shifted((high_ends, own_high), 0, -1)
    flags = jnp.stack([b == 0, b == nb - 1]).astype(jnp.int32)
    updated, top = ct_update(edge_shift, edge_frac, flags, field, velocity, xm, xp, from_low, from_high)
    received = shifted(top, 0, 1)
    partial = advect_local(updated, strip_shift, strip_frac)
    return advect_edge(updated, received, partial, strip_shift, strip_frac)


def solution(mesh):
    placed = (
        P(None, "blocks", "phi", None),
        P(None, "blocks", "phi", None),
        P("blocks"),
        P("blocks"),
        P(),
        P(),
    )
    return jax.shard_map(
        body, mesh=mesh, in_specs=placed, out_specs=P(None, "blocks", "phi", None), check_vma=False
    )
```

```python
import jax
import jax.numpy as jnp
from jax import lax
from jax.experimental import pallas as pl
from jax.experimental.pallas import tpu as pltpu
from jax.sharding import PartitionSpec as P

KMAX = 6
COURANT = 0.4
WIDE = KMAX + 2


def shifted(x, db, dp):
    nb, nq = lax.axis_size("blocks"), lax.axis_size("phi")
    if dp == 0:
        return lax.ppermute(x, "blocks", [(b, (b + db) % nb) for b in range(nb)])
    if db == 0:
        return lax.ppermute(x, "phi", [(q, (q + dp) % nq) for q in range(nq)])
    pairs = [
        (b * nq + q, ((b + db) % nb) * nq + (q + dp) % nq)
        for b in range(nb)
        for q in range(nq)
    ]
    return lax.ppermute(x, ("blocks", "phi"), pairs)


def below(v):
    return pltpu.roll(v, 1, 1)


def above(v):
    return pltpu.roll(v, v.shape[1] - 1, 1)


OFF = 7


def edge_row(dst, line, plain, ghost_on, shift, weight, base, sign):
    span = dst.shape[1]

    @pl.when(ghost_on == 0)
    def _():
        dst[...] = plain

    for k in range(KMAX + 1):
        @pl.when(jnp.logical_and(ghost_on != 0, shift == k))
        def _():
            lead = base + sign * k
            dst[...] = (1.0 - weight) * line[:, pl.ds(lead, span), :] + weight * line[:, pl.ds(lead + sign, span), :]


def ct_kernel(eshift_ref, efrac_ref, flag_ref, f_hbm, v_hbm, xm_ref, xp_ref, lend_ref, lown_ref, hend_ref, hown_ref,
              u_ref, top_ref, p_ref, ez_s, ey_s, ex_s, line, sem):
    rows = u_ref.shape[1]
    ny = u_ref.shape[2]
    copies = [
        pltpu.make_async_copy(f_hbm, p_ref.at[0:3, 1 : rows + 1, pl.ds(OFF + 1, ny)], sem.at[0]),
        pltpu.make_async_copy(v_hbm, p_ref.at[3:6, 1 : rows + 1, pl.ds(OFF + 1, ny)], sem.at[1]),
    ]
    for c in copies:
        c.start()
    for a in range(rows):
        p_ref[:, a + 1, OFF, :] = lown_ref[:, a, :]
        p_ref[:, a + 1, OFF + ny + 1, :] = hown_ref[:, a, :]

    line[:, pl.ds(0, WIDE), :] = lend_ref[:, pl.ds(0, WIDE), :]
    line[:, pl.ds(WIDE, ny), :] = xm_ref[...]
    line[:, WIDE + ny, :] = hend_ref[:, WIDE, :]
    low_plain = line[:, pl.ds(WIDE - 1, ny + 2), :]
    edge_row(p_ref.at[:, 0, pl.ds(OFF, ny + 2)], line, low_plain, flag_ref[0],
             eshift_ref[0], efrac_ref[0], WIDE - 1, -1)

    line[:, 0, :] = lend_ref[:, WIDE, :]
    line[:, pl.ds(1, ny), :] = xp_ref[...]
    line[:, pl.ds(ny + 1, WIDE), :] = hend_ref[:, pl.ds(0, WIDE), :]
    high_plain = line[:, pl.ds(0, ny + 2), :]
    edge_row(p_ref.at[:, rows + 1, pl.ds(OFF, ny + 2)], line, high_plain, flag_ref[1],
             eshift_ref[1], efrac_ref[1], 0, 1)
    for c in copies:
        c.wait()

    def emf_row(a, carry):
        fx_a = p_ref[0, a, pl.ds(OFF + 1, ny + 1), :]
        fx_ab = p_ref[0, a, pl.ds(OFF, ny + 1), :]
        fy_a = p_ref[1, a, pl.ds(OFF + 1, ny + 1), :]
        fy_m = p_ref[1, a - 1, pl.ds(OFF + 1, ny + 1), :]
        vx = (
            p_ref[3, a, pl.ds(OFF + 1, ny + 1), :]
            + p_ref[3, a - 1, pl.ds(OFF + 1, ny + 1), :]
            + p_ref[3, a, pl.ds(OFF, ny + 1), :]
            + p_ref[3, a - 1, pl.ds(OFF, ny + 1), :]
        )
        vy = (
            p_ref[4, a, pl.ds(OFF + 1, ny + 1), :]
            + p_ref[4, a - 1, pl.ds(OFF + 1, ny + 1), :]
            + p_ref[4, a, pl.ds(OFF, ny + 1), :]
            + p_ref[4, a - 1, pl.ds(OFF, ny + 1), :]
        )
        ez = (0.25 * vy) * (0.5 * (fx_a + fx_ab)) - (0.25 * vx) * (0.5 * (fy_a + fy_m))
        ez_s[a - 1, pl.ds(0, ny + 1), :] = ez

        mfx = p_ref[0, a, pl.ds(OFF + 1, ny), :]
        mfz = p_ref[2, a, pl.ds(OFF + 1, ny), :]
        mfz_m = p_ref[2, a - 1, pl.ds(OFF + 1, ny), :]
        pvx = p_ref[3, a, pl.ds(OFF + 1, ny), :] + p_ref[3, a - 1, pl.ds(OFF + 1, ny), :]
        pvz = p_ref[5, a, pl.ds(OFF + 1, ny), :] + p_ref[5, a - 1, pl.ds(OFF + 1, ny), :]
        yfx = 0.5 * (mfx + below(mfx))
        yfz = 0.5 * (mfz + mfz_m)
        yvx = 0.25 * (pvx + below(pvx))
        yvz = 0.25 * (pvz + below(pvz))
        ey_s[a - 1] = yvx * yfz - yvz * yfx

        rfy = p_ref[1, a, pl.ds(OFF + 1, ny + 1), :]
        rfz = p_ref[2, a, pl.ds(OFF + 1, ny + 1), :]
        rfz_b = p_ref[2, a, pl.ds(OFF, ny + 1), :]
        cvy = p_ref[4, a, pl.ds(OFF + 1, ny + 1), :] + p_ref[4, a, pl.ds(OFF, ny + 1), :]
        cvz = p_ref[5, a, pl.ds(OFF + 1, ny + 1), :] + p_ref[5, a, pl.ds(OFF, ny + 1), :]
        xfy = 0.5 * (rfy + below(rfy))
        xfz = 0.5 * (rfz + rfz_b)
        xvy = 0.25 * (cvy + below(cvy))
        xvz = 0.25 * (cvz + below(cvz))
        ex_s[a - 1, pl.ds(0, ny + 1), :] = xvz * xfy - xvy * xfz
        return carry

    lax.fori_loop(1, rows + 2, emf_row, 0)

    keep = KMAX + 1

    def update_row(r, carry):
        a = r + 1
        ez_r = ez_s[r, pl.ds(0, ny), :]
        ez_r1 = ez_s[r, pl.ds(1, ny), :]
        ez_n = ez_s[r + 1, pl.ds(0, ny), :]
        ey_r = ey_s[r]
        ey_n = ey_s[r + 1]
        ex_r = ex_s[r, pl.ds(0, ny), :]
        ex_r1 = ex_s[r, pl.ds(1, ny), :]
        fx = p_ref[0, a, pl.ds(OFF + 1, ny), :]
        fy = p_ref[1, a, pl.ds(OFF + 1, ny), :]
        fz = p_ref[2, a, pl.ds(OFF + 1, ny), :]
        new = (
            fx - COURANT * ((ez_r1 - ez_r) - (above(ey_r) - ey_r)),
            fy - COURANT * ((above(ex_r) - ex_r) - (ez_n - ez_r)),
            fz - COURANT * ((ey_n - ey_r) - (ex_r1 - ex_r)),
        )
        for c in range(3):
            u_ref[c, r] = new[c]
        return carry

    lax.fori_loop(0, rows, update_row, 0)
    for c in range(3):
        for r in range(rows):
            top_ref[pl.ds((c * rows + r) * keep, keep), :] = u_ref[c, r, pl.ds(ny - keep, keep), :]


def ct_update(eshift, efrac, flags, field, velocity, xm, xp, low_in, high_in):
    _, rows, ny, nz = field.shape
    keep = KMAX + 1
    vmem = pl.BlockSpec(memory_space=pltpu.VMEM)
    smem = pl.BlockSpec(memory_space=pltpu.SMEM)
    hbm = pl.BlockSpec(memory_space=pl.ANY)
    return pl.pallas_call(
        ct_kernel,
        out_shape=(
            jax.ShapeDtypeStruct((3, rows, ny, nz), field.dtype),
            jax.ShapeDtypeStruct((3 * rows * keep, nz), field.dtype),
        ),
        in_specs=[smem, smem, smem, hbm, hbm, vmem, vmem, vmem, vmem, vmem, vmem],
        out_specs=(vmem, vmem),
        scratch_shapes=[
            pltpu.VMEM((6, rows + 2, OFF + ny + 2, nz), jnp.float32),
            pltpu.VMEM((rows + 1, ny + 8, nz), jnp.float32),
            pltpu.VMEM((rows + 1, ny, nz), jnp.float32),
            pltpu.VMEM((rows + 1, ny + 8, nz), jnp.float32),
            pltpu.VMEM((6, ny + WIDE + 8, nz), jnp.float32),
            pltpu.SemaphoreType.DMA((2,)),
        ],
        cost_estimate=pl.CostEstimate(
            flops=120 * rows * ny * nz, transcendentals=0,
            bytes_accessed=4 * (6 * rows * ny + 3 * rows * ny) * nz,
        ),
    )(eshift, efrac, flags, field, velocity, xm, xp, *low_in, *high_in)


def advect_kernel(shift_ref, frac_ref, u_ref, rec_ref, o_ref, ext):
    rows, ny = u_ref.shape[1], u_ref.shape[2]
    lead = 8
    keep = KMAX + 1
    for c in range(3):
        for x in range(rows):
            ext[c, x, pl.ds(lead - keep, keep), :] = rec_ref[pl.ds((c * rows + x) * keep, keep), :]
    ext[:, :, pl.ds(lead, ny), :] = u_ref[...]

    def strip(x, carry):
        s = shift_ref[x]
        w = frac_ref[x]
        for k in range(KMAX + 1):
            @pl.when(s == k)
            def _():
                near = ext[:, x, pl.ds(lead - k, ny), :]
                far = ext[:, x, pl.ds(lead - k - 1, ny), :]
                o_ref[:, x] = (1.0 - w) * near + w * far
        return carry

    lax.fori_loop(0, rows, strip, 0)


def advect(updated, received, strip_shift, strip_frac):
    _, rows, ny, nz = updated.shape
    vmem = pl.BlockSpec(memory_space=pltpu.VMEM)
    smem = pl.BlockSpec(memory_space=pltpu.SMEM)
    return pl.pallas_call(
        advect_kernel,
        out_shape=jax.ShapeDtypeStruct(updated.shape, updated.dtype),
        in_specs=[smem, smem, vmem, vmem],
        out_specs=vmem,
        scratch_shapes=[pltpu.VMEM((3, rows, ny + 8, nz), jnp.float32)],
        cost_estimate=pl.CostEstimate(
            flops=3 * 3 * rows * ny * nz, transcendentals=0,
            bytes_accessed=4 * 3 * rows * (2 * ny + KMAX + 1) * nz,
        ),
    )(strip_shift, strip_frac, updated, received)


def body(field, velocity, strip_shift, strip_frac, edge_shift, edge_frac):
    _, nx, ny, nz = field.shape
    nb = lax.axis_size("blocks")
    b = lax.axis_index("blocks")

    xm = shifted(jnp.concatenate([field[1:, nx - 1], velocity[:, nx - 1]], axis=0), 1, 0)
    xm = jnp.concatenate([jnp.zeros_like(xm[:1]), xm], axis=0)
    xp = shifted(jnp.concatenate([field[:, 0], velocity[:, 0]], axis=0), -1, 0)
    own_low = jnp.concatenate([field[:, :, ny - 1], velocity[:, :, ny - 1]], axis=0)
    own_high = jnp.concatenate([field[:, :, 0], velocity[:, :, 0]], axis=0)
    low_ends = jnp.concatenate([xm[:, ny - WIDE :], xp[:, ny - 1 : ny]], axis=1)
    high_ends = jnp.concatenate([xp[:, :WIDE], xm[:, 0:1]], axis=1)
    from_low = shifted((low_ends, own_low), 0, 1)
    from_high = shifted((high_ends, own_high), 0, -1)
    flags = jnp.stack([b == 0, b == nb - 1]).astype(jnp.int32)
    updated, top = ct_update(edge_shift, edge_frac, flags, field, velocity, xm, xp, from_low, from_high)
    received = shifted(top, 0, 1)
    return advect(updated, received, strip_shift, strip_frac)


def solution(mesh):
    placed = (
        P(None, "blocks", "phi", None),
        P(None, "blocks", "phi", None),
        P("blocks"),
        P("blocks"),
        P(),
        P(),
    )
    return jax.shard_map(
        body, mesh=mesh, in_specs=placed, out_specs=P(None, "blocks", "phi", None), check_vma=False
    )
```

```python
import jax
import jax.numpy as jnp
from jax import lax
from jax.experimental import pallas as pl
from jax.experimental.pallas import tpu as pltpu
from jax.sharding import PartitionSpec as P

KMAX = 6
COURANT = 0.4
WIDE = KMAX + 2


def shifted(x, db, dp):
    nb, nq = lax.axis_size("blocks"), lax.axis_size("phi")
    if dp == 0:
        return lax.ppermute(x, "blocks", [(b, (b + db) % nb) for b in range(nb)])
    if db == 0:
        return lax.ppermute(x, "phi", [(q, (q + dp) % nq) for q in range(nq)])
    pairs = [
        (b * nq + q, ((b + db) % nb) * nq + (q + dp) % nq)
        for b in range(nb)
        for q in range(nq)
    ]
    return lax.ppermute(x, ("blocks", "phi"), pairs)


def below(v):
    return pltpu.roll(v, 1, 1)


def above(v):
    return pltpu.roll(v, v.shape[1] - 1, 1)


OFF = 7


def edge_row(dst, line, plain, ghost_on, shift, weight, base, sign):
    span = dst.shape[1]

    @pl.when(ghost_on == 0)
    def _():
        dst[...] = plain

    for k in range(KMAX + 1):
        @pl.when(jnp.logical_and(ghost_on != 0, shift == k))
        def _():
            lead = base + sign * k
            dst[...] = (1.0 - weight) * line[:, pl.ds(lead, span), :] + weight * line[:, pl.ds(lead + sign, span), :]


def ct_kernel(eshift_ref, efrac_ref, flag_ref, f_hbm, v_hbm, xm_ref, xp_ref, lend_ref, lown_ref, hend_ref, hown_ref,
              u_ref, top_ref, p_ref, ez_s, ey_s, ex_s, line, sem):
    rows = u_ref.shape[1]
    ny = u_ref.shape[2]
    copies = [
        pltpu.make_async_copy(f_hbm, p_ref.at[0:3, 1 : rows + 1, pl.ds(OFF + 1, ny)], sem.at[0]),
        pltpu.make_async_copy(v_hbm, p_ref.at[3:6, 1 : rows + 1, pl.ds(OFF + 1, ny)], sem.at[1]),
    ]
    for a in range(rows):
        copies.append(pltpu.make_async_copy(
            lown_ref.at[:, pl.ds(a, 1), :], p_ref.at[:, a + 1, pl.ds(OFF, 1), :], sem.at[2 + 2 * a]))
        copies.append(pltpu.make_async_copy(
            hown_ref.at[:, pl.ds(a, 1), :], p_ref.at[:, a + 1, pl.ds(OFF + ny + 1, 1), :], sem.at[3 + 2 * a]))
    for c in copies:
        c.start()

    line[:, pl.ds(0, WIDE), :] = lend_ref[:, pl.ds(0, WIDE), :]
    line[:, pl.ds(WIDE, ny), :] = xm_ref[...]
    line[:, WIDE + ny, :] = hend_ref[:, WIDE, :]
    low_plain = line[:, pl.ds(WIDE - 1, ny + 2), :]
    edge_row(p_ref.at[:, 0, pl.ds(OFF, ny + 2)], line, low_plain, flag_ref[0],
             eshift_ref[0], efrac_ref[0], WIDE - 1, -1)

    line[:, 0, :] = lend_ref[:, WIDE, :]
    line[:, pl.ds(1, ny), :] = xp_ref[...]
    line[:, pl.ds(ny + 1, WIDE), :] = hend_ref[:, pl.ds(0, WIDE), :]
    high_plain = line[:, pl.ds(0, ny + 2), :]
    edge_row(p_ref.at[:, rows + 1, pl.ds(OFF, ny + 2)], line, high_plain, flag_ref[1],
             eshift_ref[1], efrac_ref[1], 0, 1)
    for c in copies:
        c.wait()

    def emf_row(a, carry):
        fx_a = p_ref[0, a, pl.ds(OFF + 1, ny + 1), :]
        fx_ab = p_ref[0, a, pl.ds(OFF, ny + 1), :]
        fy_a = p_ref[1, a, pl.ds(OFF + 1, ny + 1), :]
        fy_m = p_ref[1, a - 1, pl.ds(OFF + 1, ny + 1), :]
        vx = (
            p_ref[3, a, pl.ds(OFF + 1, ny + 1), :]
            + p_ref[3, a - 1, pl.ds(OFF + 1, ny + 1), :]
            + p_ref[3, a, pl.ds(OFF, ny + 1), :]
            + p_ref[3, a - 1, pl.ds(OFF, ny + 1), :]
        )
        vy = (
            p_ref[4, a, pl.ds(OFF + 1, ny + 1), :]
            + p_ref[4, a - 1, pl.ds(OFF + 1, ny + 1), :]
            + p_ref[4, a, pl.ds(OFF, ny + 1), :]
            + p_ref[4, a - 1, pl.ds(OFF, ny + 1), :]
        )
        ez = (0.25 * vy) * (0.5 * (fx_a + fx_ab)) - (0.25 * vx) * (0.5 * (fy_a + fy_m))
        ez_s[a - 1, pl.ds(0, ny + 1), :] = ez

        mfx = p_ref[0, a, pl.ds(OFF + 1, ny), :]
        mfz = p_ref[2, a, pl.ds(OFF + 1, ny), :]
        mfz_m = p_ref[2, a - 1, pl.ds(OFF + 1, ny), :]
        pvx = p_ref[3, a, pl.ds(OFF + 1, ny), :] + p_ref[3, a - 1, pl.ds(OFF + 1, ny), :]
        pvz = p_ref[5, a, pl.ds(OFF + 1, ny), :] + p_ref[5, a - 1, pl.ds(OFF + 1, ny), :]
        yfx = 0.5 * (mfx + below(mfx))
        yfz = 0.5 * (mfz + mfz_m)
        yvx = 0.25 * (pvx + below(pvx))
        yvz = 0.25 * (pvz + below(pvz))
        ey_s[a - 1] = yvx * yfz - yvz * yfx

        rfy = p_ref[1, a, pl.ds(OFF + 1, ny + 1), :]
        rfz = p_ref[2, a, pl.ds(OFF + 1, ny + 1), :]
        rfz_b = p_ref[2, a, pl.ds(OFF, ny + 1), :]
        cvy = p_ref[4, a, pl.ds(OFF + 1, ny + 1), :] + p_ref[4, a, pl.ds(OFF, ny + 1), :]
        cvz = p_ref[5, a, pl.ds(OFF + 1, ny + 1), :] + p_ref[5, a, pl.ds(OFF, ny + 1), :]
        xfy = 0.5 * (rfy + below(rfy))
        xfz = 0.5 * (rfz + rfz_b)
        xvy = 0.25 * (cvy + below(cvy))
        xvz = 0.25 * (cvz + below(cvz))
        ex_s[a - 1, pl.ds(0, ny + 1), :] = xvz * xfy - xvy * xfz
        return carry

    lax.fori_loop(1, rows + 2, emf_row, 0)

    keep = KMAX + 1

    def update_row(r, carry):
        a = r + 1
        ez_r = ez_s[r, pl.ds(0, ny), :]
        ez_r1 = ez_s[r, pl.ds(1, ny), :]
        ez_n = ez_s[r + 1, pl.ds(0, ny), :]
        ey_r = ey_s[r]
        ey_n = ey_s[r + 1]
        ex_r = ex_s[r, pl.ds(0, ny), :]
        ex_r1 = ex_s[r, pl.ds(1, ny), :]
        fx = p_ref[0, a, pl.ds(OFF + 1, ny), :]
        fy = p_ref[1, a, pl.ds(OFF + 1, ny), :]
        fz = p_ref[2, a, pl.ds(OFF + 1, ny), :]
        new = (
            fx - COURANT * ((ez_r1 - ez_r) - (above(ey_r) - ey_r)),
            fy - COURANT * ((above(ex_r) - ex_r) - (ez_n - ez_r)),
            fz - COURANT * ((ey_n - ey_r) - (ex_r1 - ex_r)),
        )
        for c in range(3):
            u_ref[c, r] = new[c]
        return carry

    lax.fori_loop(0, rows, update_row, 0)
    for c in range(3):
        for r in range(rows):
            top_ref[pl.ds((c * rows + r) * keep, keep), :] = u_ref[c, r, pl.ds(ny - keep, keep), :]


def ct_update(eshift, efrac, flags, field, velocity, xm, xp, low_in, high_in):
    _, rows, ny, nz = field.shape
    keep = KMAX + 1
    vmem = pl.BlockSpec(memory_space=pltpu.VMEM)
    smem = pl.BlockSpec(memory_space=pltpu.SMEM)
    hbm = pl.BlockSpec(memory_space=pl.ANY)
    return pl.pallas_call(
        ct_kernel,
        out_shape=(
            jax.ShapeDtypeStruct((3, rows, ny, nz), field.dtype),
            jax.ShapeDtypeStruct((3 * rows * keep, nz), field.dtype),
        ),
        in_specs=[smem, smem, smem, hbm, hbm, vmem, vmem, vmem, vmem, vmem, vmem],
        out_specs=(vmem, vmem),
        scratch_shapes=[
            pltpu.VMEM((6, rows + 2, OFF + ny + 2, nz), jnp.float32),
            pltpu.VMEM((rows + 1, ny + 8, nz), jnp.float32),
            pltpu.VMEM((rows + 1, ny, nz), jnp.float32),
            pltpu.VMEM((rows + 1, ny + 8, nz), jnp.float32),
            pltpu.VMEM((6, ny + WIDE + 8, nz), jnp.float32),
            pltpu.SemaphoreType.DMA((2 + 2 * rows,)),
        ],
        cost_estimate=pl.CostEstimate(
            flops=120 * rows * ny * nz, transcendentals=0,
            bytes_accessed=4 * (6 * rows * ny + 3 * rows * ny) * nz,
        ),
    )(eshift, efrac, flags, field, velocity, xm, xp, *low_in, *high_in)


def advect_kernel(shift_ref, frac_ref, u_ref, rec_ref, o_ref, ext):
    rows, ny = u_ref.shape[1], u_ref.shape[2]
    lead = 8
    keep = KMAX + 1
    for c in range(3):
        for x in range(rows):
            ext[c, x, pl.ds(lead - keep, keep), :] = rec_ref[pl.ds((c * rows + x) * keep, keep), :]
    ext[:, :, pl.ds(lead, ny), :] = u_ref[...]

    def strip(x, carry):
        s = shift_ref[x]
        w = frac_ref[x]
        for k in range(KMAX + 1):
            @pl.when(s == k)
            def _():
                near = ext[:, x, pl.ds(lead - k, ny), :]
                far = ext[:, x, pl.ds(lead - k - 1, ny), :]
                o_ref[:, x] = (1.0 - w) * near + w * far
        return carry

    lax.fori_loop(0, rows, strip, 0)


def advect(updated, received, strip_shift, strip_frac):
    _, rows, ny, nz = updated.shape
    vmem = pl.BlockSpec(memory_space=pltpu.VMEM)
    smem = pl.BlockSpec(memory_space=pltpu.SMEM)
    return pl.pallas_call(
        advect_kernel,
        out_shape=jax.ShapeDtypeStruct(updated.shape, updated.dtype),
        in_specs=[smem, smem, vmem, vmem],
        out_specs=vmem,
        scratch_shapes=[pltpu.VMEM((3, rows, ny + 8, nz), jnp.float32)],
        cost_estimate=pl.CostEstimate(
            flops=3 * 3 * rows * ny * nz, transcendentals=0,
            bytes_accessed=4 * 3 * rows * (2 * ny + KMAX + 1) * nz,
        ),
    )(strip_shift, strip_frac, updated, received)


def body(field, velocity, strip_shift, strip_frac, edge_shift, edge_frac):
    _, nx, ny, nz = field.shape
    nb = lax.axis_size("blocks")
    b = lax.axis_index("blocks")

    xm = shifted(jnp.concatenate([field[:, nx - 1], velocity[:, nx - 1]], axis=0), 1, 0)
    xp = shifted(jnp.concatenate([field[:, 0], velocity[:, 0]], axis=0), -1, 0)
    own_low = jnp.concatenate([field[:, :, ny - 1], velocity[:, :, ny - 1]], axis=0)
    own_high = jnp.concatenate([field[:, :, 0], velocity[:, :, 0]], axis=0)
    low_ends = jnp.concatenate([xm[:, ny - WIDE :], xp[:, ny - 1 : ny]], axis=1)
    high_ends = jnp.concatenate([xp[:, :WIDE], xm[:, 0:1]], axis=1)
    from_low = shifted((low_ends, own_low), 0, 1)
    from_high = shifted((high_ends, own_high), 0, -1)
    flags = jnp.stack([b == 0, b == nb - 1]).astype(jnp.int32)
    updated, top = ct_update(edge_shift, edge_frac, flags, field, velocity, xm, xp, from_low, from_high)
    received = shifted(top, 0, 1)
    return advect(updated, received, strip_shift, strip_frac)


def solution(mesh):
    placed = (
        P(None, "blocks", "phi", None),
        P(None, "blocks", "phi", None),
        P("blocks"),
        P("blocks"),
        P(),
        P(),
    )
    return jax.shard_map(
        body, mesh=mesh, in_specs=placed, out_specs=P(None, "blocks", "phi", None), check_vma=False
    )
```

```python
import jax
import jax.numpy as jnp
from jax import lax
from jax.experimental import pallas as pl
from jax.experimental.pallas import tpu as pltpu
from jax.sharding import PartitionSpec as P

KMAX = 6
COURANT = 0.4
WIDE = KMAX + 2


def shifted(x, db, dp):
    nb, nq = lax.axis_size("blocks"), lax.axis_size("phi")
    if dp == 0:
        return lax.ppermute(x, "blocks", [(b, (b + db) % nb) for b in range(nb)])
    if db == 0:
        return lax.ppermute(x, "phi", [(q, (q + dp) % nq) for q in range(nq)])
    pairs = [
        (b * nq + q, ((b + db) % nb) * nq + (q + dp) % nq)
        for b in range(nb)
        for q in range(nq)
    ]
    return lax.ppermute(x, ("blocks", "phi"), pairs)


def below(v):
    return pltpu.roll(v, 1, 1)


def above(v):
    return pltpu.roll(v, v.shape[1] - 1, 1)


OFF = 7


def edge_row(dst, line, plain, ghost_on, shift, weight, base, sign):
    span = dst.shape[1]

    @pl.when(ghost_on == 0)
    def _():
        dst[...] = plain

    for k in range(KMAX + 1):
        @pl.when(jnp.logical_and(ghost_on != 0, shift == k))
        def _():
            lead = base + sign * k
            dst[...] = (1.0 - weight) * line[:, pl.ds(lead, span), :] + weight * line[:, pl.ds(lead + sign, span), :]


def ct_kernel(eshift_ref, efrac_ref, flag_ref, f_hbm, v_hbm, xm_ref, xp_ref, lend_ref, lown_ref, hend_ref, hown_ref,
              u_ref, top_ref, p_ref, ez_s, ey_s, ex_s, line, sem):
    rows = u_ref.shape[1]
    ny = u_ref.shape[2]
    copies = [
        pltpu.make_async_copy(f_hbm, p_ref.at[0:3, 1 : rows + 1, pl.ds(OFF + 1, ny)], sem.at[0]),
        pltpu.make_async_copy(v_hbm, p_ref.at[3:6, 1 : rows + 1, pl.ds(OFF + 1, ny)], sem.at[1]),
    ]
    for c in copies:
        c.start()
    for a in range(rows):
        p_ref[:, a + 1, OFF, :] = lown_ref[:, a, :]
        p_ref[:, a + 1, OFF + ny + 1, :] = hown_ref[:, a, :]

    line[:, pl.ds(0, WIDE), :] = lend_ref[:, pl.ds(0, WIDE), :]
    line[:, pl.ds(WIDE, ny), :] = xm_ref[...]
    line[:, WIDE + ny, :] = hend_ref[:, WIDE, :]
    low_plain = line[:, pl.ds(WIDE - 1, ny + 2), :]
    edge_row(p_ref.at[:, 0, pl.ds(OFF, ny + 2)], line, low_plain, flag_ref[0],
             eshift_ref[0], efrac_ref[0], WIDE - 1, -1)

    line[:, 0, :] = lend_ref[:, WIDE, :]
    line[:, pl.ds(1, ny), :] = xp_ref[...]
    line[:, pl.ds(ny + 1, WIDE), :] = hend_ref[:, pl.ds(0, WIDE), :]
    high_plain = line[:, pl.ds(0, ny + 2), :]
    edge_row(p_ref.at[:, rows + 1, pl.ds(OFF, ny + 2)], line, high_plain, flag_ref[1],
             eshift_ref[1], efrac_ref[1], 0, 1)
    for c in copies:
        c.wait()

    def emf_row(a, carry):
        fx_a = p_ref[0, a, pl.ds(OFF + 1, ny + 1), :]
        fx_ab = p_ref[0, a, pl.ds(OFF, ny + 1), :]
        fy_a = p_ref[1, a, pl.ds(OFF + 1, ny + 1), :]
        fy_m = p_ref[1, a - 1, pl.ds(OFF + 1, ny + 1), :]
        vx = (
            p_ref[3, a, pl.ds(OFF + 1, ny + 1), :]
            + p_ref[3, a - 1, pl.ds(OFF + 1, ny + 1), :]
            + p_ref[3, a, pl.ds(OFF, ny + 1), :]
            + p_ref[3, a - 1, pl.ds(OFF, ny + 1), :]
        )
        vy = (
            p_ref[4, a, pl.ds(OFF + 1, ny + 1), :]
            + p_ref[4, a - 1, pl.ds(OFF + 1, ny + 1), :]
            + p_ref[4, a, pl.ds(OFF, ny + 1), :]
            + p_ref[4, a - 1, pl.ds(OFF, ny + 1), :]
        )
        ez = (0.25 * vy) * (0.5 * (fx_a + fx_ab)) - (0.25 * vx) * (0.5 * (fy_a + fy_m))
        ez_s[a - 1, pl.ds(0, ny + 1), :] = ez

        mfx = p_ref[0, a, pl.ds(OFF + 1, ny), :]
        mfz = p_ref[2, a, pl.ds(OFF + 1, ny), :]
        mfz_m = p_ref[2, a - 1, pl.ds(OFF + 1, ny), :]
        pvx = p_ref[3, a, pl.ds(OFF + 1, ny), :] + p_ref[3, a - 1, pl.ds(OFF + 1, ny), :]
        pvz = p_ref[5, a, pl.ds(OFF + 1, ny), :] + p_ref[5, a - 1, pl.ds(OFF + 1, ny), :]
        yfx = 0.5 * (mfx + below(mfx))
        yfz = 0.5 * (mfz + mfz_m)
        yvx = 0.25 * (pvx + below(pvx))
        yvz = 0.25 * (pvz + below(pvz))
        ey_s[a - 1] = yvx * yfz - yvz * yfx

        rfy = p_ref[1, a, pl.ds(OFF + 1, ny + 1), :]
        rfz = p_ref[2, a, pl.ds(OFF + 1, ny + 1), :]
        rfz_b = p_ref[2, a, pl.ds(OFF, ny + 1), :]
        cvy = p_ref[4, a, pl.ds(OFF + 1, ny + 1), :] + p_ref[4, a, pl.ds(OFF, ny + 1), :]
        cvz = p_ref[5, a, pl.ds(OFF + 1, ny + 1), :] + p_ref[5, a, pl.ds(OFF, ny + 1), :]
        xfy = 0.5 * (rfy + below(rfy))
        xfz = 0.5 * (rfz + rfz_b)
        xvy = 0.25 * (cvy + below(cvy))
        xvz = 0.25 * (cvz + below(cvz))
        ex_s[a - 1, pl.ds(0, ny + 1), :] = xvz * xfy - xvy * xfz
        return carry

    lax.fori_loop(1, rows + 2, emf_row, 0)

    keep = KMAX + 1

    def update_row(r, carry):
        a = r + 1
        ez_r = ez_s[r, pl.ds(0, ny), :]
        ez_r1 = ez_s[r, pl.ds(1, ny), :]
        ez_n = ez_s[r + 1, pl.ds(0, ny), :]
        ey_r = ey_s[r]
        ey_n = ey_s[r + 1]
        ex_r = ex_s[r, pl.ds(0, ny), :]
        ex_r1 = ex_s[r, pl.ds(1, ny), :]
        fx = p_ref[0, a, pl.ds(OFF + 1, ny), :]
        fy = p_ref[1, a, pl.ds(OFF + 1, ny), :]
        fz = p_ref[2, a, pl.ds(OFF + 1, ny), :]
        new = (
            fx - COURANT * ((ez_r1 - ez_r) - (above(ey_r) - ey_r)),
            fy - COURANT * ((above(ex_r) - ex_r) - (ez_n - ez_r)),
            fz - COURANT * ((ey_n - ey_r) - (ex_r1 - ex_r)),
        )
        for c in range(3):
            u_ref[c, r] = new[c]
        return carry

    lax.fori_loop(0, rows, update_row, 0)
    for c in range(3):
        for r in range(rows):
            top_ref[pl.ds((c * rows + r) * keep, keep), :] = u_ref[c, r, pl.ds(ny - keep, keep), :]


def ct_update(eshift, efrac, flags, field, velocity, xm, xp, low_in, high_in):
    _, rows, ny, nz = field.shape
    keep = KMAX + 1
    vmem = pl.BlockSpec(memory_space=pltpu.VMEM)
    smem = pl.BlockSpec(memory_space=pltpu.SMEM)
    hbm = pl.BlockSpec(memory_space=pl.ANY)
    return pl.pallas_call(
        ct_kernel,
        out_shape=(
            jax.ShapeDtypeStruct((3, rows, ny, nz), field.dtype),
            jax.ShapeDtypeStruct((3 * rows * keep, nz), field.dtype),
        ),
        in_specs=[smem, smem, smem, hbm, hbm, vmem, vmem, vmem, vmem, vmem, vmem],
        out_specs=(vmem, vmem),
        scratch_shapes=[
            pltpu.VMEM((6, rows + 2, OFF + ny + 2, nz), jnp.float32),
            pltpu.VMEM((rows + 1, ny + 8, nz), jnp.float32),
            pltpu.VMEM((rows + 1, ny, nz), jnp.float32),
            pltpu.VMEM((rows + 1, ny + 8, nz), jnp.float32),
            pltpu.VMEM((6, ny + WIDE + 8, nz), jnp.float32),
            pltpu.SemaphoreType.DMA((2,)),
        ],
        cost_estimate=pl.CostEstimate(
            flops=120 * rows * ny * nz, transcendentals=0,
            bytes_accessed=4 * (6 * rows * ny + 3 * rows * ny) * nz,
        ),
    )(eshift, efrac, flags, field, velocity, xm, xp, *low_in, *high_in)


def advect_kernel(shift_ref, frac_ref, u_hbm, rec_hbm, o_ref, ext, rec_ref, sem):
    rows, ny = u_hbm.shape[1], u_hbm.shape[2]
    lead = 8
    keep = KMAX + 1
    body_copy = pltpu.make_async_copy(u_hbm, ext.at[:, :, pl.ds(lead, ny), :], sem.at[0])
    rec_copy = pltpu.make_async_copy(rec_hbm, rec_ref, sem.at[1])
    body_copy.start()
    rec_copy.start()
    rec_copy.wait()
    for c in range(3):
        for x in range(rows):
            ext[c, x, pl.ds(lead - keep, keep), :] = rec_ref[pl.ds((c * rows + x) * keep, keep), :]
    body_copy.wait()

    def strip(x, carry):
        s = shift_ref[x]
        w = frac_ref[x]
        for k in range(KMAX + 1):
            @pl.when(s == k)
            def _():
                near = ext[:, x, pl.ds(lead - k, ny), :]
                far = ext[:, x, pl.ds(lead - k - 1, ny), :]
                o_ref[:, x] = (1.0 - w) * near + w * far
        return carry

    lax.fori_loop(0, rows, strip, 0)


def advect(updated, received, strip_shift, strip_frac):
    _, rows, ny, nz = updated.shape
    vmem = pl.BlockSpec(memory_space=pltpu.VMEM)
    smem = pl.BlockSpec(memory_space=pltpu.SMEM)
    hbm = pl.BlockSpec(memory_space=pl.ANY)
    return pl.pallas_call(
        advect_kernel,
        out_shape=jax.ShapeDtypeStruct(updated.shape, updated.dtype),
        in_specs=[smem, smem, hbm, hbm],
        out_specs=vmem,
        scratch_shapes=[
            pltpu.VMEM((3, rows, ny + 8, nz), jnp.float32),
            pltpu.VMEM(received.shape, jnp.float32),
            pltpu.SemaphoreType.DMA((2,)),
        ],
        cost_estimate=pl.CostEstimate(
            flops=3 * 3 * rows * ny * nz, transcendentals=0,
            bytes_accessed=4 * 3 * rows * (2 * ny + KMAX + 1) * nz,
        ),
    )(strip_shift, strip_frac, updated, received)


def body(field, velocity, strip_shift, strip_frac, edge_shift, edge_frac):
    _, nx, ny, nz = field.shape
    nb = lax.axis_size("blocks")
    b = lax.axis_index("blocks")

    xm = shifted(jnp.concatenate([field[:, nx - 1], velocity[:, nx - 1]], axis=0), 1, 0)
    xp = shifted(jnp.concatenate([field[:, 0], velocity[:, 0]], axis=0), -1, 0)
    own_low = jnp.concatenate([field[:, :, ny - 1], velocity[:, :, ny - 1]], axis=0)
    own_high = jnp.concatenate([field[:, :, 0], velocity[:, :, 0]], axis=0)
    low_ends = jnp.concatenate([xm[:, ny - WIDE :], xp[:, ny - 1 : ny]], axis=1)
    high_ends = jnp.concatenate([xp[:, :WIDE], xm[:, 0:1]], axis=1)
    from_low = shifted((low_ends, own_low), 0, 1)
    from_high = shifted((high_ends, own_high), 0, -1)
    flags = jnp.stack([b == 0, b == nb - 1]).astype(jnp.int32)
    updated, top = ct_update(edge_shift, edge_frac, flags, field, velocity, xm, xp, from_low, from_high)
    received = shifted(top, 0, 1)
    return advect(updated, received, strip_shift, strip_frac)


def solution(mesh):
    placed = (
        P(None, "blocks", "phi", None),
        P(None, "blocks", "phi", None),
        P("blocks"),
        P("blocks"),
        P(),
        P(),
    )
    return jax.shard_map(
        body, mesh=mesh, in_specs=placed, out_specs=P(None, "blocks", "phi", None), check_vma=False
    )
```

```python
import jax
import jax.numpy as jnp
from jax import lax
from jax.experimental import pallas as pl
from jax.experimental.pallas import tpu as pltpu
from jax.sharding import PartitionSpec as P

KMAX = 6
COURANT = 0.4
WIDE = KMAX + 2


def shifted(x, db, dp):
    nb, nq = lax.axis_size("blocks"), lax.axis_size("phi")
    if dp == 0:
        return lax.ppermute(x, "blocks", [(b, (b + db) % nb) for b in range(nb)])
    if db == 0:
        return lax.ppermute(x, "phi", [(q, (q + dp) % nq) for q in range(nq)])
    pairs = [
        (b * nq + q, ((b + db) % nb) * nq + (q + dp) % nq)
        for b in range(nb)
        for q in range(nq)
    ]
    return lax.ppermute(x, ("blocks", "phi"), pairs)


def below(v):
    return pltpu.roll(v, 1, 1)


def above(v):
    return pltpu.roll(v, v.shape[1] - 1, 1)


OFF = 7


def edge_row(dst, line, plain, ghost_on, shift, weight, base, sign):
    span = dst.shape[1]

    @pl.when(ghost_on == 0)
    def _():
        dst[...] = plain

    for k in range(KMAX + 1):
        @pl.when(jnp.logical_and(ghost_on != 0, shift == k))
        def _():
            lead = base + sign * k
            dst[...] = (1.0 - weight) * line[:, pl.ds(lead, span), :] + weight * line[:, pl.ds(lead + sign, span), :]


def ct_kernel(eshift_ref, efrac_ref, flag_ref, f_hbm, v_hbm, xm_ref, xp_ref, lend_ref, lown_ref, hend_ref, hown_ref,
              u_ref, top_ref, p_ref, ez_s, ey_s, ex_s, line, sem):
    rows = u_ref.shape[1]
    ny = u_ref.shape[2]
    copies = [
        pltpu.make_async_copy(f_hbm, p_ref.at[0:3, 1 : rows + 1, pl.ds(OFF + 1, ny)], sem.at[0]),
        pltpu.make_async_copy(v_hbm, p_ref.at[3:6, 1 : rows + 1, pl.ds(OFF + 1, ny)], sem.at[1]),
    ]
    for c in copies:
        c.start()
    for a in range(rows):
        p_ref[:, a + 1, OFF, :] = lown_ref[:, a, :]
        p_ref[:, a + 1, OFF + ny + 1, :] = hown_ref[:, a, :]

    line[:, pl.ds(0, WIDE), :] = lend_ref[:, pl.ds(0, WIDE), :]
    line[:, pl.ds(WIDE, ny), :] = xm_ref[...]
    line[:, WIDE + ny, :] = hend_ref[:, WIDE, :]
    low_plain = line[:, pl.ds(WIDE - 1, ny + 2), :]
    edge_row(p_ref.at[:, 0, pl.ds(OFF, ny + 2)], line, low_plain, flag_ref[0],
             eshift_ref[0], efrac_ref[0], WIDE - 1, -1)

    line[:, 0, :] = lend_ref[:, WIDE, :]
    line[:, pl.ds(1, ny), :] = xp_ref[...]
    line[:, pl.ds(ny + 1, WIDE), :] = hend_ref[:, pl.ds(0, WIDE), :]
    high_plain = line[:, pl.ds(0, ny + 2), :]
    edge_row(p_ref.at[:, rows + 1, pl.ds(OFF, ny + 2)], line, high_plain, flag_ref[1],
             eshift_ref[1], efrac_ref[1], 0, 1)
    for c in copies:
        c.wait()

    def emf_row(a, carry):
        fx_a = p_ref[0, a, pl.ds(OFF + 1, ny + 1), :]
        fx_ab = p_ref[0, a, pl.ds(OFF, ny + 1), :]
        fy_a = p_ref[1, a, pl.ds(OFF + 1, ny + 1), :]
        fy_m = p_ref[1, a - 1, pl.ds(OFF + 1, ny + 1), :]
        vx = (
            p_ref[3, a, pl.ds(OFF + 1, ny + 1), :]
            + p_ref[3, a - 1, pl.ds(OFF + 1, ny + 1), :]
            + p_ref[3, a, pl.ds(OFF, ny + 1), :]
            + p_ref[3, a - 1, pl.ds(OFF, ny + 1), :]
        )
        vy = (
            p_ref[4, a, pl.ds(OFF + 1, ny + 1), :]
            + p_ref[4, a - 1, pl.ds(OFF + 1, ny + 1), :]
            + p_ref[4, a, pl.ds(OFF, ny + 1), :]
            + p_ref[4, a - 1, pl.ds(OFF, ny + 1), :]
        )
        ez = (0.25 * vy) * (0.5 * (fx_a + fx_ab)) - (0.25 * vx) * (0.5 * (fy_a + fy_m))
        ez_s[a - 1, pl.ds(0, ny + 1), :] = ez

        mfx = p_ref[0, a, pl.ds(OFF + 1, ny), :]
        mfz = p_ref[2, a, pl.ds(OFF + 1, ny), :]
        mfz_m = p_ref[2, a - 1, pl.ds(OFF + 1, ny), :]
        pvx = p_ref[3, a, pl.ds(OFF + 1, ny), :] + p_ref[3, a - 1, pl.ds(OFF + 1, ny), :]
        pvz = p_ref[5, a, pl.ds(OFF + 1, ny), :] + p_ref[5, a - 1, pl.ds(OFF + 1, ny), :]
        yfx = 0.5 * (mfx + below(mfx))
        yfz = 0.5 * (mfz + mfz_m)
        yvx = 0.25 * (pvx + below(pvx))
        yvz = 0.25 * (pvz + below(pvz))
        ey_s[a - 1] = yvx * yfz - yvz * yfx

        rfy = p_ref[1, a, pl.ds(OFF + 1, ny + 1), :]
        rfz = p_ref[2, a, pl.ds(OFF + 1, ny + 1), :]
        rfz_b = p_ref[2, a, pl.ds(OFF, ny + 1), :]
        cvy = p_ref[4, a, pl.ds(OFF + 1, ny + 1), :] + p_ref[4, a, pl.ds(OFF, ny + 1), :]
        cvz = p_ref[5, a, pl.ds(OFF + 1, ny + 1), :] + p_ref[5, a, pl.ds(OFF, ny + 1), :]
        xfy = 0.5 * (rfy + below(rfy))
        xfz = 0.5 * (rfz + rfz_b)
        xvy = 0.25 * (cvy + below(cvy))
        xvz = 0.25 * (cvz + below(cvz))
        ex_s[a - 1, pl.ds(0, ny + 1), :] = xvz * xfy - xvy * xfz
        return carry

    lax.fori_loop(1, rows + 2, emf_row, 0)

    keep = KMAX + 1

    def update_row(r, carry):
        a = r + 1
        ez_r = ez_s[r, pl.ds(0, ny), :]
        ez_r1 = ez_s[r, pl.ds(1, ny), :]
        ez_n = ez_s[r + 1, pl.ds(0, ny), :]
        ey_r = ey_s[r]
        ey_n = ey_s[r + 1]
        ex_r = ex_s[r, pl.ds(0, ny), :]
        ex_r1 = ex_s[r, pl.ds(1, ny), :]
        fx = p_ref[0, a, pl.ds(OFF + 1, ny), :]
        fy = p_ref[1, a, pl.ds(OFF + 1, ny), :]
        fz = p_ref[2, a, pl.ds(OFF + 1, ny), :]
        new = (
            fx - COURANT * ((ez_r1 - ez_r) - (above(ey_r) - ey_r)),
            fy - COURANT * ((above(ex_r) - ex_r) - (ez_n - ez_r)),
            fz - COURANT * ((ey_n - ey_r) - (ex_r1 - ex_r)),
        )
        for c in range(3):
            u_ref[c, r] = new[c]
            top_ref[pl.ds((c * rows + r) * keep, keep), :] = new[c][ny - keep :]
        return carry

    for r in range(rows):
        update_row(r, 0)


def ct_update(eshift, efrac, flags, field, velocity, xm, xp, low_in, high_in):
    _, rows, ny, nz = field.shape
    keep = KMAX + 1
    vmem = pl.BlockSpec(memory_space=pltpu.VMEM)
    smem = pl.BlockSpec(memory_space=pltpu.SMEM)
    hbm = pl.BlockSpec(memory_space=pl.ANY)
    return pl.pallas_call(
        ct_kernel,
        out_shape=(
            jax.ShapeDtypeStruct((3, rows, ny, nz), field.dtype),
            jax.ShapeDtypeStruct((3 * rows * keep, nz), field.dtype),
        ),
        in_specs=[smem, smem, smem, hbm, hbm, vmem, vmem, vmem, vmem, vmem, vmem],
        out_specs=(vmem, vmem),
        scratch_shapes=[
            pltpu.VMEM((6, rows + 2, OFF + ny + 2, nz), jnp.float32),
            pltpu.VMEM((rows + 1, ny + 8, nz), jnp.float32),
            pltpu.VMEM((rows + 1, ny, nz), jnp.float32),
            pltpu.VMEM((rows + 1, ny + 8, nz), jnp.float32),
            pltpu.VMEM((6, ny + WIDE + 8, nz), jnp.float32),
            pltpu.SemaphoreType.DMA((2,)),
        ],
        cost_estimate=pl.CostEstimate(
            flops=120 * rows * ny * nz, transcendentals=0,
            bytes_accessed=4 * (6 * rows * ny + 3 * rows * ny) * nz,
        ),
    )(eshift, efrac, flags, field, velocity, xm, xp, *low_in, *high_in)


def advect_kernel(shift_ref, frac_ref, u_ref, rec_ref, o_ref, ext):
    rows, ny = u_ref.shape[1], u_ref.shape[2]
    lead = 8
    keep = KMAX + 1
    for c in range(3):
        for x in range(rows):
            ext[c, x, pl.ds(lead - keep, keep), :] = rec_ref[pl.ds((c * rows + x) * keep, keep), :]
    ext[:, :, pl.ds(lead, ny), :] = u_ref[...]

    def strip(x, carry):
        s = shift_ref[x]
        w = frac_ref[x]
        for k in range(KMAX + 1):
            @pl.when(s == k)
            def _():
                near = ext[:, x, pl.ds(lead - k, ny), :]
                far = ext[:, x, pl.ds(lead - k - 1, ny), :]
                o_ref[:, x] = (1.0 - w) * near + w * far
        return carry

    lax.fori_loop(0, rows, strip, 0)


def advect(updated, received, strip_shift, strip_frac):
    _, rows, ny, nz = updated.shape
    vmem = pl.BlockSpec(memory_space=pltpu.VMEM)
    smem = pl.BlockSpec(memory_space=pltpu.SMEM)
    return pl.pallas_call(
        advect_kernel,
        out_shape=jax.ShapeDtypeStruct(updated.shape, updated.dtype),
        in_specs=[smem, smem, vmem, vmem],
        out_specs=vmem,
        scratch_shapes=[pltpu.VMEM((3, rows, ny + 8, nz), jnp.float32)],
        cost_estimate=pl.CostEstimate(
            flops=3 * 3 * rows * ny * nz, transcendentals=0,
            bytes_accessed=4 * 3 * rows * (2 * ny + KMAX + 1) * nz,
        ),
    )(strip_shift, strip_frac, updated, received)


def body(field, velocity, strip_shift, strip_frac, edge_shift, edge_frac):
    _, nx, ny, nz = field.shape
    nb = lax.axis_size("blocks")
    b = lax.axis_index("blocks")

    xm = shifted(jnp.concatenate([field[:, nx - 1], velocity[:, nx - 1]], axis=0), 1, 0)
    xp = shifted(jnp.concatenate([field[:, 0], velocity[:, 0]], axis=0), -1, 0)
    own_low = jnp.concatenate([field[:, :, ny - 1], velocity[:, :, ny - 1]], axis=0)
    own_high = jnp.concatenate([field[:, :, 0], velocity[:, :, 0]], axis=0)
    low_ends = jnp.concatenate([xm[:, ny - WIDE :], xp[:, ny - 1 : ny]], axis=1)
    high_ends = jnp.concatenate([xp[:, :WIDE], xm[:, 0:1]], axis=1)
    from_low = shifted((low_ends, own_low), 0, 1)
    from_high = shifted((high_ends, own_high), 0, -1)
    flags = jnp.stack([b == 0, b == nb - 1]).astype(jnp.int32)
    updated, top = ct_update(edge_shift, edge_frac, flags, field, velocity, xm, xp, from_low, from_high)
    received = shifted(top, 0, 1)
    return advect(updated, received, strip_shift, strip_frac)


def solution(mesh):
    placed = (
        P(None, "blocks", "phi", None),
        P(None, "blocks", "phi", None),
        P("blocks"),
        P("blocks"),
        P(),
        P(),
    )
    return jax.shard_map(
        body, mesh=mesh, in_specs=placed, out_specs=P(None, "blocks", "phi", None), check_vma=False
    )
```

```python
import jax
import jax.numpy as jnp
from jax import lax
from jax.experimental import pallas as pl
from jax.experimental.pallas import tpu as pltpu
from jax.sharding import PartitionSpec as P

KMAX = 6
COURANT = 0.4
WIDE = KMAX + 2


def shifted(x, db, dp):
    nb, nq = lax.axis_size("blocks"), lax.axis_size("phi")
    if dp == 0:
        return lax.ppermute(x, "blocks", [(b, (b + db) % nb) for b in range(nb)])
    if db == 0:
        return lax.ppermute(x, "phi", [(q, (q + dp) % nq) for q in range(nq)])
    pairs = [
        (b * nq + q, ((b + db) % nb) * nq + (q + dp) % nq)
        for b in range(nb)
        for q in range(nq)
    ]
    return lax.ppermute(x, ("blocks", "phi"), pairs)


def below(v):
    return pltpu.roll(v, 1, 1)


def above(v):
    return pltpu.roll(v, v.shape[1] - 1, 1)


OFF = 7


def edge_row(dst, line, plain, ghost_on, shift, weight, base, sign):
    span = dst.shape[1]

    @pl.when(ghost_on == 0)
    def _():
        dst[...] = plain

    for k in range(KMAX + 1):
        @pl.when(jnp.logical_and(ghost_on != 0, shift == k))
        def _():
            lead = base + sign * k
            dst[...] = (1.0 - weight) * line[:, pl.ds(lead, span), :] + weight * line[:, pl.ds(lead + sign, span), :]


def ct_kernel(eshift_ref, efrac_ref, flag_ref, f_hbm, v_hbm, xm_ref, xp_ref, lend_ref, lown_ref, hend_ref, hown_ref,
              u_ref, top_ref, p_ref, ez_s, ey_s, ex_s, line, sem):
    rows = u_ref.shape[1]
    ny = u_ref.shape[2]
    copies = [
        pltpu.make_async_copy(f_hbm, p_ref.at[0:3, 1 : rows + 1, pl.ds(OFF + 1, ny)], sem.at[0]),
        pltpu.make_async_copy(v_hbm, p_ref.at[3:6, 1 : rows + 1, pl.ds(OFF + 1, ny)], sem.at[1]),
    ]
    for c in copies:
        c.start()
    for a in range(rows):
        p_ref[:, a + 1, OFF, :] = lown_ref[:, a, :]
        p_ref[:, a + 1, OFF + ny + 1, :] = hown_ref[:, a, :]

    line[:, pl.ds(0, WIDE), :] = lend_ref[:, pl.ds(0, WIDE), :]
    line[:, pl.ds(WIDE, ny), :] = xm_ref[...]
    line[:, WIDE + ny, :] = hend_ref[:, WIDE, :]
    low_plain = line[:, pl.ds(WIDE - 1, ny + 2), :]
    edge_row(p_ref.at[:, 0, pl.ds(OFF, ny + 2)], line, low_plain, flag_ref[0],
             eshift_ref[0], efrac_ref[0], WIDE - 1, -1)

    line[:, 0, :] = lend_ref[:, WIDE, :]
    line[:, pl.ds(1, ny), :] = xp_ref[...]
    line[:, pl.ds(ny + 1, WIDE), :] = hend_ref[:, pl.ds(0, WIDE), :]
    high_plain = line[:, pl.ds(0, ny + 2), :]
    edge_row(p_ref.at[:, rows + 1, pl.ds(OFF, ny + 2)], line, high_plain, flag_ref[1],
             eshift_ref[1], efrac_ref[1], 0, 1)
    for c in copies:
        c.wait()

    def emf_row(a, carry):
        fx_a = p_ref[0, a, pl.ds(OFF + 1, ny + 1), :]
        fx_ab = p_ref[0, a, pl.ds(OFF, ny + 1), :]
        fy_a = p_ref[1, a, pl.ds(OFF + 1, ny + 1), :]
        fy_m = p_ref[1, a - 1, pl.ds(OFF + 1, ny + 1), :]
        vx = (
            p_ref[3, a, pl.ds(OFF + 1, ny + 1), :]
            + p_ref[3, a - 1, pl.ds(OFF + 1, ny + 1), :]
            + p_ref[3, a, pl.ds(OFF, ny + 1), :]
            + p_ref[3, a - 1, pl.ds(OFF, ny + 1), :]
        )
        vy = (
            p_ref[4, a, pl.ds(OFF + 1, ny + 1), :]
            + p_ref[4, a - 1, pl.ds(OFF + 1, ny + 1), :]
            + p_ref[4, a, pl.ds(OFF, ny + 1), :]
            + p_ref[4, a - 1, pl.ds(OFF, ny + 1), :]
        )
        ez = (0.25 * vy) * (0.5 * (fx_a + fx_ab)) - (0.25 * vx) * (0.5 * (fy_a + fy_m))
        ez_s[a - 1, pl.ds(0, ny + 1), :] = ez

        mfx = p_ref[0, a, pl.ds(OFF + 1, ny), :]
        mfz = p_ref[2, a, pl.ds(OFF + 1, ny), :]
        mfz_m = p_ref[2, a - 1, pl.ds(OFF + 1, ny), :]
        pvx = p_ref[3, a, pl.ds(OFF + 1, ny), :] + p_ref[3, a - 1, pl.ds(OFF + 1, ny), :]
        pvz = p_ref[5, a, pl.ds(OFF + 1, ny), :] + p_ref[5, a - 1, pl.ds(OFF + 1, ny), :]
        yfx = 0.5 * (mfx + below(mfx))
        yfz = 0.5 * (mfz + mfz_m)
        yvx = 0.25 * (pvx + below(pvx))
        yvz = 0.25 * (pvz + below(pvz))
        ey_s[a - 1] = yvx * yfz - yvz * yfx

        rfy = p_ref[1, a, pl.ds(OFF + 1, ny + 1), :]
        rfz = p_ref[2, a, pl.ds(OFF + 1, ny + 1), :]
        rfz_b = p_ref[2, a, pl.ds(OFF, ny + 1), :]
        cvy = p_ref[4, a, pl.ds(OFF + 1, ny + 1), :] + p_ref[4, a, pl.ds(OFF, ny + 1), :]
        cvz = p_ref[5, a, pl.ds(OFF + 1, ny + 1), :] + p_ref[5, a, pl.ds(OFF, ny + 1), :]
        xfy = 0.5 * (rfy + below(rfy))
        xfz = 0.5 * (rfz + rfz_b)
        xvy = 0.25 * (cvy + below(cvy))
        xvz = 0.25 * (cvz + below(cvz))
        ex_s[a - 1, pl.ds(0, ny + 1), :] = xvz * xfy - xvy * xfz
        return carry

    for a in range(1, rows + 2):
        emf_row(a, 0)

    keep = KMAX + 1

    def update_row(r, carry):
        a = r + 1
        ez_r = ez_s[r, pl.ds(0, ny), :]
        ez_r1 = ez_s[r, pl.ds(1, ny), :]
        ez_n = ez_s[r + 1, pl.ds(0, ny), :]
        ey_r = ey_s[r]
        ey_n = ey_s[r + 1]
        ex_r = ex_s[r, pl.ds(0, ny), :]
        ex_r1 = ex_s[r, pl.ds(1, ny), :]
        fx = p_ref[0, a, pl.ds(OFF + 1, ny), :]
        fy = p_ref[1, a, pl.ds(OFF + 1, ny), :]
        fz = p_ref[2, a, pl.ds(OFF + 1, ny), :]
        new = (
            fx - COURANT * ((ez_r1 - ez_r) - (above(ey_r) - ey_r)),
            fy - COURANT * ((above(ex_r) - ex_r) - (ez_n - ez_r)),
            fz - COURANT * ((ey_n - ey_r) - (ex_r1 - ex_r)),
        )
        for c in range(3):
            u_ref[c, r] = new[c]
            top_ref[pl.ds((c * rows + r) * keep, keep), :] = new[c][ny - keep :]
        return carry

    for r in range(rows):
        update_row(r, 0)


def ct_update(eshift, efrac, flags, field, velocity, xm, xp, low_in, high_in):
    _, rows, ny, nz = field.shape
    keep = KMAX + 1
    vmem = pl.BlockSpec(memory_space=pltpu.VMEM)
    smem = pl.BlockSpec(memory_space=pltpu.SMEM)
    hbm = pl.BlockSpec(memory_space=pl.ANY)
    return pl.pallas_call(
        ct_kernel,
        out_shape=(
            jax.ShapeDtypeStruct((3, rows, ny, nz), field.dtype),
            jax.ShapeDtypeStruct((3 * rows * keep, nz), field.dtype),
        ),
        in_specs=[smem, smem, smem, hbm, hbm, vmem, vmem, vmem, vmem, vmem, vmem],
        out_specs=(vmem, vmem),
        scratch_shapes=[
            pltpu.VMEM((6, rows + 2, OFF + ny + 2, nz), jnp.float32),
            pltpu.VMEM((rows + 1, ny + 8, nz), jnp.float32),
            pltpu.VMEM((rows + 1, ny, nz), jnp.float32),
            pltpu.VMEM((rows + 1, ny + 8, nz), jnp.float32),
            pltpu.VMEM((6, ny + WIDE + 8, nz), jnp.float32),
            pltpu.SemaphoreType.DMA((2,)),
        ],
        cost_estimate=pl.CostEstimate(
            flops=120 * rows * ny * nz, transcendentals=0,
            bytes_accessed=4 * (6 * rows * ny + 3 * rows * ny) * nz,
        ),
    )(eshift, efrac, flags, field, velocity, xm, xp, *low_in, *high_in)


def advect_kernel(shift_ref, frac_ref, u_ref, rec_ref, o_ref, ext):
    rows, ny = u_ref.shape[1], u_ref.shape[2]
    lead = 8
    keep = KMAX + 1
    for c in range(3):
        for x in range(rows):
            ext[c, x, pl.ds(lead - keep, keep), :] = rec_ref[pl.ds((c * rows + x) * keep, keep), :]
    ext[:, :, pl.ds(lead, ny), :] = u_ref[...]

    def strip(x, carry):
        s = shift_ref[x]
        w = frac_ref[x]
        for k in range(KMAX + 1):
            @pl.when(s == k)
            def _():
                near = ext[:, x, pl.ds(lead - k, ny), :]
                far = ext[:, x, pl.ds(lead - k - 1, ny), :]
                o_ref[:, x] = (1.0 - w) * near + w * far
        return carry

    lax.fori_loop(0, rows, strip, 0)


def advect(updated, received, strip_shift, strip_frac):
    _, rows, ny, nz = updated.shape
    vmem = pl.BlockSpec(memory_space=pltpu.VMEM)
    smem = pl.BlockSpec(memory_space=pltpu.SMEM)
    return pl.pallas_call(
        advect_kernel,
        out_shape=jax.ShapeDtypeStruct(updated.shape, updated.dtype),
        in_specs=[smem, smem, vmem, vmem],
        out_specs=vmem,
        scratch_shapes=[pltpu.VMEM((3, rows, ny + 8, nz), jnp.float32)],
        cost_estimate=pl.CostEstimate(
            flops=3 * 3 * rows * ny * nz, transcendentals=0,
            bytes_accessed=4 * 3 * rows * (2 * ny + KMAX + 1) * nz,
        ),
    )(strip_shift, strip_frac, updated, received)


def body(field, velocity, strip_shift, strip_frac, edge_shift, edge_frac):
    _, nx, ny, nz = field.shape
    nb = lax.axis_size("blocks")
    b = lax.axis_index("blocks")

    xm = shifted(jnp.concatenate([field[:, nx - 1], velocity[:, nx - 1]], axis=0), 1, 0)
    xp = shifted(jnp.concatenate([field[:, 0], velocity[:, 0]], axis=0), -1, 0)
    own_low = jnp.concatenate([field[:, :, ny - 1], velocity[:, :, ny - 1]], axis=0)
    own_high = jnp.concatenate([field[:, :, 0], velocity[:, :, 0]], axis=0)
    low_ends = jnp.concatenate([xm[:, ny - WIDE :], xp[:, ny - 1 : ny]], axis=1)
    high_ends = jnp.concatenate([xp[:, :WIDE], xm[:, 0:1]], axis=1)
    from_low = shifted((low_ends, own_low), 0, 1)
    from_high = shifted((high_ends, own_high), 0, -1)
    flags = jnp.stack([b == 0, b == nb - 1]).astype(jnp.int32)
    updated, top = ct_update(edge_shift, edge_frac, flags, field, velocity, xm, xp, from_low, from_high)
    received = shifted(top, 0, 1)
    return advect(updated, received, strip_shift, strip_frac)


def solution(mesh):
    placed = (
        P(None, "blocks", "phi", None),
        P(None, "blocks", "phi", None),
        P("blocks"),
        P("blocks"),
        P(),
        P(),
    )
    return jax.shard_map(
        body, mesh=mesh, in_specs=placed, out_specs=P(None, "blocks", "phi", None), check_vma=False
    )
```

```python
import jax
import jax.numpy as jnp
from jax import lax
from jax.experimental import pallas as pl
from jax.experimental.pallas import tpu as pltpu
from jax.sharding import PartitionSpec as P

KMAX = 6
COURANT = 0.4
WIDE = KMAX + 2


def shifted(x, db, dp):
    nb, nq = lax.axis_size("blocks"), lax.axis_size("phi")
    if dp == 0:
        return lax.ppermute(x, "blocks", [(b, (b + db) % nb) for b in range(nb)])
    if db == 0:
        return lax.ppermute(x, "phi", [(q, (q + dp) % nq) for q in range(nq)])
    pairs = [
        (b * nq + q, ((b + db) % nb) * nq + (q + dp) % nq)
        for b in range(nb)
        for q in range(nq)
    ]
    return lax.ppermute(x, ("blocks", "phi"), pairs)


def below(v):
    return pltpu.roll(v, 1, 1)


def above(v):
    return pltpu.roll(v, v.shape[1] - 1, 1)


OFF = 7


def edge_row(dst, line, plain, ghost_on, shift, weight, base, sign):
    span = dst.shape[1]

    @pl.when(ghost_on == 0)
    def _():
        dst[...] = plain

    for k in range(KMAX + 1):
        @pl.when(jnp.logical_and(ghost_on != 0, shift == k))
        def _():
            lead = base + sign * k
            dst[...] = (1.0 - weight) * line[:, pl.ds(lead, span), :] + weight * line[:, pl.ds(lead + sign, span), :]


def ct_kernel(eshift_ref, efrac_ref, flag_ref, f_hbm, v_hbm, xm_ref, xp_ref, lend_ref, lown_ref, hend_ref, hown_ref,
              u_ref, top_ref, p_ref, ez_s, ey_s, ex_s, line, sem):
    rows = u_ref.shape[1]
    ny = u_ref.shape[2]
    copies = [
        pltpu.make_async_copy(f_hbm, p_ref.at[0:3, 1 : rows + 1, pl.ds(OFF + 1, ny)], sem.at[0]),
        pltpu.make_async_copy(v_hbm, p_ref.at[3:6, 1 : rows + 1, pl.ds(OFF + 1, ny)], sem.at[1]),
    ]
    for c in copies:
        c.start()
    for a in range(rows):
        p_ref[:, a + 1, OFF, :] = lown_ref[:, a, :]
        p_ref[:, a + 1, OFF + ny + 1, :] = hown_ref[:, a, :]

    line[:, pl.ds(0, WIDE), :] = lend_ref[:, pl.ds(0, WIDE), :]
    line[:, pl.ds(WIDE, ny), :] = xm_ref[...]
    line[:, WIDE + ny, :] = hend_ref[:, WIDE, :]
    low_plain = line[:, pl.ds(WIDE - 1, ny + 2), :]
    edge_row(p_ref.at[:, 0, pl.ds(OFF, ny + 2)], line, low_plain, flag_ref[0],
             eshift_ref[0], efrac_ref[0], WIDE - 1, -1)

    line[:, 0, :] = lend_ref[:, WIDE, :]
    line[:, pl.ds(1, ny), :] = xp_ref[...]
    line[:, pl.ds(ny + 1, WIDE), :] = hend_ref[:, pl.ds(0, WIDE), :]
    high_plain = line[:, pl.ds(0, ny + 2), :]
    edge_row(p_ref.at[:, rows + 1, pl.ds(OFF, ny + 2)], line, high_plain, flag_ref[1],
             eshift_ref[1], efrac_ref[1], 0, 1)
    for c in copies:
        c.wait()

    def emf_row(a, carry):
        fx_a = p_ref[0, a, pl.ds(OFF + 1, ny + 1), :]
        fx_ab = p_ref[0, a, pl.ds(OFF, ny + 1), :]
        fy_a = p_ref[1, a, pl.ds(OFF + 1, ny + 1), :]
        fy_m = p_ref[1, a - 1, pl.ds(OFF + 1, ny + 1), :]
        vx = (
            p_ref[3, a, pl.ds(OFF + 1, ny + 1), :]
            + p_ref[3, a - 1, pl.ds(OFF + 1, ny + 1), :]
            + p_ref[3, a, pl.ds(OFF, ny + 1), :]
            + p_ref[3, a - 1, pl.ds(OFF, ny + 1), :]
        )
        vy = (
            p_ref[4, a, pl.ds(OFF + 1, ny + 1), :]
            + p_ref[4, a - 1, pl.ds(OFF + 1, ny + 1), :]
            + p_ref[4, a, pl.ds(OFF, ny + 1), :]
            + p_ref[4, a - 1, pl.ds(OFF, ny + 1), :]
        )
        ez = (0.25 * vy) * (0.5 * (fx_a + fx_ab)) - (0.25 * vx) * (0.5 * (fy_a + fy_m))
        ez_s[a - 1, pl.ds(0, ny + 1), :] = ez

        mfx = p_ref[0, a, pl.ds(OFF + 1, ny), :]
        mfz = p_ref[2, a, pl.ds(OFF + 1, ny), :]
        mfz_m = p_ref[2, a - 1, pl.ds(OFF + 1, ny), :]
        pvx = p_ref[3, a, pl.ds(OFF + 1, ny), :] + p_ref[3, a - 1, pl.ds(OFF + 1, ny), :]
        pvz = p_ref[5, a, pl.ds(OFF + 1, ny), :] + p_ref[5, a - 1, pl.ds(OFF + 1, ny), :]
        yfx = 0.5 * (mfx + below(mfx))
        yfz = 0.5 * (mfz + mfz_m)
        yvx = 0.25 * (pvx + below(pvx))
        yvz = 0.25 * (pvz + below(pvz))
        ey_s[a - 1] = yvx * yfz - yvz * yfx

        rfy = p_ref[1, a, pl.ds(OFF + 1, ny + 1), :]
        rfz = p_ref[2, a, pl.ds(OFF + 1, ny + 1), :]
        rfz_b = p_ref[2, a, pl.ds(OFF, ny + 1), :]
        cvy = p_ref[4, a, pl.ds(OFF + 1, ny + 1), :] + p_ref[4, a, pl.ds(OFF, ny + 1), :]
        cvz = p_ref[5, a, pl.ds(OFF + 1, ny + 1), :] + p_ref[5, a, pl.ds(OFF, ny + 1), :]
        xfy = 0.5 * (rfy + below(rfy))
        xfz = 0.5 * (rfz + rfz_b)
        xvy = 0.25 * (cvy + below(cvy))
        xvz = 0.25 * (cvz + below(cvz))
        ex_s[a - 1, pl.ds(0, ny + 1), :] = xvz * xfy - xvy * xfz
        return carry

    for a in range(1, rows + 2):
        emf_row(a, 0)

    keep = KMAX + 1

    def update_row(r, carry):
        a = r + 1
        ez_r = ez_s[r, pl.ds(0, ny), :]
        ez_r1 = ez_s[r, pl.ds(1, ny), :]
        ez_n = ez_s[r + 1, pl.ds(0, ny), :]
        ey_r = ey_s[r]
        ey_n = ey_s[r + 1]
        ex_r = ex_s[r, pl.ds(0, ny), :]
        ex_r1 = ex_s[r, pl.ds(1, ny), :]
        fx = p_ref[0, a, pl.ds(OFF + 1, ny), :]
        fy = p_ref[1, a, pl.ds(OFF + 1, ny), :]
        fz = p_ref[2, a, pl.ds(OFF + 1, ny), :]
        new = (
            fx - COURANT * ((ez_r1 - ez_r) - (above(ey_r) - ey_r)),
            fy - COURANT * ((above(ex_r) - ex_r) - (ez_n - ez_r)),
            fz - COURANT * ((ey_n - ey_r) - (ex_r1 - ex_r)),
        )
        for c in range(3):
            u_ref[c, r] = new[c]
            top_ref[pl.ds((c * rows + r) * keep, keep), :] = new[c][ny - keep :]
        return carry

    for r in range(rows):
        update_row(r, 0)


def ct_update(eshift, efrac, flags, field, velocity, xm, xp, low_in, high_in):
    _, rows, ny, nz = field.shape
    keep = KMAX + 1
    vmem = pl.BlockSpec(memory_space=pltpu.VMEM)
    smem = pl.BlockSpec(memory_space=pltpu.SMEM)
    hbm = pl.BlockSpec(memory_space=pl.ANY)
    return pl.pallas_call(
        ct_kernel,
        out_shape=(
            jax.ShapeDtypeStruct((3, rows, ny, nz), field.dtype),
            jax.ShapeDtypeStruct((3 * rows * keep, nz), field.dtype),
        ),
        in_specs=[smem, smem, smem, hbm, hbm, vmem, vmem, vmem, vmem, vmem, vmem],
        out_specs=(vmem, vmem),
        scratch_shapes=[
            pltpu.VMEM((6, rows + 2, OFF + ny + 2, nz), jnp.float32),
            pltpu.VMEM((rows + 1, ny + 8, nz), jnp.float32),
            pltpu.VMEM((rows + 1, ny, nz), jnp.float32),
            pltpu.VMEM((rows + 1, ny + 8, nz), jnp.float32),
            pltpu.VMEM((6, ny + WIDE + 8, nz), jnp.float32),
            pltpu.SemaphoreType.DMA((2,)),
        ],
        cost_estimate=pl.CostEstimate(
            flops=120 * rows * ny * nz, transcendentals=0,
            bytes_accessed=4 * (6 * rows * ny + 3 * rows * ny) * nz,
        ),
    )(eshift, efrac, flags, field, velocity, xm, xp, *low_in, *high_in)


def advect_kernel(shift_ref, frac_ref, u_ref, rec_ref, o_ref, ext):
    rows, ny = u_ref.shape[1], u_ref.shape[2]
    lead = 8
    keep = KMAX + 1
    for c in range(3):
        for x in range(rows):
            ext[c, x, pl.ds(lead - keep, keep), :] = rec_ref[pl.ds((c * rows + x) * keep, keep), :]
    ext[:, :, pl.ds(lead, ny), :] = u_ref[...]

    def strip(x, carry):
        s = shift_ref[x]
        w = frac_ref[x]
        for k in range(KMAX + 1):
            @pl.when(s == k)
            def _():
                near = ext[:, x, pl.ds(lead - k, ny), :]
                far = ext[:, x, pl.ds(lead - k - 1, ny), :]
                o_ref[:, x] = (1.0 - w) * near + w * far
        return carry

    for x in range(rows):
        strip(x, 0)


def advect(updated, received, strip_shift, strip_frac):
    _, rows, ny, nz = updated.shape
    vmem = pl.BlockSpec(memory_space=pltpu.VMEM)
    smem = pl.BlockSpec(memory_space=pltpu.SMEM)
    return pl.pallas_call(
        advect_kernel,
        out_shape=jax.ShapeDtypeStruct(updated.shape, updated.dtype),
        in_specs=[smem, smem, vmem, vmem],
        out_specs=vmem,
        scratch_shapes=[pltpu.VMEM((3, rows, ny + 8, nz), jnp.float32)],
        cost_estimate=pl.CostEstimate(
            flops=3 * 3 * rows * ny * nz, transcendentals=0,
            bytes_accessed=4 * 3 * rows * (2 * ny + KMAX + 1) * nz,
        ),
    )(strip_shift, strip_frac, updated, received)


def body(field, velocity, strip_shift, strip_frac, edge_shift, edge_frac):
    _, nx, ny, nz = field.shape
    nb = lax.axis_size("blocks")
    b = lax.axis_index("blocks")

    xm = shifted(jnp.concatenate([field[:, nx - 1], velocity[:, nx - 1]], axis=0), 1, 0)
    xp = shifted(jnp.concatenate([field[:, 0], velocity[:, 0]], axis=0), -1, 0)
    own_low = jnp.concatenate([field[:, :, ny - 1], velocity[:, :, ny - 1]], axis=0)
    own_high = jnp.concatenate([field[:, :, 0], velocity[:, :, 0]], axis=0)
    low_ends = jnp.concatenate([xm[:, ny - WIDE :], xp[:, ny - 1 : ny]], axis=1)
    high_ends = jnp.concatenate([xp[:, :WIDE], xm[:, 0:1]], axis=1)
    from_low = shifted((low_ends, own_low), 0, 1)
    from_high = shifted((high_ends, own_high), 0, -1)
    flags = jnp.stack([b == 0, b == nb - 1]).astype(jnp.int32)
    updated, top = ct_update(edge_shift, edge_frac, flags, field, velocity, xm, xp, from_low, from_high)
    received = shifted(top, 0, 1)
    return advect(updated, received, strip_shift, strip_frac)


def solution(mesh):
    placed = (
        P(None, "blocks", "phi", None),
        P(None, "blocks", "phi", None),
        P("blocks"),
        P("blocks"),
        P(),
        P(),
    )
    return jax.shard_map(
        body, mesh=mesh, in_specs=placed, out_specs=P(None, "blocks", "phi", None), check_vma=False
    )
```
